128 devices in a mesh: cell: 4 (over z), wide: 32 (over y, x, core).
Axes of the slice: x: 4, y: 4, z: 4, core: 2. Of those that a mesh axis runs over, the one named last changes fastest.
Arguments:
- positions: float32 [3, 4, 256, 128], P(None, 'cell', 'wide'), may hold values from 0 to 1
- rhs: float32 [3, 4, 256, 128], P(None, 'cell', 'wide'), may hold values from -6 to 6
- blob_owner: int32 [4, 256, 128, 1], P('cell', 'wide'), may hold values from 0 to 127; in each aligned block of 1024 rows (0 to 1023, 1024 to 2047, ..., all dimensions but the last counted through in order) at most 32 rows name the same one
- blob_row: int32 [4, 256, 128], P('cell', 'wide'), may hold values from 0 to 31
- blob_arm: float32 [3, 4, 256, 128], P(None, 'cell', 'wide'), may hold values from -1 to 1
- body_inverse: float32 [6, 6, 4096], P(None, None, ('cell', 'wide'))
Outputs:
- blob_forces: float32 [3, 4, 256, 128], P(None, 'cell', 'wide')
- body_motion: float32 [6, 4096], P(None, ('cell', 'wide'))
The draws below stay inside these ranges and needn't reach their ends.
Inputs may be any that keep to these rules, and one draw needn't show every extreme that they name: `blob_owner`: at most 32 of the blobs of one device have bodies of one owner, and that many in some device.
All inputs are finite; a program needn't handle non-finite values.
Results may differ from the reference program's by a relative error of at most 0.0003.
Values sent between devices are 32-bit elements; how exact they have to be, the bound alone decides.
No kernel may reach another device: no remote copies, remote signals or barrier semaphores. Data moves between devices by JAX's collectives and lax.ppermute only.
A program may use at most 64 MiB of HBM per device.

```python
import math
import jax
import jax.numpy as jnp
import numpy as np
from jax import lax

TILE = 128
NEIGH = 9
ITERS = 3
TY = 8
BODY_DEV = 32
GX = 4
GY = 256
BLOB_DEV = 1024
NBODY = 4096
BLOB_BODY = 32
CAP = 32
N_CELL = 4
N_WIDE = 32
DEVICES = 128


def draw_body_inverse(key, part):
    first, second = jax.random.split(jax.random.fold_in(key, 23))
    noise = jax.random.normal(first, (6, 6, NBODY), jnp.float32) * 0.15
    symmetric = 0.5 * (noise + jnp.transpose(noise, (1, 0, 2)))
    scales = jnp.exp(jax.random.uniform(second, (NBODY,), jnp.float32, 0.0, math.log(4.0))) / BLOB_BODY
    unit = jnp.eye(6, dtype=jnp.float32)[:, :, None]
    return ((unit + symmetric) * scales[None, None]).astype(jnp.float32)


def plant(drawn, stream_key, smallest, largest):
    shape = drawn.shape
    spot = [jax.random.randint(jax.random.fold_in(stream_key, axis), (), 0, shape[axis]) for axis in range(len(shape))]
    drawn = drawn.at[tuple(spot)].set(smallest)
    longest = shape.index(max(shape))
    spot[longest] = (spot[longest] + 1) % shape[longest]
    return drawn.at[tuple(spot)].set(largest)


def steps_of(stream_key, dims, pieces, least, high):
    gain, own = 1.0, jax.random.fold_in(stream_key, 6)
    for position, blocks in pieces:
        steps = jnp.exp(jax.random.uniform(jax.random.fold_in(own, position), (blocks,), jnp.float32, least / len(pieces), high / len(pieces)))
        gain = gain * jnp.repeat(steps, dims[position] // blocks).reshape([-1 if axis == position else 1 for axis in range(len(dims))])
    return gain


def assign_block(own_key, own, number, rows, amount, top, most, lean):
    ranking = jax.random.permutation(own_key, amount)
    crowded, usual = shares(amount, rows * top, most, lean, True), shares(amount, rows * top, most, lean, False)
    places = jnp.arange(amount)

    def named(tallies, turn):
        used = int((tallies > 0).sum())
        fixed = max(1, used // 4)
        moved = fixed + (places - fixed + turn * (used - fixed)) % max(1, amount - fixed)
        return jnp.zeros((amount,), jnp.int32).at[ranking[jnp.where(places < fixed, places, moved)]].set(jnp.asarray(tallies, jnp.int32))

    tallies = jnp.where(number % 4 == 0, named(crowded, number // 4), named(usual, number - number // 4 - 1))
    mixed = jax.random.permutation(jax.random.fold_in(own, 3), amount)
    giver, taker = mixed[0:amount // 2 * 2:2], mixed[1:amount // 2 * 2:2]
    slack = jnp.minimum(tallies[giver] - 1, most - tallies[taker]) // 2
    slack = jnp.where((giver == ranking[0]) | (taker == ranking[0]) | (tallies[taker] == 0), 0, jnp.maximum(slack, 0))
    moved = jax.random.randint(jax.random.fold_in(own, 4), (amount // 2,), 0, 1 << 20) % (slack + 1)
    tallies = tallies.at[giver].add(-moved).at[taker].add(moved)
    items = jnp.searchsorted(jnp.cumsum(tallies), jnp.arange(rows * top), side="right").astype(jnp.int32)
    grid = items.reshape(top, rows).T
    grid = grid[jax.random.permutation(jax.random.fold_in(own, 1), rows)]
    turn = jax.random.randint(jax.random.fold_in(own, 2), (rows, 1), 0, top)
    return jnp.take_along_axis(grid, (jnp.arange(top)[None, :] + turn) % top, axis=1)


def shares(count, total, limit, skew, full):
    loads = [(1 << 20) // math.isqrt(rank ** skew) + 1 for rank in range(1, count + 1)]
    largest = limit if full else min(limit, max(-(-total // count), total * loads[0] // sum(loads)))
    least = 1 if total - largest >= count - 1 else 0
    counts, spare = [largest] + [least] * (count - 1), total - largest - least * (count - 1)
    while spare > 0:
        candidates = [i for i in range(1, count) if counts[i] < largest] or [i for i in range(1, count) if counts[i] < limit]
        pool, left = sum([loads[i] for i in candidates]), spare
        for i in candidates:
            more = min(limit - counts[i], max(1, left * loads[i] // pool), spare)
            counts[i] = counts[i] + more
            spare = spare - more
    return np.array(counts)


def scatter_about(own_key, extent, width, limit, cuts=(), kind=jnp.bfloat16):
    values = jax.random.normal(own_key, extent, jnp.float32) * width
    if len(cuts) > 0:
        values = steps_of(own_key, extent, cuts, -0.22, 0.18) * values
    return jnp.clip(values, min=-limit, max=limit).astype(kind)


def setup_inputs(seed: int = 0) -> dict:
    streams_of = jax.random.split(jax.random.key(seed), 7)
    positions = jnp.clip(1.0 * jax.random.uniform(streams_of[0], (3, GX, GY, TILE), jnp.float32) ** steps_of(streams_of[0], (3, GX, GY, TILE), ((1, 4), (2, 32)), -0.2, 0.2), 0.0, 1.0)
    rhs = scatter_about(streams_of[1], (3, GX, GY, TILE), 1.0, 6.0, ((1, 4), (2, 32)), jnp.float32)
    blob_owner_keys = jax.random.split(jax.random.fold_in(streams_of[2], 1), GX * GY * TILE // BLOB_DEV)
    blob_owner_turns = jax.random.permutation(jax.random.fold_in(streams_of[2], 3), GX * GY * TILE // BLOB_DEV)
    blob_owner = jax.vmap(lambda own, number: assign_block(jax.random.fold_in(streams_of[2], 2), own, number, BLOB_DEV, DEVICES, 1, CAP, 2))(blob_owner_keys, blob_owner_turns).reshape((GX, GY, TILE, 1))
    blob_row = plant(jax.random.randint(streams_of[3], (GX, GY, TILE), 0, BODY_DEV), jax.random.fold_in(streams_of[3], 1), 0, BODY_DEV - 1).astype(jnp.int32)
    blob_arm = jnp.clip(jax.random.uniform(streams_of[4], (3, GX, GY, TILE), jnp.float32, -1.0, 1.0) * steps_of(streams_of[4], (3, GX, GY, TILE), ((1, 4), (2, 32)), -0.4, 0.0), -1.0, 1.0)
    body_inverse = draw_body_inverse(jax.random.fold_in(streams_of[6], 71), 0)
    return {"positions": positions, "rhs": rhs, "blob_owner": blob_owner, "blob_row": blob_row, "blob_arm": blob_arm, "body_inverse": body_inverse}


EPS2 = 0.04
KAPPA = 0.3

def pair_sum(target, source, forces):
    sep = target[..., :, None] - source[..., None, :]
    dist2 = lax.optimization_barrier(jnp.sum(sep * sep, axis=0))
    soft = dist2 + EPS2
    inverse = 1.0 / (soft * jnp.sqrt(soft))
    near = (dist2 + 2.0 * EPS2) * inverse
    along = lax.optimization_barrier(jnp.sum(sep * forces[..., None, :], axis=0))
    return lax.optimization_barrier(jnp.sum(near[None] * forces[..., None, :] + (inverse * along)[None] * sep, axis=-1))

def shifted(field, code, with_offset):
    step_x = code // 3 - 1
    step_y = code % 3 - 1
    moved = jnp.roll(field, (-step_x, -step_y), axis=(1, 2))
    if with_offset:
        moved = moved + jnp.array([step_x, step_y, 0], jnp.float32)[:, None, None, None]
    return moved

def blocks(field):
    return jnp.moveaxis(field.reshape(3, N_CELL * N_WIDE, TY, TILE), 1, 0)

def mobility(field, positions):
    total = jnp.zeros_like(field)
    for code in range(NEIGH):
        source = shifted(positions, code, True)
        forces = shifted(field, code, False)
        part = lax.map(lambda item: pair_sum(item[0], item[1], item[2]), (blocks(positions), blocks(source), blocks(forces)))
        total = total + jnp.moveaxis(part, 0, 1).reshape(field.shape)
    return field + KAPPA / math.sqrt(NEIGH * TILE) * total

def precondition(field, arms, body_ids, body_inverse):
    values = field.reshape(3, -1)
    sent = jnp.concatenate([values, jnp.cross(arms, values, axis=0)], 0)
    sums = jax.ops.segment_sum(sent.T, body_ids, num_segments=NBODY).T
    motion = jnp.einsum('abn,bn->an', body_inverse, sums, precision=lax.Precision.HIGHEST)
    back = motion[:, body_ids]
    extra = back[:3] + jnp.cross(back[3:], arms, axis=0)
    return (field + extra.reshape(field.shape), motion)

def reference(positions, rhs, blob_owner, blob_row, blob_arm, body_inverse):
    body_ids = (blob_owner.reshape(-1) * BODY_DEV + blob_row.reshape(-1)).astype(jnp.int32)
    arms = blob_arm.reshape(3, -1)
    beta = jnp.sqrt(jnp.sum(rhs * rhs))
    basis = [rhs / beta]
    hessen = jnp.zeros((ITERS + 1, ITERS), jnp.float32)
    for column in range(ITERS):
        moved, unused = precondition(basis[column], arms, body_ids, body_inverse)
        fresh = mobility(moved, positions)
        inners = [jnp.sum(basis[row] * fresh) for row in range(column + 1)]
        for row in range(column + 1):
            fresh = fresh - inners[row] * basis[row]
            hessen = hessen.at[row, column].set(inners[row])
        length = jnp.sqrt(jnp.sum(fresh * fresh))
        hessen = hessen.at[column + 1, column].set(length)
        basis.append(fresh / length)
    normal_matrix = jnp.dot(hessen.T, hessen, precision=lax.Precision.HIGHEST)
    target = beta * hessen[0]
    factor = jnp.linalg.cholesky(normal_matrix)
    coeffs = jax.scipy.linalg.cho_solve((factor, True), target)
    combined = jnp.zeros_like(rhs)
    for column in range(ITERS):
        combined = combined + coeffs[column] * basis[column]
    blob_forces, body_motion = precondition(combined, arms, body_ids, body_inverse)
    return (blob_forces, body_motion)
```

```python
import math

import jax
import jax.numpy as jnp
from jax import lax
from jax.experimental import pallas as pl
from jax.experimental.pallas import tpu as pltpu
from jax.sharding import Mesh
from jax.sharding import PartitionSpec as P

ITERS = 3
WIDE = ("wide_0", "wide_1", "wide_2")
CELL_WIDE = ("cell", "wide_0", "wide_1", "wide_2")
EPS2 = 0.04
KAPPA = 0.3
FACTOR = KAPPA / math.sqrt(9 * 128)
F32 = jnp.float32
BF16 = jnp.bfloat16

TY = 8
TILE = 128
NDEV = 128
NWIDE = 32
ROWS = 32
HALO_AT = 64
DOT_AT = 88
BLOCKS = 6
EDGE_OF = {-1: 3, 0: 4, 1: 5}
ROW_OF = {-1: 1, 0: 0, 1: 2}


def iota(shape, axis):
    return lax.broadcasted_iota(jnp.int32, shape, axis)


def split2(x):
    hi = x.astype(BF16).astype(F32)
    return hi, x - hi


def cross(a, b):
    return (
        a[1] * b[2] - a[2] * b[1],
        a[2] * b[0] - a[0] * b[2],
        a[0] * b[1] - a[1] * b[0],
    )


def rows_of(message_ref, part, parts):
    return message_ref[pl.ds(part, NDEV, stride=parts), :]


def body_sums(field, arms, owner, row, onehot_ref, high_ref, low_ref):
    sent = list(field) + list(cross(arms, field))
    pieces = [split2(x) for x in sent]
    owner_ids = iota((NDEV, TILE), 0)
    row_ids = iota((ROWS, TILE), 0)
    for tile in range(TY):
        lanes = pl.ds(tile * TILE, TILE)
        pick = slice(tile, tile + 1)
        onehot_ref[:, lanes] = jnp.where(owner_ids == owner[pick], 1.0, 0.0).astype(BF16)
        mine = row_ids == row[pick]
        for part in range(6):
            place = slice(part * ROWS, (part + 1) * ROWS)
            high, low = pieces[part]
            high_ref[place, lanes] = jnp.where(mine, high[pick], 0.0).astype(BF16)
            low_ref[place, lanes] = jnp.where(mine, low[pick], 0.0).astype(BF16)
    contract = (((1,), (1,)), ((), ()))
    onehot = onehot_ref[...]
    return lax.dot_general(
        onehot, high_ref[...], contract, preferred_element_type=F32
    ) + lax.dot_general(onehot, low_ref[...], contract, preferred_element_type=F32)


def total(x):
    return jnp.sum(jnp.sum(x, axis=1, keepdims=True), axis=0, keepdims=True)


def forward_message(field, sums, dots, out_ref, parts):
    lane = iota((NDEV, TILE), 1)
    stacked = jnp.concatenate(
        [jnp.zeros((HALO_AT, TILE), F32)]
        + list(field)
        + [jnp.zeros((TILE - DOT_AT, TILE), F32)],
        axis=0,
    )
    second = jnp.concatenate([sums[:, TILE:], jnp.zeros((NDEV, 64), F32)], axis=1)
    second = second + stacked.T
    for at, dot in enumerate(dots):
        second = jnp.where(lane == DOT_AT + at, dot, second)
    out_ref[pl.ds(0, NDEV, stride=parts), :] = sums[:, :TILE]
    out_ref[pl.ds(1, NDEV, stride=parts), :] = second


def start_kernel(pos_ref, rhs_ref, owner_ref, row_ref, arm_ref, out_ref, onehot, high, low):
    field = [rhs_ref[8 * c : 8 * c + 8, :] for c in range(3)]
    arms = [arm_ref[8 * c : 8 * c + 8, :] for c in range(3)]
    owner, row = owner_ref[...], row_ref[...]
    sums = body_sums(field, arms, owner, row, onehot, high, low)
    square = total(field[0] * field[0] + field[1] * field[1] + field[2] * field[2])
    forward_message(field, sums, [square], out_ref, 3)
    fixed = jnp.concatenate(
        [
            pos_ref[...],
            arm_ref[...],
            owner.astype(F32),
            row.astype(F32),
            jnp.zeros((64, TILE), F32),
        ],
        axis=0,
    )
    out_ref[pl.ds(2, NDEV, stride=3), :] = fixed.T


def turned(x, by):
    by = (by % 4) * NWIDE
    return x if by == 0 else jnp.concatenate([x[by:], x[:by]], axis=0)


def beside(x, by):
    groups = [x[z * NWIDE : (z + 1) * NWIDE] for z in range(4)]
    return jnp.concatenate([pltpu.roll(g, (-by) % NWIDE, 0) for g in groups], axis=0)


def routed(x, first, width):
    lane = iota((NDEV, TILE), 1)
    x = jnp.where((lane >= first) & (lane < first + width), x, 0.0)
    place = (lane - first) & 7
    edge = jnp.where(place == 7, beside(x, -1), jnp.where(place == 0, beside(x, 1), 0.0))
    return [turned(x, -1), turned(x, 1), turned(edge, -1), edge, turned(edge, 1)]


def shifted(x, by):
    by = by % TILE
    return x if by == 0 else pltpu.roll(x, by, 1)


def spread(row, lane):
    return jnp.broadcast_to(row[:, lane : lane + 1], (1, TILE))


def owner_kernel(step, parts, inverse_ref, message_ref, *refs):
    states = refs[:step]
    out_ref, state_ref = refs[step:]
    first = rows_of(message_ref, 0, parts)
    second = rows_of(message_ref, 1, parts)
    sums = [jnp.sum(first, axis=0, keepdims=True), jnp.sum(second, axis=0, keepdims=True)]
    inners = [spread(sums[1], DOT_AT + 1 + i) for i in range(step)]
    square = spread(sums[1], DOT_AT)
    for inner in inners:
        square = square - inner * inner
    length = jnp.sqrt(square)
    scale = 1.0 / length
    for i in range(step):
        for half in range(2):
            sums[half] = sums[half] - inners[i] * states[i][half : half + 1, :]
    sums = [s * scale for s in sums]
    sub, lane = iota((8, TILE), 0), iota((8, TILE), 1)
    tiled = jnp.where(sub < 4, sums[0], sums[1])
    tiled = jnp.where((lane // ROWS == sub % 4) & (sub < 6), tiled, 0.0)
    tiled = tiled + pltpu.roll(tiled, 32, 1)
    tiled = tiled + pltpu.roll(tiled, 64, 1)
    motion = [
        jnp.sum(inverse_ref[8 * half : 8 * half + 8, :] * tiled, axis=0, keepdims=True)
        for half in range(2)
    ]
    zero = jnp.zeros((1, TILE), F32)
    state_ref[...] = jnp.concatenate(
        sums + motion + [length, scale] + inners + [zero] * (2 - step), axis=0
    )
    back = 6 if parts == 3 else 3
    for half in range(2):
        out_ref[pl.ds(half, NDEV, stride=back), :] = jnp.broadcast_to(motion[half], (NDEV, TILE))
    blocks = routed(second, HALO_AT, 24)
    rim = shifted(blocks[0], -HALO_AT)
    for k in range(1, 5):
        rim = rim + shifted(blocks[k], 24 * k - HALO_AT)
    out_ref[pl.ds(2, NDEV, stride=back), :] = rim
    if parts == 3:
        blocks = routed(rows_of(message_ref, 2, parts), 0, 64)
        out_ref[pl.ds(3, NDEV, stride=back), :] = blocks[0] + shifted(blocks[1], 64)
        out_ref[pl.ds(4, NDEV, stride=back), :] = blocks[2] + shifted(blocks[3], 64)
        out_ref[pl.ds(5, NDEV, stride=back), :] = blocks[4]


def picked_motion(first, second, owner_ref, row_ref):
    table = jnp.concatenate([first.T, second.T[:64]], axis=0)
    high, low = split2(table)
    table = jnp.concatenate([high.astype(BF16), low.astype(BF16)], axis=1)
    owner_ids = iota((NDEV, TILE), 0)
    row_ids = iota((ROWS, TILE), 0)
    sub = iota((8, TILE), 0)
    results = []
    for block in range(BLOCKS):
        owner = owner_ref[8 * block : 8 * block + 8, :]
        row = row_ref[8 * block : 8 * block + 8, :]
        values = [jnp.zeros((8, TILE), F32) for _ in range(6)]
        for tile in range(TY) if block < 3 else (0, 7):
            pick = slice(tile, tile + 1)
            onehot = jnp.where(owner_ids == owner[pick], 1.0, 0.0).astype(BF16)
            onehot = jnp.concatenate([onehot, onehot], axis=0)
            found = jnp.dot(table, onehot, preferred_element_type=F32)
            mine = row_ids == row[pick]
            for part in range(6):
                chosen = jnp.where(mine, found[part * ROWS : (part + 1) * ROWS], 0.0)
                value = jnp.sum(chosen, axis=0, keepdims=True)
                values[part] = jnp.where(sub == tile, value, values[part])
        results.append(values)
    return results


def mobility(pos_ref, moved, source_ref):
    sub = iota((8, TILE), 0)

    def block(get, number, part):
        return get(number, part)

    def at(number, part):
        return pos_ref[24 * number + 8 * part : 24 * number + 8 * part + 8, :]

    def moved_at(number, part):
        return moved[number][part]

    for code in range(9):
        dx, dy = code // 3 - 1, code % 3 - 1
        for kind, get in enumerate((at, moved_at)):
            for part in range(3):
                x = get(ROW_OF[dx], part)
                if dy == -1:
                    x = jnp.where(sub == 7, get(EDGE_OF[dx], part), x)
                    x = pltpu.roll(x, 1, 0)
                elif dy == 1:
                    x = jnp.where(sub == 0, get(EDGE_OF[dx], part), x)
                    x = pltpu.roll(x, 7, 0)
                if kind == 0 and part < 2:
                    x = x + float((dx, dy)[part])
                place = 24 * kind + 8 * part
                source_ref[code, place : place + 8, :] = x
    target = [at(0, part) for part in range(3)]
    unroll = 8

    def of_code(code, sums):
        source = [source_ref[code, 8 * k : 8 * k + 8, :] for k in range(6)]

        def of_turn(turn, sums):
            for k in range(unroll):
                there = [pltpu.roll(s, turn * unroll + k, 1) for s in source]
                sep = [target[a] - there[a] for a in range(3)]
                soft = sep[0] * sep[0] + sep[1] * sep[1] + (sep[2] * sep[2] + EPS2)
                root = lax.rsqrt(soft)
                inverse = root * root * root
                near = root + EPS2 * inverse
                along = sep[0] * there[3] + sep[1] * there[4] + sep[2] * there[5]
                along = along * inverse
                sums = tuple(
                    sums[a] + (near * there[3 + a] + along * sep[a]) for a in range(3)
                )
            return sums

        return lax.fori_loop(0, TILE // unroll, of_turn, sums)

    zero = jnp.zeros((8, TILE), F32)
    return lax.fori_loop(0, 9, of_code, (zero, zero, zero))


def local_kernel(step, *refs):
    refs = list(refs)
    take = lambda n: [refs.pop(0) for _ in range(n)]
    message_ref, state_ref, field_ref = take(3)
    back = 6 if step == 0 else 3
    if step == 0:
        own_pos, own_arm, own_owner, own_row = take(4)
    else:
        pos_ref, arm_ref, owner_ref, row_ref = take(4)
    bases = take(step)
    if step == 0:
        pos_ref, arm_ref, owner_ref, row_ref = take(4)
    basis_ref, moved_ref, fresh_ref, out_ref = take(4)
    source_ref, onehot, high, low = take(4)
    if step == 0:
        near = rows_of(message_ref, 3, back).T
        edge = rows_of(message_ref, 4, back).T
        last = rows_of(message_ref, 5, back).T
        fixed = [near[:64], near[64:], edge[:64], edge[64:], last[:64]]
        pos_ref[0:24, :] = own_pos[...]
        arm_ref[0:24, :] = own_arm[...]
        owner_ref[0:8, :] = own_owner[...]
        row_ref[0:8, :] = own_row[...]
        for k in range(5):
            pos_ref[24 * (k + 1) : 24 * (k + 2), :] = fixed[k][0:24]
            arm_ref[24 * (k + 1) : 24 * (k + 2), :] = fixed[k][24:48]
            owner_ref[8 * (k + 1) : 8 * (k + 2), :] = fixed[k][48:56].astype(jnp.int32)
            row_ref[8 * (k + 1) : 8 * (k + 2), :] = fixed[k][56:64].astype(jnp.int32)
    rim = rows_of(message_ref, 2, back).T
    basis = jnp.concatenate([field_ref[...], rim[:120]], axis=0)
    for i in range(step):
        basis = basis - state_ref[6 + i : 7 + i, :] * bases[i][...]
    basis = basis * state_ref[5:6, :]
    basis_ref[...] = basis
    motions = picked_motion(
        rows_of(message_ref, 0, back), rows_of(message_ref, 1, back), owner_ref, row_ref
    )
    moved = []
    for block in range(BLOCKS):
        arm = [arm_ref[24 * block + 8 * a : 24 * block + 8 * a + 8, :] for a in range(3)]
        turn = cross(motions[block][3:], arm)
        moved.append(
            [
                basis[24 * block + 8 * a : 24 * block + 8 * a + 8]
                + (motions[block][a] + turn[a])
                for a in range(3)
            ]
        )
    pairs = mobility(pos_ref, moved, source_ref)
    fresh = [moved[0][a] + FACTOR * pairs[a] for a in range(3)]
    for a in range(3):
        moved_ref[8 * a : 8 * a + 8, :] = moved[0][a]
        fresh_ref[8 * a : 8 * a + 8, :] = fresh[a]

    def dot(get):
        return total(fresh[0] * get(0) + fresh[1] * get(1) + fresh[2] * get(2))

    dots = [dot(lambda a: fresh[a])]
    for i in range(step):
        dots.append(dot(lambda a: bases[i][8 * a : 8 * a + 8, :]))
    dots.append(dot(lambda a: basis[8 * a : 8 * a + 8]))
    if step < ITERS - 1:
        arms = [arm_ref[8 * a : 8 * a + 8, :] for a in range(3)]
        sums = body_sums(
            fresh, arms, owner_ref[0:8, :], row_ref[0:8, :], onehot, high, low
        )
        forward_message(fresh, sums, dots, out_ref, 2)
    else:
        lane = iota((NDEV, TILE), 1)
        message = jnp.zeros((NDEV, TILE), F32)
        for at, value in enumerate(dots):
            message = jnp.where(lane == at, value, message)
        out_ref[...] = message


def final_kernel(message_ref, *refs):
    states, moved = refs[:3], refs[3:6]
    forces_ref, motion_ref = refs[6:]
    sums = jnp.sum(message_ref[...], axis=0, keepdims=True)
    beta = states[0][4:5, :]
    a = [states[1][6:7, :], states[1][4:5, :]]
    b = [states[2][6:7, :], states[2][7:8, :], states[2][4:5, :]]
    c = [spread(sums, 1 + i) for i in range(3)]
    square = spread(sums, 0) - c[0] * c[0] - c[1] * c[1] - c[2] * c[2]
    c.append(jnp.sqrt(square))
    inner = lambda p, q: sum([x * y for x, y in zip(p, q)][1:], p[0] * q[0])
    n00, n01, n02 = inner(a, a), inner(a, b), inner(a, c)
    n11, n12, n22 = inner(b, b), inner(b, c), inner(c, c)
    l00 = jnp.sqrt(n00)
    l10, l20 = n01 / l00, n02 / l00
    l11 = jnp.sqrt(n11 - l10 * l10)
    l21 = (n12 - l20 * l10) / l11
    l22 = jnp.sqrt(n22 - l20 * l20 - l21 * l21)
    t0 = beta * a[0] / l00
    t1 = (beta * b[0] - l10 * t0) / l11
    t2 = (beta * c[0] - l20 * t0 - l21 * t1) / l22
    y2 = t2 / l22
    y1 = (t1 - l21 * y2) / l11
    y0 = (t0 - l10 * y1 - l20 * y2) / l00
    forces_ref[...] = y0 * moved[0][...] + y1 * moved[1][...] + y2 * moved[2][...]
    for part in range(6):
        half, at = part // 4, (part % 4) * ROWS
        row = slice(2 + half, 3 + half)
        whole = y0 * states[0][row, :] + y1 * states[1][row, :] + y2 * states[2][row, :]
        motion_ref[part : part + 1, :] = whole[:, at : at + ROWS]


def f32(*shape):
    return jax.ShapeDtypeStruct(shape, F32)


def i32(*shape):
    return jax.ShapeDtypeStruct(shape, jnp.int32)


PARAMS = pltpu.CompilerParams(vmem_limit_bytes=24 * 1024 * 1024)


def sums_scratch():
    return [
        pltpu.VMEM((NDEV, TY * TILE), BF16),
        pltpu.VMEM((6 * ROWS, TY * TILE), BF16),
        pltpu.VMEM((6 * ROWS, TY * TILE), BF16),
    ]


def call(body, out, scratch=()):
    return pl.pallas_call(body, out_shape=out, scratch_shapes=list(scratch), compiler_params=PARAMS)


def exchange(message):
    return lax.all_to_all(message, CELL_WIDE, split_axis=0, concat_axis=0, tiled=True)


def local(positions, rhs, blob_owner, blob_row, blob_arm, body_inverse):
    pos = positions.reshape(24, TILE)
    field = rhs.reshape(24, TILE)
    arm = blob_arm.reshape(24, TILE)
    owner = blob_owner.reshape(TY, TILE)
    row = blob_row.reshape(TY, TILE)
    inverse = jnp.transpose(body_inverse, (1, 0, 2)).reshape(6, 6 * ROWS)
    inverse = jnp.pad(inverse, ((0, 2), (0, 64)))
    inverse = jnp.concatenate([inverse[:, :TILE], inverse[:, TILE:]], axis=0)
    message = call(start_kernel, f32(3 * NDEV, TILE), sums_scratch())(pos, field, owner, row, arm)
    fixed = (pos, arm, owner, row)
    states, bases, moveds = [], [], []
    for step in range(ITERS):
        parts = 3 if step == 0 else 2
        back = 6 if step == 0 else 3
        arrived = exchange(message)
        message, state = call(
            lambda *refs, step=step, parts=parts: owner_kernel(step, parts, *refs),
            (f32(back * NDEV, TILE), f32(8, TILE)),
        )(inverse, arrived, *states)
        arrived = exchange(message)
        outs = [
            f32(24 * BLOCKS, TILE),
            f32(24, TILE),
            f32(24, TILE),
            f32(NDEV if step == ITERS - 1 else 2 * NDEV, TILE),
        ]
        if step == 0:
            outs = [
                f32(24 * BLOCKS, TILE),
                f32(24 * BLOCKS, TILE),
                i32(8 * BLOCKS, TILE),
                i32(8 * BLOCKS, TILE),
            ] + outs
        results = call(
            lambda *refs, step=step: local_kernel(step, *refs),
            tuple(outs),
            [pltpu.VMEM((9, 48, TILE), F32)] + sums_scratch(),
        )(arrived, state, field, *fixed, *bases)
        if step == 0:
            fixed = results[:4]
        basis, moved, field, message = results[-4:]
        states.append(state)
        bases.append(basis)
        moveds.append(moved)
    arrived = exchange(message)
    forces, motion = call(final_kernel, (f32(24, TILE), f32(6, ROWS)))(arrived, *states, *moveds)
    return (forces.reshape(rhs.shape), motion)


def solution(mesh):
    split = Mesh(
        mesh.devices.reshape(mesh.shape["cell"], 4, 4, 2), ("cell", "wide_0", "wide_1", "wide_2")
    )
    in_specs = (
        P(None, "cell", WIDE, None),
        P(None, "cell", WIDE, None),
        P("cell", WIDE, None, None),
        P("cell", WIDE, None),
        P(None, "cell", WIDE, None),
        P(None, None, CELL_WIDE),
    )
    out_specs = (P(None, "cell", WIDE, None), P(None, CELL_WIDE))
    return jax.shard_map(local, mesh=split, in_specs=in_specs, out_specs=out_specs, check_vma=False)
```

```python
import math

import jax
import jax.numpy as jnp
from jax import lax
from jax.experimental import pallas as pl
from jax.experimental.pallas import tpu as pltpu
from jax.sharding import Mesh
from jax.sharding import PartitionSpec as P

ITERS = 3
WIDE = ("wide_0", "wide_1", "wide_2")
CELL_WIDE = ("cell", "wide_0", "wide_1", "wide_2")
EPS2 = 0.04
KAPPA = 0.3
FACTOR = KAPPA / math.sqrt(9 * 128)
F32 = jnp.float32
BF16 = jnp.bfloat16

TY = 8
TILE = 128
NDEV = 128
NWIDE = 32
ROWS = 32
HALO_AT = 64
DOT_AT = 88
BACK = 4
BLOCKS = 6
EDGE_OF = {-1: 3, 0: 4, 1: 5}
ROW_OF = {-1: 1, 0: 0, 1: 2}


def iota(shape, axis):
    return lax.broadcasted_iota(jnp.int32, shape, axis)


def split2(x):
    hi = x.astype(BF16).astype(F32)
    return hi, x - hi


def cross(a, b):
    return (
        a[1] * b[2] - a[2] * b[1],
        a[2] * b[0] - a[0] * b[2],
        a[0] * b[1] - a[1] * b[0],
    )


def rows_of(message_ref, part, parts):
    return message_ref[pl.ds(part, NDEV, stride=parts), :]


def body_sums(field, arms, owner, row, onehot_ref, high_ref, low_ref):
    sent = list(field) + list(cross(arms, field))
    pieces = [split2(x) for x in sent]
    owner_ids = iota((NDEV, TILE), 0)
    row_ids = iota((ROWS, TILE), 0)
    for tile in range(TY):
        lanes = pl.ds(tile * TILE, TILE)
        pick = slice(tile, tile + 1)
        onehot_ref[:, lanes] = jnp.where(owner_ids == owner[pick], 1.0, 0.0).astype(BF16)
        mine = row_ids == row[pick]
        for part in range(6):
            place = slice(part * ROWS, (part + 1) * ROWS)
            high, low = pieces[part]
            high_ref[place, lanes] = jnp.where(mine, high[pick], 0.0).astype(BF16)
            low_ref[place, lanes] = jnp.where(mine, low[pick], 0.0).astype(BF16)
    contract = (((1,), (1,)), ((), ()))
    onehot = onehot_ref[...]
    return lax.dot_general(
        onehot, high_ref[...], contract, preferred_element_type=F32
    ) + lax.dot_general(onehot, low_ref[...], contract, preferred_element_type=F32)


def total(x):
    return jnp.sum(jnp.sum(x, axis=1, keepdims=True), axis=0, keepdims=True)


def forward_message(field, sums, dots, out_ref):
    lane = iota((NDEV, TILE), 1)
    stacked = jnp.concatenate(
        [jnp.zeros((HALO_AT, TILE), F32)]
        + list(field)
        + [jnp.zeros((TILE - DOT_AT, TILE), F32)],
        axis=0,
    )
    second = jnp.concatenate([sums[:, TILE:], jnp.zeros((NDEV, 64), F32)], axis=1)
    second = second + stacked.T
    for at, dot in enumerate(dots):
        second = jnp.where(lane == DOT_AT + at, dot, second)
    out_ref[pl.ds(0, NDEV, stride=2), :] = sums[:, :TILE]
    out_ref[pl.ds(1, NDEV, stride=2), :] = second


def start_kernel(
    pos_hbm, rhs_hbm, owner_hbm, row_hbm, arm_hbm, out_ref, pack_ref, rhs_ref,
    owner_ref, row_ref, sems, onehot, high, low,
):
    copies = [
        pltpu.make_async_copy(source, target, sems.at[at])
        for at, (source, target) in enumerate(
            (
                (rhs_hbm, rhs_ref),
                (arm_hbm, pack_ref.at[24:48, :]),
                (owner_hbm, owner_ref),
                (row_hbm, row_ref),
                (pos_hbm, pack_ref.at[0:24, :]),
            )
        )
    ]
    for copy in copies:
        copy.start()
    for copy in copies:
        copy.wait()
    field = [rhs_ref[8 * c : 8 * c + 8, :] for c in range(3)]
    arms = [pack_ref[24 + 8 * c : 32 + 8 * c, :] for c in range(3)]
    owner, row = owner_ref[...], row_ref[...]
    pack_ref[48:56, :] = owner.astype(F32)
    pack_ref[56:64, :] = row.astype(F32)
    sums = body_sums(field, arms, owner, row, onehot, high, low)
    square = total(field[0] * field[0] + field[1] * field[1] + field[2] * field[2])
    forward_message(field, sums, [square], out_ref)


def turned(x, by):
    by = (by % 4) * NWIDE
    return x if by == 0 else jnp.concatenate([x[by:], x[:by]], axis=0)


def beside(x, by):
    groups = [x[z * NWIDE : (z + 1) * NWIDE] for z in range(4)]
    return jnp.concatenate([pltpu.roll(g, (-by) % NWIDE, 0) for g in groups], axis=0)


def routed(x, first, width):
    lane = iota((NDEV, TILE), 1)
    x = jnp.where((lane >= first) & (lane < first + width), x, 0.0)
    place = (lane - first) & 7
    edge = jnp.where(place == 7, beside(x, -1), jnp.where(place == 0, beside(x, 1), 0.0))
    return [turned(x, -1), turned(x, 1), turned(edge, -1), edge, turned(edge, 1)]


def shifted(x, by):
    by = by % TILE
    return x if by == 0 else pltpu.roll(x, by, 1)


def spread(row, lane):
    return jnp.broadcast_to(row[:, lane : lane + 1], (1, TILE))


def owner_kernel(step, inverse_ref, message_ref, *refs):
    states = refs[:step]
    out_ref, state_ref = refs[step:]
    first = rows_of(message_ref, 0, 2)
    second = rows_of(message_ref, 1, 2)
    sums = [jnp.sum(first, axis=0, keepdims=True), jnp.sum(second, axis=0, keepdims=True)]
    inners = [spread(sums[1], DOT_AT + 1 + i) for i in range(step)]
    square = spread(sums[1], DOT_AT)
    for inner in inners:
        square = square - inner * inner
    length = jnp.sqrt(square)
    scale = 1.0 / length
    for i in range(step):
        for half in range(2):
            sums[half] = sums[half] - inners[i] * states[i][half : half + 1, :]
    sums = [s * scale for s in sums]
    sub, lane = iota((8, TILE), 0), iota((8, TILE), 1)
    tiled = jnp.where(sub < 4, sums[0], sums[1])
    tiled = jnp.where((lane // ROWS == sub % 4) & (sub < 6), tiled, 0.0)
    tiled = tiled + pltpu.roll(tiled, 32, 1)
    tiled = tiled + pltpu.roll(tiled, 64, 1)
    motion = [
        jnp.sum(inverse_ref[8 * half : 8 * half + 8, :] * tiled, axis=0, keepdims=True)
        for half in range(2)
    ]
    zero = jnp.zeros((1, TILE), F32)
    state_ref[...] = jnp.concatenate(
        sums + motion + [length, scale] + inners + [zero] * (2 - step), axis=0
    )
    for half in range(2):
        out_ref[pl.ds(half, NDEV, stride=BACK), :] = jnp.broadcast_to(motion[half], (NDEV, TILE))
    blocks = routed(second, HALO_AT, 24)
    rim = shifted(blocks[0], -HALO_AT)
    for k in range(1, 5):
        rim = rim + shifted(blocks[k], 24 * k - HALO_AT)
    out_ref[pl.ds(2, NDEV, stride=BACK), :] = rim
    out_ref[pl.ds(3, NDEV, stride=BACK), :] = jnp.zeros((NDEV, TILE), F32)


def picked_motion(first, second, owner_ref, row_ref):
    table = jnp.concatenate([first.T, second.T[:64]], axis=0)
    high, low = split2(table)
    table = jnp.concatenate([high.astype(BF16), low.astype(BF16)], axis=1)
    owner_ids = iota((NDEV, TILE), 0)
    row_ids = iota((ROWS, TILE), 0)
    sub = iota((8, TILE), 0)
    results = []
    for block in range(BLOCKS):
        owner = owner_ref[8 * block : 8 * block + 8, :]
        row = row_ref[8 * block : 8 * block + 8, :]
        values = [jnp.zeros((8, TILE), F32) for _ in range(6)]
        for tile in range(TY) if block < 3 else (0, 7):
            pick = slice(tile, tile + 1)
            onehot = jnp.where(owner_ids == owner[pick], 1.0, 0.0).astype(BF16)
            onehot = jnp.concatenate([onehot, onehot], axis=0)
            found = jnp.dot(table, onehot, preferred_element_type=F32)
            mine = row_ids == row[pick]
            for part in range(6):
                chosen = jnp.where(mine, found[part * ROWS : (part + 1) * ROWS], 0.0)
                value = jnp.sum(chosen, axis=0, keepdims=True)
                values[part] = jnp.where(sub == tile, value, values[part])
        results.append(values)
    return results


def source_rows(get, rows_ref):
    for i, dx in enumerate((-1, 0, 1)):
        for part in range(3):
            at = 30 * part + 10 * i
            edge = get(EDGE_OF[dx], part)
            rows_ref[at : at + 1, :] = edge[7:8]
            rows_ref[at + 1 : at + 9, :] = get(ROW_OF[dx], part)
            rows_ref[at + 9 : at + 10, :] = edge[0:1]


def sources_of(rows_ref, tile):
    return [
        [rows_ref[pl.ds(30 * part + 10 * i + tile + j, 8, stride=0), :] for part in range(3)]
        for i in range(3)
        for j in range(3)
    ]


def pair_kernel(
    pack_ref, before_ref, after_ref, left_ref, right_ref,
    pair_hbm, arm_ref, owner_ref, row_ref, rows_ref, pair_ref, sems,
):
    sub = iota((8, TILE), 0)

    def get(block, part):
        if block < 3:
            ref = (pack_ref, before_ref, after_ref)[block]
            return ref[8 * part : 8 * part + 8, :]
        at = 8 * (block - 3) + part
        left, right = left_ref[at : at + 1, :], right_ref[at : at + 1, :]
        return jnp.where(sub == 7, left, jnp.where(sub == 0, right, 0.0))

    for block in range(BLOCKS):
        for part in range(3):
            place = 24 * block + 8 * part
            arm_ref[place : place + 8, :] = get(block, 3 + part)
        owner_ref[8 * block : 8 * block + 8, :] = get(block, 6).astype(jnp.int32)
        row_ref[8 * block : 8 * block + 8, :] = get(block, 7).astype(jnp.int32)
    source_rows(get, rows_ref)
    columns = jnp.concatenate([pack_ref[0:24, :], jnp.zeros((104, TILE), F32)], axis=0).T

    def of_tile(tile, carry):
        turned_columns = pltpu.roll(columns, TILE - tile, 1)
        sources = sources_of(rows_ref, tile)
        for k in range(9):
            for part, step in ((0, k // 3 - 1), (1, k % 3 - 1)):
                if step != 0:
                    sources[k][part] = sources[k][part] + float(step)
        for group in range(TILE // 8):
            rows = turned_columns[8 * group : 8 * group + 8]
            target = [jnp.broadcast_to(rows[:, 8 * a : 8 * a + 1], (8, TILE)) for a in range(3)]
            for k in range(9):
                sep = [target[a] - sources[k][a] for a in range(3)]
                soft = sep[0] * sep[0] + sep[1] * sep[1] + (sep[2] * sep[2] + EPS2)
                root = lax.rsqrt(soft)
                square = root * root
                pair_ref[tile, group, k, 0] = root + EPS2 * (square * root)
                scale = square * lax.rsqrt(root)
                for a in range(3):
                    pair_ref[tile, group, k, 1 + a] = sep[a] * scale
        pltpu.make_async_copy(pair_ref.at[tile], pair_hbm.at[tile], sems.at[tile]).start()
        return carry

    lax.fori_loop(0, TY, of_tile, 0)
    for tile in range(TY):
        pltpu.make_async_copy(pair_ref.at[tile], pair_hbm.at[tile], sems.at[tile]).wait()


def mobility(pair_ref, moved, rows_ref, pairs_ref, arrive):
    source_rows(lambda block, part: moved[block][part], rows_ref)

    def of_tile(tile, carry):
        arrive(tile)
        sources = sources_of(rows_ref, tile)
        sums = [[], [], []]
        for group in range(TILE // 8):
            terms = None
            for k in range(9):
                near = pair_ref[tile, group, k, 0]
                sep = [pair_ref[tile, group, k, 1 + a] for a in range(3)]
                force = sources[k]
                along = sep[0] * force[0] + sep[1] * force[1] + sep[2] * force[2]
                term = [near * force[a] + along * sep[a] for a in range(3)]
                terms = term if terms is None else [terms[a] + term[a] for a in range(3)]
            for a in range(3):
                sums[a].append(terms[a])
        for a in range(3):
            across = jnp.concatenate(sums[a], axis=0).T
            pairs_ref[pl.ds(8 * a + tile, 1), :] = jnp.sum(across, axis=0, keepdims=True)
        return carry

    lax.fori_loop(0, TY, of_tile, 0, unroll=2)
    return [pairs_ref[8 * a : 8 * a + 8, :] for a in range(3)]


def local_kernel(step, *refs):
    refs = list(refs)
    take = lambda n: [refs.pop(0) for _ in range(n)]
    message_ref, state_ref, field_ref = take(3)
    pair_ref, arm_ref, owner_ref, row_ref = take(4)
    bases = take(step)
    basis_ref, moved_ref, fresh_ref, out_ref = take(4)
    rows_ref, pairs_ref, onehot, high, low = take(5)
    arrive = lambda tile: None
    if step == 0:
        pair_hbm = pair_ref
        pair_ref, sems = take(2)
        fetch = lambda tile: pltpu.make_async_copy(
            pair_hbm.at[tile], pair_ref.at[tile], sems.at[tile]
        )
        for tile in range(TY):
            fetch(tile).start()
        arrive = lambda tile: fetch(tile).wait()
    rim = rows_of(message_ref, 2, BACK).T
    basis = jnp.concatenate([field_ref[...], rim[:120]], axis=0)
    for i in range(step):
        basis = basis - state_ref[6 + i : 7 + i, :] * bases[i][...]
    basis = basis * state_ref[5:6, :]
    basis_ref[...] = basis
    motions = picked_motion(
        rows_of(message_ref, 0, BACK), rows_of(message_ref, 1, BACK), owner_ref, row_ref
    )
    moved = []
    for block in range(BLOCKS):
        arm = [arm_ref[24 * block + 8 * a : 24 * block + 8 * a + 8, :] for a in range(3)]
        turn = cross(motions[block][3:], arm)
        moved.append(
            [
                basis[24 * block + 8 * a : 24 * block + 8 * a + 8]
                + (motions[block][a] + turn[a])
                for a in range(3)
            ]
        )
    pairs = mobility(pair_ref, moved, rows_ref, pairs_ref, arrive)
    fresh = [moved[0][a] + FACTOR * pairs[a] for a in range(3)]
    for a in range(3):
        moved_ref[8 * a : 8 * a + 8, :] = moved[0][a]
        fresh_ref[8 * a : 8 * a + 8, :] = fresh[a]

    def dot(get):
        return total(fresh[0] * get(0) + fresh[1] * get(1) + fresh[2] * get(2))

    dots = [dot(lambda a: fresh[a])]
    for i in range(step):
        dots.append(dot(lambda a: bases[i][8 * a : 8 * a + 8, :]))
    dots.append(dot(lambda a: basis[8 * a : 8 * a + 8]))
    if step < ITERS - 1:
        arms = [arm_ref[8 * a : 8 * a + 8, :] for a in range(3)]
        sums = body_sums(
            fresh, arms, owner_ref[0:8, :], row_ref[0:8, :], onehot, high, low
        )
        forward_message(fresh, sums, dots, out_ref)
    else:
        lane = iota((NDEV, TILE), 1)
        message = jnp.zeros((NDEV, TILE), F32)
        for at, value in enumerate(dots):
            message = jnp.where(lane == at, value, message)
        out_ref[...] = message


def final_kernel(message_ref, *refs):
    states, moved = refs[:3], refs[3:6]
    forces_ref, motion_ref = refs[6:]
    sums = jnp.sum(message_ref[...], axis=0, keepdims=True)
    beta = states[0][4:5, :]
    a = [states[1][6:7, :], states[1][4:5, :]]
    b = [states[2][6:7, :], states[2][7:8, :], states[2][4:5, :]]
    c = [spread(sums, 1 + i) for i in range(3)]
    square = spread(sums, 0) - c[0] * c[0] - c[1] * c[1] - c[2] * c[2]
    c.append(jnp.sqrt(square))
    inner = lambda p, q: sum([x * y for x, y in zip(p, q)][1:], p[0] * q[0])
    n00, n01, n02 = inner(a, a), inner(a, b), inner(a, c)
    n11, n12, n22 = inner(b, b), inner(b, c), inner(c, c)
    l00 = jnp.sqrt(n00)
    l10, l20 = n01 / l00, n02 / l00
    l11 = jnp.sqrt(n11 - l10 * l10)
    l21 = (n12 - l20 * l10) / l11
    l22 = jnp.sqrt(n22 - l20 * l20 - l21 * l21)
    t0 = beta * a[0] / l00
    t1 = (beta * b[0] - l10 * t0) / l11
    t2 = (beta * c[0] - l20 * t0 - l21 * t1) / l22
    y2 = t2 / l22
    y1 = (t1 - l21 * y2) / l11
    y0 = (t0 - l10 * y1 - l20 * y2) / l00
    forces_ref[...] = y0 * moved[0][...] + y1 * moved[1][...] + y2 * moved[2][...]
    for part in range(6):
        half, at = part // 4, (part % 4) * ROWS
        row = slice(2 + half, 3 + half)
        whole = y0 * states[0][row, :] + y1 * states[1][row, :] + y2 * states[2][row, :]
        motion_ref[part : part + 1, :] = whole[:, at : at + ROWS]


HBM = pl.BlockSpec(memory_space=pltpu.HBM)
VMEM = pl.BlockSpec(memory_space=pltpu.VMEM)


def f32(*shape):
    return jax.ShapeDtypeStruct(shape, F32)


def i32(*shape):
    return jax.ShapeDtypeStruct(shape, jnp.int32)


PAIRS = (TY, TILE // 8, 9, 4, 8, TILE)


def sums_scratch():
    return [
        pltpu.VMEM((NDEV, TY * TILE), BF16),
        pltpu.VMEM((6 * ROWS, TY * TILE), BF16),
        pltpu.VMEM((6 * ROWS, TY * TILE), BF16),
    ]


def call(body, out, scratch=(), mib=16, **options):
    return pl.pallas_call(
        body,
        out_shape=out,
        scratch_shapes=list(scratch),
        compiler_params=pltpu.CompilerParams(vmem_limit_bytes=mib * 1024 * 1024),
        **options,
    )


def exchange(message):
    return lax.all_to_all(message, CELL_WIDE, split_axis=0, concat_axis=0, tiled=True)


def ring(array, axes, step):
    count = lax.axis_size(axes)
    return lax.ppermute(array, axes, [(i, (i + step) % count) for i in range(count)])


def rims(pack):
    before, after = ring(pack, "cell", 1), ring(pack, "cell", -1)
    rows = [x.reshape(8, TY, TILE) for x in (before, pack, after)]
    last = jnp.concatenate([x[:, TY - 1] for x in rows], axis=0)
    first = jnp.concatenate([x[:, 0] for x in rows], axis=0)
    return before, after, ring(last, WIDE, 1), ring(first, WIDE, -1)


def local(positions, rhs, blob_owner, blob_row, blob_arm, body_inverse):
    pos = positions.reshape(24, TILE)
    field = rhs.reshape(24, TILE)
    arm = blob_arm.reshape(24, TILE)
    owner = blob_owner.reshape(TY, TILE)
    row = blob_row.reshape(TY, TILE)
    inverse = jnp.transpose(body_inverse, (1, 0, 2)).reshape(6, 6 * ROWS)
    inverse = jnp.pad(inverse, ((0, 2), (0, 64)))
    inverse = jnp.concatenate([inverse[:, :TILE], inverse[:, TILE:]], axis=0)
    message, pack, field = call(
        start_kernel,
        (f32(2 * NDEV, TILE), f32(64, TILE), f32(24, TILE)),
        [
            pltpu.VMEM((TY, TILE), jnp.int32),
            pltpu.VMEM((TY, TILE), jnp.int32),
            pltpu.SemaphoreType.DMA((5,)),
        ]
        + sums_scratch(),
        in_specs=[HBM] * 5,
    )(*[pltpu.with_memory_space_constraint(x, pltpu.HBM) for x in (pos, field, owner, row, arm)])
    before, after, left, right = rims(pack)
    arrived, left, right = lax.optimization_barrier((exchange(message), left, right))
    pair_count = 9 * TY * TILE * TILE
    pairs, *fixed = call(
        pair_kernel,
        (
            f32(*PAIRS),
            f32(24 * BLOCKS, TILE),
            i32(8 * BLOCKS, TILE),
            i32(8 * BLOCKS, TILE),
        ),
        [pltpu.VMEM((96, TILE), F32), pltpu.VMEM(PAIRS, F32), pltpu.SemaphoreType.DMA((TY,))],
        mib=40,
        out_specs=(HBM, VMEM, VMEM, VMEM),
        cost_estimate=pl.CostEstimate(
            flops=20 * pair_count, transcendentals=2 * pair_count, bytes_accessed=16 * pair_count
        ),
    )(pack, before, after, left, right)
    states, bases, moveds = [], [], []
    for step in range(ITERS):
        if step > 0:
            arrived = exchange(message)
        message, state = call(
            lambda *refs, step=step: owner_kernel(step, *refs),
            (f32(BACK * NDEV, TILE), f32(8, TILE)),
        )(inverse, arrived, *states)
        arrived = exchange(message)
        basis, moved, field, message = call(
            lambda *refs, step=step: local_kernel(step, *refs),
            (
                f32(24 * BLOCKS, TILE),
                f32(24, TILE),
                f32(24, TILE),
                f32(NDEV if step == ITERS - 1 else 2 * NDEV, TILE),
            ),
            [pltpu.VMEM((96, TILE), F32), pltpu.VMEM((24, TILE), F32)]
            + sums_scratch()
            + ([pltpu.VMEM(PAIRS, F32), pltpu.SemaphoreType.DMA((TY,))] if step == 0 else []),
            mib=40 if step == 0 else 16,
            in_specs=[VMEM] * 3 + [HBM if step == 0 else VMEM] + [VMEM] * (3 + step),
        )(arrived, state, field, pairs, *fixed, *bases)
        if step == 0:
            pairs = pltpu.with_memory_space_constraint(pairs, pltpu.VMEM)
        states.append(state)
        bases.append(basis)
        moveds.append(moved)
    arrived = exchange(message)
    forces, motion = call(final_kernel, (f32(24, TILE), f32(6, ROWS)))(arrived, *states, *moveds)
    return (forces.reshape(rhs.shape), motion)


def solution(mesh):
    split = Mesh(
        mesh.devices.reshape(mesh.shape["cell"], 4, 4, 2), ("cell", "wide_0", "wide_1", "wide_2")
    )
    in_specs = (
        P(None, "cell", WIDE, None),
        P(None, "cell", WIDE, None),
        P("cell", WIDE, None, None),
        P("cell", WIDE, None),
        P(None, "cell", WIDE, None),
        P(None, None, CELL_WIDE),
    )
    out_specs = (P(None, "cell", WIDE, None), P(None, CELL_WIDE))
    return jax.shard_map(local, mesh=split, in_specs=in_specs, out_specs=out_specs, check_vma=False)
```

```python
import math

import jax
import jax.numpy as jnp
from jax import lax
from jax.experimental import pallas as pl
from jax.experimental.pallas import tpu as pltpu
from jax.sharding import Mesh
from jax.sharding import PartitionSpec as P

ITERS = 3
WIDE = ("wide_0", "wide_1", "wide_2")
CELL_WIDE = ("cell", "wide_0", "wide_1", "wide_2")
EPS2 = 0.04
KAPPA = 0.3
FACTOR = KAPPA / math.sqrt(9 * 128)
F32 = jnp.float32
BF16 = jnp.bfloat16

TY = 8
TILE = 128
NDEV = 128
NWIDE = 32
ROWS = 32
HALO_AT = 64
DOT_AT = 88
FIRST = 4
BACK = 4
FIXED = 56
BLOCKS = 6
EDGE_OF = {-1: 3, 0: 4, 1: 5}
ROW_OF = {-1: 1, 0: 0, 1: 2}
EDGES_AT = 64
EDGE_STEP = (1, 0, 2)


def iota(shape, axis):
    return lax.broadcasted_iota(jnp.int32, shape, axis)


def split2(x):
    hi = x.astype(BF16).astype(F32)
    return hi, x - hi


def cross(a, b):
    return (
        a[1] * b[2] - a[2] * b[1],
        a[2] * b[0] - a[0] * b[2],
        a[0] * b[1] - a[1] * b[0],
    )


def rows_of(message_ref, part, parts):
    return message_ref[pl.ds(part, NDEV, stride=parts), :]


def body_sums(field, arms, owner, row, onehot_ref, high_ref, low_ref):
    sent = list(field) + list(cross(arms, field))
    pieces = [split2(x) for x in sent]
    owner_ids = iota((NDEV, TILE), 0)
    row_ids = iota((ROWS, TILE), 0)
    for tile in range(TY):
        lanes = pl.ds(tile * TILE, TILE)
        pick = slice(tile, tile + 1)
        onehot_ref[:, lanes] = jnp.where(owner_ids == owner[pick], 1.0, 0.0).astype(BF16)
        mine = row_ids == row[pick]
        for part in range(6):
            place = slice(part * ROWS, (part + 1) * ROWS)
            high, low = pieces[part]
            high_ref[place, lanes] = jnp.where(mine, high[pick], 0.0).astype(BF16)
            low_ref[place, lanes] = jnp.where(mine, low[pick], 0.0).astype(BF16)
    contract = (((1,), (1,)), ((), ()))
    onehot = onehot_ref[...]
    return lax.dot_general(
        onehot, high_ref[...], contract, preferred_element_type=F32
    ) + lax.dot_general(onehot, low_ref[...], contract, preferred_element_type=F32)


def total(x):
    return jnp.sum(jnp.sum(x, axis=1, keepdims=True), axis=0, keepdims=True)


def forward_message(field, sums, dots, out_ref, parts):
    lane = iota((NDEV, TILE), 1)
    stacked = jnp.concatenate(
        [jnp.zeros((HALO_AT, TILE), F32)]
        + list(field)
        + [jnp.zeros((TILE - DOT_AT, TILE), F32)],
        axis=0,
    )
    second = jnp.concatenate([sums[:, TILE:], jnp.zeros((NDEV, 64), F32)], axis=1)
    second = second + stacked.T
    for at, dot in enumerate(dots):
        second = jnp.where(lane == DOT_AT + at, dot, second)
    out_ref[pl.ds(0, NDEV, stride=parts), :] = sums[:, :TILE]
    out_ref[pl.ds(1, NDEV, stride=parts), :] = second


def start_kernel(
    pos_hbm, rhs_hbm, owner_hbm, row_hbm, arm_hbm, out_ref, pack_ref, rhs_ref,
    owner_ref, row_ref, sems, onehot, high, low,
):
    copies = [
        pltpu.make_async_copy(source, target, sems.at[at])
        for at, (source, target) in enumerate(
            (
                (rhs_hbm, rhs_ref),
                (arm_hbm, pack_ref.at[24:48, :]),
                (owner_hbm, owner_ref),
                (row_hbm, row_ref),
                (pos_hbm, pack_ref.at[0:24, :]),
            )
        )
    ]
    for copy in copies:
        copy.start()
    for copy in copies:
        copy.wait()
    field = [rhs_ref[8 * c : 8 * c + 8, :] for c in range(3)]
    arms = [pack_ref[24 + 8 * c : 32 + 8 * c, :] for c in range(3)]
    owner, row = owner_ref[...], row_ref[...]
    pack_ref[48:56, :] = (owner * ROWS + row).astype(F32)
    pack_ref[56:128, :] = jnp.zeros((72, TILE), F32)
    sums = body_sums(field, arms, owner, row, onehot, high, low)
    square = total(field[0] * field[0] + field[1] * field[1] + field[2] * field[2])
    forward_message(field, sums, [square], out_ref, FIRST)
    out_ref[pl.ds(2, NDEV, stride=FIRST), :] = pack_ref[...].T
    out_ref[pl.ds(3, NDEV, stride=FIRST), :] = jnp.zeros((NDEV, TILE), F32)


def turned(x, by):
    by = (by % 4) * NWIDE
    return x if by == 0 else jnp.concatenate([x[by:], x[:by]], axis=0)


def beside(x, by):
    groups = [x[z * NWIDE : (z + 1) * NWIDE] for z in range(4)]
    return jnp.concatenate([pltpu.roll(g, (-by) % NWIDE, 0) for g in groups], axis=0)


def routed(x, first, width):
    lane = iota((NDEV, TILE), 1)
    x = jnp.where((lane >= first) & (lane < first + width), x, 0.0)
    place = (lane - first) & 7
    edge = jnp.where(place == 7, beside(x, -1), jnp.where(place == 0, beside(x, 1), 0.0))
    return [turned(x, -1), turned(x, 1), turned(edge, -1), edge, turned(edge, 1)]


def shifted(x, by):
    by = by % TILE
    return x if by == 0 else pltpu.roll(x, by, 1)


def spread(row, lane):
    return jnp.broadcast_to(row[:, lane : lane + 1], (1, TILE))


def owner_kernel(step, inverse_ref, message_ref, *refs):
    states = refs[:step]
    out_ref, state_ref = refs[step:]
    parts = FIRST if step == 0 else 2
    first = rows_of(message_ref, 0, parts)
    second = rows_of(message_ref, 1, parts)
    sums = [jnp.sum(first, axis=0, keepdims=True), jnp.sum(second, axis=0, keepdims=True)]
    inners = [spread(sums[1], DOT_AT + 1 + i) for i in range(step)]
    square = spread(sums[1], DOT_AT)
    for inner in inners:
        square = square - inner * inner
    length = jnp.sqrt(square)
    scale = 1.0 / length
    for i in range(step):
        for half in range(2):
            sums[half] = sums[half] - inners[i] * states[i][half : half + 1, :]
    sums = [s * scale for s in sums]
    sub, lane = iota((8, TILE), 0), iota((8, TILE), 1)
    tiled = jnp.where(sub < 4, sums[0], sums[1])
    tiled = jnp.where((lane // ROWS == sub % 4) & (sub < 6), tiled, 0.0)
    tiled = tiled + pltpu.roll(tiled, 32, 1)
    tiled = tiled + pltpu.roll(tiled, 64, 1)
    motion = [
        jnp.sum(inverse_ref[8 * half : 8 * half + 8, :] * tiled, axis=0, keepdims=True)
        for half in range(2)
    ]
    zero = jnp.zeros((1, TILE), F32)
    state_ref[...] = jnp.concatenate(
        sums + motion + [length, scale] + inners + [zero] * (2 - step), axis=0
    )
    sent = [jnp.broadcast_to(m, (NDEV, TILE)) for m in motion]
    blocks = routed(second, HALO_AT, 24)
    rim = shifted(blocks[0], -HALO_AT)
    for k in range(1, 5):
        rim = rim + shifted(blocks[k], 24 * k - HALO_AT)
    sent.append(rim)
    if step == 0:
        blocks = routed(rows_of(message_ref, 2, parts), 0, FIXED)
        for k in range(3):
            sent[1] = sent[1] + shifted(blocks[2 + k], EDGES_AT + 2 * EDGE_STEP[k])
        sent.append(blocks[0] + shifted(blocks[1], 64))
    else:
        sent.append(jnp.zeros((NDEV, TILE), F32))
    for part in range(BACK):
        out_ref[pl.ds(part, NDEV, stride=BACK), :] = sent[part]


def picked_motion(first, second, owner_ref, row_ref):
    table = jnp.concatenate([first.T, second.T[:64]], axis=0)
    high, low = split2(table)
    table = jnp.concatenate([high.astype(BF16), low.astype(BF16)], axis=1)
    owner_ids = iota((NDEV, TILE), 0)
    row_ids = iota((ROWS, TILE), 0)
    sub = iota((8, TILE), 0)
    results = []
    for block in range(BLOCKS):
        owner = owner_ref[8 * block : 8 * block + 8, :]
        row = row_ref[8 * block : 8 * block + 8, :]
        values = [jnp.zeros((8, TILE), F32) for _ in range(6)]
        for tile in range(TY) if block < 3 else (0, 7):
            pick = slice(tile, tile + 1)
            onehot = jnp.where(owner_ids == owner[pick], 1.0, 0.0).astype(BF16)
            onehot = jnp.concatenate([onehot, onehot], axis=0)
            found = jnp.dot(table, onehot, preferred_element_type=F32)
            mine = row_ids == row[pick]
            for part in range(6):
                chosen = jnp.where(mine, found[part * ROWS : (part + 1) * ROWS], 0.0)
                value = jnp.sum(chosen, axis=0, keepdims=True)
                values[part] = jnp.where(sub == tile, value, values[part])
        results.append(values)
    return results


def source_rows(get, rows_ref):
    for i, dx in enumerate((-1, 0, 1)):
        for part in range(3):
            at = 30 * part + 10 * i
            edge = get(EDGE_OF[dx], part)
            rows_ref[at : at + 1, :] = edge[7:8]
            rows_ref[at + 1 : at + 9, :] = get(ROW_OF[dx], part)
            rows_ref[at + 9 : at + 10, :] = edge[0:1]


def sources_of(rows_ref, tile):
    return [
        [rows_ref[pl.ds(30 * part + 10 * i + tile + j, 8, stride=0), :] for part in range(3)]
        for i in range(3)
        for j in range(3)
    ]


def mobility(moved, rows_ref, pairs_ref, pair_at):
    source_rows(lambda block, part: moved[block][part], rows_ref)

    def of_tile(tile, carry):
        sources = sources_of(rows_ref, tile)
        sums = [[], [], []]
        pair = pair_at(tile)
        for group in range(TILE // 8):
            terms = None
            for k in range(9):
                near, *sep = pair(group, k)
                force = sources[k]
                along = sep[0] * force[0] + sep[1] * force[1] + sep[2] * force[2]
                term = [near * force[a] + along * sep[a] for a in range(3)]
                terms = term if terms is None else [terms[a] + term[a] for a in range(3)]
            for a in range(3):
                sums[a].append(terms[a])
        for a in range(3):
            across = jnp.concatenate(sums[a], axis=0).T
            pairs_ref[pl.ds(8 * a + tile, 1), :] = jnp.sum(across, axis=0, keepdims=True)
        return carry

    lax.fori_loop(0, TY, of_tile, 0, unroll=2)
    return [pairs_ref[8 * a : 8 * a + 8, :] for a in range(3)]


def stored_pairs(pair_ref):
    def pair_at(tile):
        return lambda group, k: [pair_ref[tile, group, k, part] for part in range(4)]

    return pair_at


def new_pairs(pair_ref, own_position, rows_ref):
    columns = jnp.concatenate([own_position, jnp.zeros((104, TILE), F32)], axis=0).T

    def pair_at(tile):
        turned_columns = pltpu.roll(columns, TILE - tile, 1)
        sources = sources_of(rows_ref, tile)
        targets = {}

        def pair(group, k):
            if group not in targets:
                rows = turned_columns[8 * group : 8 * group + 8]
                targets[group] = [
                    jnp.broadcast_to(rows[:, 8 * a : 8 * a + 1], (8, TILE)) for a in range(3)
                ]
            target = targets[group]
            shift = (float(k // 3 - 1), float(k % 3 - 1), 0.0)
            sep = [target[a] - (sources[k][a] + shift[a]) for a in range(3)]
            soft = sep[0] * sep[0] + sep[1] * sep[1] + (sep[2] * sep[2] + EPS2)
            root = lax.rsqrt(soft)
            square = root * root
            scale = square * lax.rsqrt(root)
            found = [root + EPS2 * (square * root)] + [sep[a] * scale for a in range(3)]
            for part in range(4):
                pair_ref[tile, group, k, part] = found[part]
            return found

        return pair

    return pair_at


def local_kernel(step, *refs):
    refs = list(refs)
    take = lambda n: [refs.pop(0) for _ in range(n)]
    message_ref, state_ref, field_ref = take(3)
    if step == 0:
        (pack_ref,) = take(1)
    else:
        pair_ref, arm_ref, owner_ref, row_ref = take(4)
    bases = take(step)
    if step == 0:
        pair_ref, arm_ref, owner_ref, row_ref = take(4)
    basis_ref, moved_ref, fresh_ref, out_ref = take(4)
    rows_ref, pairs_ref, onehot, high, low = take(5)
    if step == 0:
        (places_ref,) = take(1)
        rows = rows_of(message_ref, 3, BACK).T
        edges = rows_of(message_ref, 1, BACK).T
        fixed = [pack_ref[0:FIXED, :], rows[:FIXED], rows[64 : 64 + FIXED]]
        for k in range(3):
            at = EDGES_AT + 2 * EDGE_STEP[k]
            fixed.append(edges[at : at + FIXED])
        for block in range(BLOCKS):
            arm_ref[24 * block : 24 * block + 24, :] = fixed[block][24:48]
            code = fixed[block][48:56].astype(jnp.int32)
            owner_ref[8 * block : 8 * block + 8, :] = lax.shift_right_logical(code, 5)
            row_ref[8 * block : 8 * block + 8, :] = code & (ROWS - 1)
        source_rows(lambda block, part: fixed[block][8 * part : 8 * part + 8], places_ref)
        pair_at = new_pairs(pair_ref, fixed[0][0:24], places_ref)
    else:
        pair_at = stored_pairs(pair_ref)
    rim = rows_of(message_ref, 2, BACK).T
    basis = jnp.concatenate([field_ref[...], rim[:120]], axis=0)
    for i in range(step):
        basis = basis - state_ref[6 + i : 7 + i, :] * bases[i][...]
    basis = basis * state_ref[5:6, :]
    basis_ref[...] = basis
    motions = picked_motion(
        rows_of(message_ref, 0, BACK), rows_of(message_ref, 1, BACK), owner_ref, row_ref
    )
    moved = []
    for block in range(BLOCKS):
        arm = [arm_ref[24 * block + 8 * a : 24 * block + 8 * a + 8, :] for a in range(3)]
        turn = cross(motions[block][3:], arm)
        moved.append(
            [
                basis[24 * block + 8 * a : 24 * block + 8 * a + 8]
                + (motions[block][a] + turn[a])
                for a in range(3)
            ]
        )
    pairs = mobility(moved, rows_ref, pairs_ref, pair_at)
    fresh = [moved[0][a] + FACTOR * pairs[a] for a in range(3)]
    for a in range(3):
        moved_ref[8 * a : 8 * a + 8, :] = moved[0][a]
        fresh_ref[8 * a : 8 * a + 8, :] = fresh[a]

    def dot(get):
        return total(fresh[0] * get(0) + fresh[1] * get(1) + fresh[2] * get(2))

    dots = [dot(lambda a: fresh[a])]
    for i in range(step):
        dots.append(dot(lambda a: bases[i][8 * a : 8 * a + 8, :]))
    dots.append(dot(lambda a: basis[8 * a : 8 * a + 8]))
    if step < ITERS - 1:
        arms = [arm_ref[8 * a : 8 * a + 8, :] for a in range(3)]
        sums = body_sums(
            fresh, arms, owner_ref[0:8, :], row_ref[0:8, :], onehot, high, low
        )
        forward_message(fresh, sums, dots, out_ref, 2)
    else:
        lane = iota((NDEV, TILE), 1)
        message = jnp.zeros((NDEV, TILE), F32)
        for at, value in enumerate(dots):
            message = jnp.where(lane == at, value, message)
        out_ref[...] = message


def final_kernel(message_ref, *refs):
    states, moved = refs[:3], refs[3:6]
    forces_ref, motion_ref = refs[6:]
    sums = jnp.sum(message_ref[...], axis=0, keepdims=True)
    beta = states[0][4:5, :]
    a = [states[1][6:7, :], states[1][4:5, :]]
    b = [states[2][6:7, :], states[2][7:8, :], states[2][4:5, :]]
    c = [spread(sums, 1 + i) for i in range(3)]
    square = spread(sums, 0) - c[0] * c[0] - c[1] * c[1] - c[2] * c[2]
    c.append(jnp.sqrt(square))
    inner = lambda p, q: sum([x * y for x, y in zip(p, q)][1:], p[0] * q[0])
    n00, n01, n02 = inner(a, a), inner(a, b), inner(a, c)
    n11, n12, n22 = inner(b, b), inner(b, c), inner(c, c)
    l00 = jnp.sqrt(n00)
    l10, l20 = n01 / l00, n02 / l00
    l11 = jnp.sqrt(n11 - l10 * l10)
    l21 = (n12 - l20 * l10) / l11
    l22 = jnp.sqrt(n22 - l20 * l20 - l21 * l21)
    t0 = beta * a[0] / l00
    t1 = (beta * b[0] - l10 * t0) / l11
    t2 = (beta * c[0] - l20 * t0 - l21 * t1) / l22
    y2 = t2 / l22
    y1 = (t1 - l21 * y2) / l11
    y0 = (t0 - l10 * y1 - l20 * y2) / l00
    forces_ref[...] = y0 * moved[0][...] + y1 * moved[1][...] + y2 * moved[2][...]
    for part in range(6):
        half, at = part // 4, (part % 4) * ROWS
        row = slice(2 + half, 3 + half)
        whole = y0 * states[0][row, :] + y1 * states[1][row, :] + y2 * states[2][row, :]
        motion_ref[part : part + 1, :] = whole[:, at : at + ROWS]


HBM = pl.BlockSpec(memory_space=pltpu.HBM)
VMEM = pl.BlockSpec(memory_space=pltpu.VMEM)


def f32(*shape):
    return jax.ShapeDtypeStruct(shape, F32)


def i32(*shape):
    return jax.ShapeDtypeStruct(shape, jnp.int32)


PAIRS = (TY, TILE // 8, 9, 4, 8, TILE)


def sums_scratch():
    return [
        pltpu.VMEM((NDEV, TY * TILE), BF16),
        pltpu.VMEM((6 * ROWS, TY * TILE), BF16),
        pltpu.VMEM((6 * ROWS, TY * TILE), BF16),
    ]


def call(body, out, scratch=(), mib=16, **options):
    return pl.pallas_call(
        body,
        out_shape=out,
        scratch_shapes=list(scratch),
        compiler_params=pltpu.CompilerParams(vmem_limit_bytes=mib * 1024 * 1024),
        **options,
    )


def exchange(message):
    return lax.all_to_all(message, CELL_WIDE, split_axis=0, concat_axis=0, tiled=True)


def local(positions, rhs, blob_owner, blob_row, blob_arm, body_inverse):
    pos = positions.reshape(24, TILE)
    field = rhs.reshape(24, TILE)
    arm = blob_arm.reshape(24, TILE)
    owner = blob_owner.reshape(TY, TILE)
    row = blob_row.reshape(TY, TILE)
    inverse = jnp.transpose(body_inverse, (1, 0, 2)).reshape(6, 6 * ROWS)
    inverse = jnp.pad(inverse, ((0, 2), (0, 64)))
    inverse = jnp.concatenate([inverse[:, :TILE], inverse[:, TILE:]], axis=0)
    message, pack, field = call(
        start_kernel,
        (f32(FIRST * NDEV, TILE), f32(TILE, TILE), f32(24, TILE)),
        [
            pltpu.VMEM((TY, TILE), jnp.int32),
            pltpu.VMEM((TY, TILE), jnp.int32),
            pltpu.SemaphoreType.DMA((5,)),
        ]
        + sums_scratch(),
        in_specs=[HBM] * 5,
    )(*[pltpu.with_memory_space_constraint(x, pltpu.HBM) for x in (pos, field, owner, row, arm)])
    states, bases, moveds = [], [], []
    for step in range(ITERS):
        arrived = exchange(message)
        message, state = call(
            lambda *refs, step=step: owner_kernel(step, *refs),
            (f32(BACK * NDEV, TILE), f32(8, TILE)),
        )(inverse, arrived, *states)
        arrived = exchange(message)
        outs = [
            f32(24 * BLOCKS, TILE),
            f32(24, TILE),
            f32(24, TILE),
            f32(NDEV if step == ITERS - 1 else 2 * NDEV, TILE),
        ]
        scratch = [pltpu.VMEM((96, TILE), F32), pltpu.VMEM((24, TILE), F32)] + sums_scratch()
        if step == 0:
            outs = [
                pltpu.VMEM(PAIRS, F32),
                f32(24 * BLOCKS, TILE),
                i32(8 * BLOCKS, TILE),
                i32(8 * BLOCKS, TILE),
            ] + outs
            scratch.append(pltpu.VMEM((96, TILE), F32))
        results = call(
            lambda *refs, step=step: local_kernel(step, *refs), tuple(outs), scratch
        )(arrived, state, field, *(fixed if step else (pack,)), *bases)
        if step == 0:
            pairs = pltpu.with_memory_space_constraint(results[0], pltpu.VMEM)
            fixed = (pairs, *results[1:4])
        basis, moved, field, message = results[-4:]
        states.append(state)
        bases.append(basis)
        moveds.append(moved)
    arrived = exchange(message)
    forces, motion = call(final_kernel, (f32(24, TILE), f32(6, ROWS)))(arrived, *states, *moveds)
    return (forces.reshape(rhs.shape), motion)


def solution(mesh):
    split = Mesh(
        mesh.devices.reshape(mesh.shape["cell"], 4, 4, 2), ("cell", "wide_0", "wide_1", "wide_2")
    )
    in_specs = (
        P(None, "cell", WIDE, None),
        P(None, "cell", WIDE, None),
        P("cell", WIDE, None, None),
        P("cell", WIDE, None),
        P(None, "cell", WIDE, None),
        P(None, None, CELL_WIDE),
    )
    out_specs = (P(None, "cell", WIDE, None), P(None, CELL_WIDE))
    return jax.shard_map(local, mesh=split, in_specs=in_specs, out_specs=out_specs, check_vma=False)
```

```python
import math

import jax
import jax.numpy as jnp
from jax import lax
from jax.experimental import pallas as pl
from jax.experimental.pallas import tpu as pltpu
from jax.sharding import Mesh
from jax.sharding import PartitionSpec as P

ITERS = 3
WIDE = ("wide_0", "wide_1", "wide_2")
CELL_WIDE = ("cell", "wide_0", "wide_1", "wide_2")
EPS2 = 0.04
KAPPA = 0.3
FACTOR = KAPPA / math.sqrt(9 * 128)
F32 = jnp.float32
BF16 = jnp.bfloat16

TY = 8
TILE = 128
NDEV = 128
NWIDE = 32
ROWS = 32
HALO_AT = 64
DOT_AT = 88
FIRST = 4
BACK = 4
FIXED = 56
BLOCKS = 6
EDGE_OF = {-1: 3, 0: 4, 1: 5}
ROW_OF = {-1: 1, 0: 0, 1: 2}
EDGES_AT = 64
EDGE_STEP = (1, 0, 2)


def iota(shape, axis):
    return lax.broadcasted_iota(jnp.int32, shape, axis)


def split2(x):
    hi = x.astype(BF16).astype(F32)
    return hi, x - hi


def cross(a, b):
    return (
        a[1] * b[2] - a[2] * b[1],
        a[2] * b[0] - a[0] * b[2],
        a[0] * b[1] - a[1] * b[0],
    )


def rows_of(message_ref, part, parts):
    return message_ref[pl.ds(part, NDEV, stride=parts), :]


def body_sums(field, arms, owner, row, onehot_ref, high_ref, low_ref):
    sent = list(field) + list(cross(arms, field))
    pieces = [split2(x) for x in sent]
    owner_ids = iota((NDEV, TILE), 0)
    row_ids = iota((ROWS, TILE), 0)
    for tile in range(TY):
        lanes = pl.ds(tile * TILE, TILE)
        pick = slice(tile, tile + 1)
        onehot_ref[:, lanes] = jnp.where(owner_ids == owner[pick], 1.0, 0.0).astype(BF16)
        mine = row_ids == row[pick]
        for part in range(6):
            place = slice(part * ROWS, (part + 1) * ROWS)
            high, low = pieces[part]
            high_ref[place, lanes] = jnp.where(mine, high[pick], 0.0).astype(BF16)
            low_ref[place, lanes] = jnp.where(mine, low[pick], 0.0).astype(BF16)
    contract = (((1,), (1,)), ((), ()))
    onehot = onehot_ref[...]
    return lax.dot_general(
        onehot, high_ref[...], contract, preferred_element_type=F32
    ) + lax.dot_general(onehot, low_ref[...], contract, preferred_element_type=F32)


def total(x):
    return jnp.sum(jnp.sum(x, axis=1, keepdims=True), axis=0, keepdims=True)


def forward_message(field, sums, dots, out_ref, parts):
    lane = iota((NDEV, TILE), 1)
    stacked = jnp.concatenate(
        [jnp.zeros((HALO_AT, TILE), F32)]
        + list(field)
        + [jnp.zeros((TILE - DOT_AT, TILE), F32)],
        axis=0,
    )
    second = jnp.concatenate([sums[:, TILE:], jnp.zeros((NDEV, 64), F32)], axis=1)
    second = second + stacked.T
    for at, dot in enumerate(dots):
        second = jnp.where(lane == DOT_AT + at, dot, second)
    out_ref[pl.ds(0, NDEV, stride=parts), :] = sums[:, :TILE]
    out_ref[pl.ds(1, NDEV, stride=parts), :] = second


def start_kernel(
    rhs_hbm, owner_hbm, row_hbm, arm_hbm, pos_hbm, inverse_hbm,
    out_ref, pack_ref, rhs_ref, inverse_ref,
    owner_ref, row_ref, sems, onehot, high, low,
):
    copies = [
        pltpu.make_async_copy(source, target, sems.at[at])
        for at, (source, target) in enumerate(
            (
                (rhs_hbm, rhs_ref),
                (owner_hbm, owner_ref),
                (row_hbm, row_ref),
                (arm_hbm, pack_ref.at[24:48, :]),
                (pos_hbm, pack_ref.at[0:24, :]),
                (inverse_hbm, inverse_ref),
            )
        )
    ]
    for copy in copies:
        copy.start()
    for copy in copies[:4]:
        copy.wait()
    field = [rhs_ref[8 * c : 8 * c + 8, :] for c in range(3)]
    arms = [pack_ref[24 + 8 * c : 32 + 8 * c, :] for c in range(3)]
    owner, row = owner_ref[...], row_ref[...]
    pack_ref[48:56, :] = (owner * ROWS + row).astype(F32)
    pack_ref[56:128, :] = jnp.zeros((72, TILE), F32)
    sums = body_sums(field, arms, owner, row, onehot, high, low)
    square = total(field[0] * field[0] + field[1] * field[1] + field[2] * field[2])
    forward_message(field, sums, [square], out_ref, FIRST)
    for copy in copies[4:]:
        copy.wait()
    out_ref[pl.ds(2, NDEV, stride=FIRST), :] = pack_ref[...].T
    out_ref[pl.ds(3, NDEV, stride=FIRST), :] = jnp.zeros((NDEV, TILE), F32)


def turned(x, by):
    by = (by % 4) * NWIDE
    return x if by == 0 else jnp.concatenate([x[by:], x[:by]], axis=0)


def beside(x, by):
    groups = [x[z * NWIDE : (z + 1) * NWIDE] for z in range(4)]
    return jnp.concatenate([pltpu.roll(g, (-by) % NWIDE, 0) for g in groups], axis=0)


def routed(x, first, width):
    lane = iota((NDEV, TILE), 1)
    x = jnp.where((lane >= first) & (lane < first + width), x, 0.0)
    place = (lane - first) & 7
    edge = jnp.where(place == 7, beside(x, -1), jnp.where(place == 0, beside(x, 1), 0.0))
    return [turned(x, -1), turned(x, 1), turned(edge, -1), edge, turned(edge, 1)]


def shifted(x, by):
    by = by % TILE
    return x if by == 0 else pltpu.roll(x, by, 1)


def spread(row, lane):
    return jnp.broadcast_to(row[:, lane : lane + 1], (1, TILE))


def owner_kernel(step, inverse_ref, message_ref, *refs):
    states = refs[:step]
    out_ref, state_ref = refs[step:]
    parts = FIRST if step == 0 else 2
    first = rows_of(message_ref, 0, parts)
    second = rows_of(message_ref, 1, parts)
    sums = [jnp.sum(first, axis=0, keepdims=True), jnp.sum(second, axis=0, keepdims=True)]
    inners = [spread(sums[1], DOT_AT + 1 + i) for i in range(step)]
    square = spread(sums[1], DOT_AT)
    for inner in inners:
        square = square - inner * inner
    length = jnp.sqrt(square)
    scale = 1.0 / length
    for i in range(step):
        for half in range(2):
            sums[half] = sums[half] - inners[i] * states[i][half : half + 1, :]
    sums = [s * scale for s in sums]
    sub, lane = iota((8, TILE), 0), iota((8, TILE), 1)
    tiled = jnp.where(sub < 4, sums[0], sums[1])
    tiled = jnp.where((lane // ROWS == sub % 4) & (sub < 6), tiled, 0.0)
    tiled = tiled + pltpu.roll(tiled, 32, 1)
    tiled = tiled + pltpu.roll(tiled, 64, 1)
    zero = jnp.zeros((1, TILE), F32)
    by_row = [inverse_ref[a] for a in range(6)]
    by_row += [jnp.zeros((6, ROWS), F32)] * 2
    motion = []
    for half in range(2):
        inverse = jnp.concatenate(by_row[4 * half : 4 * half + 4], axis=1)
        motion.append(jnp.sum(inverse * tiled[0:6], axis=0, keepdims=True))
    state_ref[...] = jnp.concatenate(
        sums + motion + [length, scale] + inners + [zero] * (2 - step), axis=0
    )
    sent = [jnp.broadcast_to(m, (NDEV, TILE)) for m in motion]
    blocks = routed(second, HALO_AT, 24)
    rim = shifted(blocks[0], -HALO_AT)
    for k in range(1, 5):
        rim = rim + shifted(blocks[k], 24 * k - HALO_AT)
    sent.append(rim)
    if step == 0:
        blocks = routed(rows_of(message_ref, 2, parts), 0, FIXED)
        for k in range(3):
            sent[1] = sent[1] + shifted(blocks[2 + k], EDGES_AT + 2 * EDGE_STEP[k])
        sent.append(blocks[0] + shifted(blocks[1], 64))
    else:
        sent.append(jnp.zeros((NDEV, TILE), F32))
    for part in range(BACK):
        out_ref[pl.ds(part, NDEV, stride=BACK), :] = sent[part]


def picked_motion(first, second, owner_ref, row_ref):
    table = jnp.concatenate([first.T, second.T[:64]], axis=0)
    high, low = split2(table)
    table = jnp.concatenate([high.astype(BF16), low.astype(BF16)], axis=1)
    owner_ids = iota((NDEV, TILE), 0)
    row_ids = iota((ROWS, TILE), 0)
    sub = iota((8, TILE), 0)
    results = []
    for block in range(BLOCKS):
        owner = owner_ref[8 * block : 8 * block + 8, :]
        row = row_ref[8 * block : 8 * block + 8, :]
        values = [jnp.zeros((8, TILE), F32) for _ in range(6)]
        for pair in ((0, 1), (2, 3), (4, 5), (6, 7)) if block < 3 else ((0, 7),):
            onehot = jnp.concatenate(
                [
                    jnp.where(owner_ids == owner[tile : tile + 1], 1.0, 0.0).astype(BF16)
                    for tile in pair
                ],
                axis=1,
            )
            onehot = jnp.concatenate([onehot, onehot], axis=0)
            found = jnp.dot(table, onehot, preferred_element_type=F32)
            for at, tile in enumerate(pair):
                mine = row_ids == row[tile : tile + 1]
                lanes = slice(at * TILE, (at + 1) * TILE)
                for part in range(6):
                    chosen = jnp.where(mine, found[part * ROWS : (part + 1) * ROWS, lanes], 0.0)
                    value = jnp.sum(chosen, axis=0, keepdims=True)
                    values[part] = jnp.where(sub == tile, value, values[part])
        results.append(values)
    return results


def source_rows(get, rows_ref):
    for i, dx in enumerate((-1, 0, 1)):
        for part in range(3):
            at = 30 * part + 10 * i
            edge = get(EDGE_OF[dx], part)
            rows_ref[at : at + 1, :] = edge[7:8]
            rows_ref[at + 1 : at + 9, :] = get(ROW_OF[dx], part)
            rows_ref[at + 9 : at + 10, :] = edge[0:1]


def sources_of(rows_ref, tile):
    return [
        [rows_ref[pl.ds(30 * part + 10 * i + tile + j, 8, stride=0), :] for part in range(3)]
        for i in range(3)
        for j in range(3)
    ]


def mobility(moved, rows_ref, pairs_ref, pair_at):
    source_rows(lambda block, part: moved[block][part], rows_ref)

    def of_tile(tile, carry):
        sources = sources_of(rows_ref, tile)
        sums = [[], [], []]
        pair = pair_at(tile)
        for group in range(TILE // 8):
            terms = None
            for k in range(9):
                near, *sep = pair(group, k)
                force = sources[k]
                along = sep[0] * force[0] + sep[1] * force[1] + sep[2] * force[2]
                term = [near * force[a] + along * sep[a] for a in range(3)]
                terms = term if terms is None else [terms[a] + term[a] for a in range(3)]
            for a in range(3):
                sums[a].append(terms[a])
        for a in range(3):
            across = jnp.concatenate(sums[a], axis=0).T
            pairs_ref[pl.ds(8 * a + tile, 1), :] = jnp.sum(across, axis=0, keepdims=True)
        return carry

    lax.fori_loop(0, TY, of_tile, 0, unroll=4)
    return [pairs_ref[8 * a : 8 * a + 8, :] for a in range(3)]


def stored_pairs(pair_ref):
    def pair_at(tile):
        return lambda group, k: [pair_ref[tile, group, k, part] for part in range(4)]

    return pair_at


def new_pairs(pair_ref, own_position, rows_ref):
    columns = jnp.concatenate([own_position, jnp.zeros((104, TILE), F32)], axis=0).T

    def pair_at(tile):
        turned_columns = pltpu.roll(columns, TILE - tile, 1)
        sources = sources_of(rows_ref, tile)
        targets = {}

        def pair(group, k):
            if group not in targets:
                rows = turned_columns[8 * group : 8 * group + 8]
                targets[group] = [
                    jnp.broadcast_to(rows[:, 8 * a : 8 * a + 1], (8, TILE)) for a in range(3)
                ]
            target = targets[group]
            shift = (float(k // 3 - 1), float(k % 3 - 1), 0.0)
            sep = [target[a] - (sources[k][a] + shift[a]) for a in range(3)]
            soft = sep[0] * sep[0] + sep[1] * sep[1] + (sep[2] * sep[2] + EPS2)
            root = lax.rsqrt(soft)
            square = root * root
            scale = square * lax.rsqrt(root)
            found = [root + EPS2 * (square * root)] + [sep[a] * scale for a in range(3)]
            for part in range(4):
                pair_ref[tile, group, k, part] = found[part]
            return found

        return pair

    return pair_at


def local_kernel(step, *refs):
    refs = list(refs)
    take = lambda n: [refs.pop(0) for _ in range(n)]
    message_ref, state_ref, field_ref = take(3)
    if step == 0:
        (pack_ref,) = take(1)
    else:
        pair_ref, arm_ref, owner_ref, row_ref = take(4)
    bases = take(step)
    if step == 0:
        pair_ref, arm_ref, owner_ref, row_ref = take(4)
    if step < ITERS - 1:
        basis_ref, fresh_ref = take(2)
    moved_ref, out_ref = take(2)
    rows_ref, pairs_ref, onehot, high, low = take(5)
    if step == 0:
        (places_ref,) = take(1)
        rows = rows_of(message_ref, 3, BACK).T
        edges = rows_of(message_ref, 1, BACK).T
        fixed = [pack_ref[0:FIXED, :], rows[:FIXED], rows[64 : 64 + FIXED]]
        for k in range(3):
            at = EDGES_AT + 2 * EDGE_STEP[k]
            fixed.append(edges[at : at + FIXED])
        for block in range(BLOCKS):
            arm_ref[24 * block : 24 * block + 24, :] = fixed[block][24:48]
            code = fixed[block][48:56].astype(jnp.int32)
            owner_ref[8 * block : 8 * block + 8, :] = lax.shift_right_logical(code, 5)
            row_ref[8 * block : 8 * block + 8, :] = code & (ROWS - 1)
        source_rows(lambda block, part: fixed[block][8 * part : 8 * part + 8], places_ref)
        pair_at = new_pairs(pair_ref, fixed[0][0:24], places_ref)
    else:
        pair_at = stored_pairs(pair_ref)
    rim = rows_of(message_ref, 2, BACK).T
    basis = jnp.concatenate([field_ref[...], rim[:120]], axis=0)
    for i in range(step):
        basis = basis - state_ref[6 + i : 7 + i, :] * bases[i][...]
    basis = basis * state_ref[5:6, :]
    motions = picked_motion(
        rows_of(message_ref, 0, BACK), rows_of(message_ref, 1, BACK), owner_ref, row_ref
    )
    moved = []
    for block in range(BLOCKS):
        arm = [arm_ref[24 * block + 8 * a : 24 * block + 8 * a + 8, :] for a in range(3)]
        turn = cross(motions[block][3:], arm)
        moved.append(
            [
                basis[24 * block + 8 * a : 24 * block + 8 * a + 8]
                + (motions[block][a] + turn[a])
                for a in range(3)
            ]
        )
    pairs = mobility(moved, rows_ref, pairs_ref, pair_at)
    fresh = [moved[0][a] + FACTOR * pairs[a] for a in range(3)]
    for a in range(3):
        moved_ref[8 * a : 8 * a + 8, :] = moved[0][a]

    def dot(get):
        return total(fresh[0] * get(0) + fresh[1] * get(1) + fresh[2] * get(2))

    dots = [dot(lambda a: fresh[a])]
    for i in range(step):
        dots.append(dot(lambda a: bases[i][8 * a : 8 * a + 8, :]))
    dots.append(dot(lambda a: basis[8 * a : 8 * a + 8]))
    if step < ITERS - 1:
        basis_ref[...] = basis
        for a in range(3):
            fresh_ref[8 * a : 8 * a + 8, :] = fresh[a]
        arms = [arm_ref[8 * a : 8 * a + 8, :] for a in range(3)]
        sums = body_sums(
            fresh, arms, owner_ref[0:8, :], row_ref[0:8, :], onehot, high, low
        )
        forward_message(fresh, sums, dots, out_ref, 2)
    else:
        lane = iota((NDEV, TILE), 1)
        message = jnp.zeros((NDEV, TILE), F32)
        for at, value in enumerate(dots):
            message = jnp.where(lane == at, value, message)
        out_ref[...] = message


def final_kernel(message_ref, *refs):
    states, moved = refs[:3], refs[3:6]
    forces_ref, motion_ref = refs[6:]
    sums = jnp.sum(message_ref[...], axis=0, keepdims=True)
    beta = states[0][4:5, :]
    a = [states[1][6:7, :], states[1][4:5, :]]
    b = [states[2][6:7, :], states[2][7:8, :], states[2][4:5, :]]
    c = [spread(sums, 1 + i) for i in range(3)]
    square = spread(sums, 0) - c[0] * c[0] - c[1] * c[1] - c[2] * c[2]
    c.append(jnp.sqrt(square))
    inner = lambda p, q: sum([x * y for x, y in zip(p, q)][1:], p[0] * q[0])
    n00, n01, n02 = inner(a, a), inner(a, b), inner(a, c)
    n11, n12, n22 = inner(b, b), inner(b, c), inner(c, c)
    l00 = jnp.sqrt(n00)
    l10, l20 = n01 / l00, n02 / l00
    l11 = jnp.sqrt(n11 - l10 * l10)
    l21 = (n12 - l20 * l10) / l11
    l22 = jnp.sqrt(n22 - l20 * l20 - l21 * l21)
    t0 = beta * a[0] / l00
    t1 = (beta * b[0] - l10 * t0) / l11
    t2 = (beta * c[0] - l20 * t0 - l21 * t1) / l22
    y2 = t2 / l22
    y1 = (t1 - l21 * y2) / l11
    y0 = (t0 - l10 * y1 - l20 * y2) / l00
    forces_ref[...] = y0 * moved[0][...] + y1 * moved[1][...] + y2 * moved[2][...]
    for part in range(6):
        half, at = part // 4, (part % 4) * ROWS
        row = slice(2 + half, 3 + half)
        whole = y0 * states[0][row, :] + y1 * states[1][row, :] + y2 * states[2][row, :]
        motion_ref[part : part + 1, :] = whole[:, at : at + ROWS]


HBM = pl.BlockSpec(memory_space=pltpu.HBM)
VMEM = pl.BlockSpec(memory_space=pltpu.VMEM)


def f32(*shape):
    return jax.ShapeDtypeStruct(shape, F32)


def i32(*shape):
    return jax.ShapeDtypeStruct(shape, jnp.int32)


PAIRS = (TY, TILE // 8, 9, 4, 8, TILE)


def sums_scratch():
    return [
        pltpu.VMEM((NDEV, TY * TILE), BF16),
        pltpu.VMEM((6 * ROWS, TY * TILE), BF16),
        pltpu.VMEM((6 * ROWS, TY * TILE), BF16),
    ]


def call(body, out, scratch=(), mib=16, **options):
    return pl.pallas_call(
        body,
        out_shape=out,
        scratch_shapes=list(scratch),
        compiler_params=pltpu.CompilerParams(vmem_limit_bytes=mib * 1024 * 1024),
        **options,
    )


def exchange(message):
    return lax.all_to_all(message, CELL_WIDE, split_axis=0, concat_axis=0, tiled=True)


def local(positions, rhs, blob_owner, blob_row, blob_arm, body_inverse):
    pos = positions.reshape(24, TILE)
    field = rhs.reshape(24, TILE)
    arm = blob_arm.reshape(24, TILE)
    owner = blob_owner.reshape(TY, TILE)
    row = blob_row.reshape(TY, TILE)
    held = (field, owner, row, arm, pos, body_inverse)
    message, pack, field, inverse = call(
        start_kernel,
        (f32(FIRST * NDEV, TILE), f32(TILE, TILE), f32(24, TILE), f32(6, 6, ROWS)),
        [
            pltpu.VMEM((TY, TILE), jnp.int32),
            pltpu.VMEM((TY, TILE), jnp.int32),
            pltpu.SemaphoreType.DMA((6,)),
        ]
        + sums_scratch(),
        in_specs=[HBM] * 6,
    )(*[pltpu.with_memory_space_constraint(x, pltpu.HBM) for x in held])
    states, bases, moveds = [], [], []
    for step in range(ITERS):
        arrived = exchange(message)
        message, state = call(
            lambda *refs, step=step: owner_kernel(step, *refs),
            (f32(BACK * NDEV, TILE), f32(8, TILE)),
        )(inverse, arrived, *states)
        arrived = exchange(message)
        last = step == ITERS - 1
        outs = [f32(24, TILE), f32(NDEV if last else 2 * NDEV, TILE)]
        if not last:
            outs = [f32(24 * BLOCKS, TILE), f32(24, TILE)] + outs
        scratch = [pltpu.VMEM((96, TILE), F32), pltpu.VMEM((24, TILE), F32)] + sums_scratch()
        if step == 0:
            outs = [
                pltpu.VMEM(PAIRS, F32),
                f32(24 * BLOCKS, TILE),
                i32(8 * BLOCKS, TILE),
                i32(8 * BLOCKS, TILE),
            ] + outs
            scratch.append(pltpu.VMEM((96, TILE), F32))
        results = call(
            lambda *refs, step=step: local_kernel(step, *refs), tuple(outs), scratch
        )(arrived, state, field, *(fixed if step else (pack,)), *bases)
        if step == 0:
            pairs = pltpu.with_memory_space_constraint(results[0], pltpu.VMEM)
            fixed = (pairs, *results[1:4])
        moved, message = results[-2:]
        states.append(state)
        moveds.append(moved)
        if not last:
            bases.append(results[-4])
            field = results[-3]
    arrived = exchange(message)
    forces, motion = call(final_kernel, (f32(24, TILE), f32(6, ROWS)))(arrived, *states, *moveds)
    return (forces.reshape(rhs.shape), motion)


def solution(mesh):
    split = Mesh(
        mesh.devices.reshape(mesh.shape["cell"], 4, 4, 2), ("cell", "wide_0", "wide_1", "wide_2")
    )
    in_specs = (
        P(None, "cell", WIDE, None),
        P(None, "cell", WIDE, None),
        P("cell", WIDE, None, None),
        P("cell", WIDE, None),
        P(None, "cell", WIDE, None),
        P(None, None, CELL_WIDE),
    )
    out_specs = (P(None, "cell", WIDE, None), P(None, CELL_WIDE))
    return jax.shard_map(local, mesh=split, in_specs=in_specs, out_specs=out_specs, check_vma=False)
```

```python
import math

import jax
import jax.numpy as jnp
from jax import lax
from jax.experimental import pallas as pl
from jax.experimental.pallas import tpu as pltpu
from jax.sharding import Mesh
from jax.sharding import PartitionSpec as P

ITERS = 3
WIDE = ("wide_0", "wide_1", "wide_2")
CELL_WIDE = ("cell", "wide_0", "wide_1", "wide_2")
EPS2 = 0.04
KAPPA = 0.3
FACTOR = KAPPA / math.sqrt(9 * 128)
F32 = jnp.float32
BF16 = jnp.bfloat16

TY = 8
TILE = 128
NDEV = 128
NWIDE = 32
ROWS = 32
HALO_AT = 64
DOT_AT = 88
FIRST = 3
BACK = (4, 3, 3)
FIXED = 56
BLOCKS = 6
EDGE_OF = {-1: 3, 0: 4, 1: 5}
ROW_OF = {-1: 1, 0: 0, 1: 2}
EDGES_AT = 64
EDGE_STEP = (1, 0, 2)


def iota(shape, axis):
    return lax.broadcasted_iota(jnp.int32, shape, axis)


def split2(x):
    hi = x.astype(BF16).astype(F32)
    return hi, x - hi


def cross(a, b):
    return (
        a[1] * b[2] - a[2] * b[1],
        a[2] * b[0] - a[0] * b[2],
        a[0] * b[1] - a[1] * b[0],
    )


def rows_of(message_ref, part, parts):
    return message_ref[pl.ds(part, NDEV, stride=parts), :]


def body_sums(field, arms, owner, row, onehot_ref, high_ref, low_ref):
    sent = list(field) + list(cross(arms, field))
    pieces = [split2(x) for x in sent]
    owner_ids = iota((NDEV, TILE), 0)
    row_ids = iota((ROWS, TILE), 0)
    for tile in range(TY):
        lanes = pl.ds(tile * TILE, TILE)
        pick = slice(tile, tile + 1)
        onehot_ref[:, lanes] = jnp.where(owner_ids == owner[pick], 1.0, 0.0).astype(BF16)
        mine = row_ids == row[pick]
        for part in range(6):
            place = slice(part * ROWS, (part + 1) * ROWS)
            high, low = pieces[part]
            high_ref[place, lanes] = jnp.where(mine, high[pick], 0.0).astype(BF16)
            low_ref[place, lanes] = jnp.where(mine, low[pick], 0.0).astype(BF16)
    contract = (((1,), (1,)), ((), ()))
    onehot = onehot_ref[...]
    return lax.dot_general(
        onehot, high_ref[...], contract, preferred_element_type=F32
    ) + lax.dot_general(onehot, low_ref[...], contract, preferred_element_type=F32)


def total(x):
    return jnp.sum(jnp.sum(x, axis=1, keepdims=True), axis=0, keepdims=True)


def forward_message(field, sums, dots, out_ref, parts):
    lane = iota((NDEV, TILE), 1)
    stacked = jnp.concatenate(
        [jnp.zeros((HALO_AT, TILE), F32)]
        + list(field)
        + [jnp.zeros((TILE - DOT_AT, TILE), F32)],
        axis=0,
    )
    second = jnp.concatenate([sums[:, TILE:], jnp.zeros((NDEV, 64), F32)], axis=1)
    second = second + stacked.T
    for at, dot in enumerate(dots):
        second = jnp.where(lane == DOT_AT + at, dot, second)
    out_ref[pl.ds(0, NDEV, stride=parts), :] = sums[:, :TILE]
    out_ref[pl.ds(1, NDEV, stride=parts), :] = second


def start_kernel(
    rhs_hbm, owner_hbm, row_hbm, arm_hbm, pos_hbm, inverse_hbm,
    out_ref, pack_ref, rhs_ref, inverse_ref,
    owner_ref, row_ref, sems, onehot, high, low,
):
    copies = [
        pltpu.make_async_copy(source, target, sems.at[at])
        for at, (source, target) in enumerate(
            (
                (rhs_hbm, rhs_ref),
                (owner_hbm, owner_ref),
                (row_hbm, row_ref),
                (arm_hbm, pack_ref.at[24:48, :]),
                (pos_hbm, pack_ref.at[0:24, :]),
                (inverse_hbm, inverse_ref),
            )
        )
    ]
    for copy in copies:
        copy.start()
    for copy in copies[:4]:
        copy.wait()
    field = [rhs_ref[8 * c : 8 * c + 8, :] for c in range(3)]
    arms = [pack_ref[24 + 8 * c : 32 + 8 * c, :] for c in range(3)]
    owner, row = owner_ref[...], row_ref[...]
    pack_ref[48:56, :] = (owner * ROWS + row).astype(F32)
    pack_ref[56:128, :] = jnp.zeros((72, TILE), F32)
    sums = body_sums(field, arms, owner, row, onehot, high, low)
    square = total(field[0] * field[0] + field[1] * field[1] + field[2] * field[2])
    forward_message(field, sums, [square], out_ref, FIRST)
    for copy in copies[4:]:
        copy.wait()
    out_ref[pl.ds(2, NDEV, stride=FIRST), :] = pack_ref[...].T


def turned(x, by):
    by = (by % 4) * NWIDE
    return x if by == 0 else jnp.concatenate([x[by:], x[:by]], axis=0)


def beside(x, by):
    groups = [x[z * NWIDE : (z + 1) * NWIDE] for z in range(4)]
    return jnp.concatenate([pltpu.roll(g, (-by) % NWIDE, 0) for g in groups], axis=0)


def routed(x, first, width):
    lane = iota((NDEV, TILE), 1)
    x = jnp.where((lane >= first) & (lane < first + width), x, 0.0)
    place = (lane - first) & 7
    edge = jnp.where(place == 7, beside(x, -1), jnp.where(place == 0, beside(x, 1), 0.0))
    return [turned(x, -1), turned(x, 1), turned(edge, -1), edge, turned(edge, 1)]


def shifted(x, by):
    by = by % TILE
    return x if by == 0 else pltpu.roll(x, by, 1)


def spread(row, lane):
    return jnp.broadcast_to(row[:, lane : lane + 1], (1, TILE))


def owner_kernel(step, inverse_ref, message_ref, *refs):
    states = refs[:step]
    out_ref, state_ref = refs[step:]
    parts = FIRST if step == 0 else 2
    first = rows_of(message_ref, 0, parts)
    second = rows_of(message_ref, 1, parts)
    sums = [jnp.sum(first, axis=0, keepdims=True), jnp.sum(second, axis=0, keepdims=True)]
    inners = [spread(sums[1], DOT_AT + 1 + i) for i in range(step)]
    square = spread(sums[1], DOT_AT)
    for inner in inners:
        square = square - inner * inner
    length = jnp.sqrt(square)
    scale = 1.0 / length
    for i in range(step):
        for half in range(2):
            sums[half] = sums[half] - inners[i] * states[i][half : half + 1, :]
    sums = [s * scale for s in sums]
    sub, lane = iota((8, TILE), 0), iota((8, TILE), 1)
    tiled = jnp.where(sub < 4, sums[0], sums[1])
    tiled = jnp.where((lane // ROWS == sub % 4) & (sub < 6), tiled, 0.0)
    tiled = tiled + pltpu.roll(tiled, 32, 1)
    tiled = tiled + pltpu.roll(tiled, 64, 1)
    zero = jnp.zeros((1, TILE), F32)
    by_row = [inverse_ref[a] for a in range(6)]
    by_row += [jnp.zeros((6, ROWS), F32)] * 2
    motion = []
    for half in range(2):
        inverse = jnp.concatenate(by_row[4 * half : 4 * half + 4], axis=1)
        motion.append(jnp.sum(inverse * tiled[0:6], axis=0, keepdims=True))
    state_ref[...] = jnp.concatenate(
        sums + motion + [length, scale] + inners + [zero] * (2 - step), axis=0
    )
    sent = [jnp.broadcast_to(m, (NDEV, TILE)) for m in motion]
    blocks = routed(second, HALO_AT, 24)
    rim = shifted(blocks[0], -HALO_AT)
    for k in range(1, 5):
        rim = rim + shifted(blocks[k], 24 * k - HALO_AT)
    sent.append(rim)
    if step == 0:
        blocks = routed(rows_of(message_ref, 2, parts), 0, FIXED)
        for k in range(3):
            sent[1] = sent[1] + shifted(blocks[2 + k], EDGES_AT + 2 * EDGE_STEP[k])
        sent.append(blocks[0] + shifted(blocks[1], 64))
    for part in range(BACK[step]):
        out_ref[pl.ds(part, NDEV, stride=BACK[step]), :] = sent[part]


def picked_motion(first, second, owner_ref, row_ref):
    table = jnp.concatenate([first.T, second.T[:64]], axis=0)
    high, low = split2(table)
    table = jnp.concatenate([high.astype(BF16), low.astype(BF16)], axis=1)
    owner_ids = iota((NDEV, TILE), 0)
    row_ids = iota((ROWS, TILE), 0)
    sub = iota((8, TILE), 0)
    results = []
    for block in range(BLOCKS):
        owner = owner_ref[8 * block : 8 * block + 8, :]
        row = row_ref[8 * block : 8 * block + 8, :]
        values = [jnp.zeros((8, TILE), F32) for _ in range(6)]
        for pair in ((0, 1), (2, 3), (4, 5), (6, 7)) if block < 3 else ((0, 7),):
            onehot = jnp.concatenate(
                [
                    jnp.where(owner_ids == owner[tile : tile + 1], 1.0, 0.0).astype(BF16)
                    for tile in pair
                ],
                axis=1,
            )
            onehot = jnp.concatenate([onehot, onehot], axis=0)
            found = jnp.dot(table, onehot, preferred_element_type=F32)
            for at, tile in enumerate(pair):
                mine = row_ids == row[tile : tile + 1]
                lanes = slice(at * TILE, (at + 1) * TILE)
                for part in range(6):
                    chosen = jnp.where(mine, found[part * ROWS : (part + 1) * ROWS, lanes], 0.0)
                    value = jnp.sum(chosen, axis=0, keepdims=True)
                    values[part] = jnp.where(sub == tile, value, values[part])
        results.append(values)
    return results


def source_rows(get, rows_ref):
    for i, dx in enumerate((-1, 0, 1)):
        for part in range(3):
            at = 30 * part + 10 * i
            edge = get(EDGE_OF[dx], part)
            rows_ref[at : at + 1, :] = edge[7:8]
            rows_ref[at + 1 : at + 9, :] = get(ROW_OF[dx], part)
            rows_ref[at + 9 : at + 10, :] = edge[0:1]


def sources_of(rows_ref, tile):
    return [
        [rows_ref[pl.ds(30 * part + 10 * i + tile + j, 8, stride=0), :] for part in range(3)]
        for i in range(3)
        for j in range(3)
    ]


def mobility(moved, rows_ref, pairs_ref, pair_at):
    source_rows(lambda block, part: moved[block][part], rows_ref)

    def of_tile(tile, carry):
        sources = sources_of(rows_ref, tile)
        sums = [[], [], []]
        pair = pair_at(tile)
        for group in range(TILE // 8):
            terms = None
            for k in range(9):
                near, *sep = pair(group, k)
                force = sources[k]
                along = sep[0] * force[0] + sep[1] * force[1] + sep[2] * force[2]
                term = [near * force[a] + along * sep[a] for a in range(3)]
                terms = term if terms is None else [terms[a] + term[a] for a in range(3)]
            for a in range(3):
                sums[a].append(terms[a])
        for a in range(3):
            across = jnp.concatenate(sums[a], axis=0).T
            pairs_ref[pl.ds(8 * a + tile, 1), :] = jnp.sum(across, axis=0, keepdims=True)
        return carry

    lax.fori_loop(0, TY, of_tile, 0, unroll=4)
    return [pairs_ref[8 * a : 8 * a + 8, :] for a in range(3)]


def stored_pairs(pair_ref):
    def pair_at(tile):
        return lambda group, k: [pair_ref[tile, group, k, part] for part in range(4)]

    return pair_at


def new_pairs(pair_ref, own_position, rows_ref):
    columns = jnp.concatenate([own_position, jnp.zeros((104, TILE), F32)], axis=0).T

    def pair_at(tile):
        turned_columns = pltpu.roll(columns, TILE - tile, 1)
        sources = sources_of(rows_ref, tile)
        targets = {}

        def pair(group, k):
            if group not in targets:
                rows = turned_columns[8 * group : 8 * group + 8]
                targets[group] = [
                    jnp.broadcast_to(rows[:, 8 * a : 8 * a + 1], (8, TILE)) for a in range(3)
                ]
            target = targets[group]
            shift = (float(k // 3 - 1), float(k % 3 - 1), 0.0)
            sep = [target[a] - (sources[k][a] + shift[a]) for a in range(3)]
            soft = sep[0] * sep[0] + sep[1] * sep[1] + (sep[2] * sep[2] + EPS2)
            root = lax.rsqrt(soft)
            square = root * root
            scale = square * lax.rsqrt(root)
            found = [root + EPS2 * (square * root)] + [sep[a] * scale for a in range(3)]
            for part in range(4):
                pair_ref[tile, group, k, part] = found[part]
            return found

        return pair

    return pair_at


def local_kernel(step, *refs):
    refs = list(refs)
    back = BACK[step]
    take = lambda n: [refs.pop(0) for _ in range(n)]
    message_ref, state_ref, field_ref = take(3)
    if step == 0:
        (pack_ref,) = take(1)
    else:
        pair_ref, arm_ref, owner_ref, row_ref = take(4)
    bases = take(step)
    if step == 0:
        pair_ref, arm_ref, owner_ref, row_ref = take(4)
    if step < ITERS - 1:
        basis_ref, fresh_ref = take(2)
    moved_ref, out_ref = take(2)
    rows_ref, pairs_ref, onehot, high, low = take(5)
    if step == 0:
        (places_ref,) = take(1)
        rows = rows_of(message_ref, 3, back).T
        edges = rows_of(message_ref, 1, back).T
        fixed = [pack_ref[0:FIXED, :], rows[:FIXED], rows[64 : 64 + FIXED]]
        for k in range(3):
            at = EDGES_AT + 2 * EDGE_STEP[k]
            fixed.append(edges[at : at + FIXED])
        for block in range(BLOCKS):
            arm_ref[24 * block : 24 * block + 24, :] = fixed[block][24:48]
            code = fixed[block][48:56].astype(jnp.int32)
            owner_ref[8 * block : 8 * block + 8, :] = lax.shift_right_logical(code, 5)
            row_ref[8 * block : 8 * block + 8, :] = code & (ROWS - 1)
        source_rows(lambda block, part: fixed[block][8 * part : 8 * part + 8], places_ref)
        pair_at = new_pairs(pair_ref, fixed[0][0:24], places_ref)
    else:
        pair_at = stored_pairs(pair_ref)
    rim = rows_of(message_ref, 2, back).T
    basis = jnp.concatenate([field_ref[...], rim[:120]], axis=0)
    for i in range(step):
        basis = basis - state_ref[6 + i : 7 + i, :] * bases[i][...]
    basis = basis * state_ref[5:6, :]
    motions = picked_motion(
        rows_of(message_ref, 0, back), rows_of(message_ref, 1, back), owner_ref, row_ref
    )
    moved = []
    for block in range(BLOCKS):
        arm = [arm_ref[24 * block + 8 * a : 24 * block + 8 * a + 8, :] for a in range(3)]
        turn = cross(motions[block][3:], arm)
        moved.append(
            [
                basis[24 * block + 8 * a : 24 * block + 8 * a + 8]
                + (motions[block][a] + turn[a])
                for a in range(3)
            ]
        )
    pairs = mobility(moved, rows_ref, pairs_ref, pair_at)
    fresh = [moved[0][a] + FACTOR * pairs[a] for a in range(3)]
    for a in range(3):
        moved_ref[8 * a : 8 * a + 8, :] = moved[0][a]

    def dot(get):
        return total(fresh[0] * get(0) + fresh[1] * get(1) + fresh[2] * get(2))

    dots = [dot(lambda a: fresh[a])]
    for i in range(step):
        dots.append(dot(lambda a: bases[i][8 * a : 8 * a + 8, :]))
    dots.append(dot(lambda a: basis[8 * a : 8 * a + 8]))
    if step < ITERS - 1:
        basis_ref[...] = basis
        for a in range(3):
            fresh_ref[8 * a : 8 * a + 8, :] = fresh[a]
        arms = [arm_ref[8 * a : 8 * a + 8, :] for a in range(3)]
        sums = body_sums(
            fresh, arms, owner_ref[0:8, :], row_ref[0:8, :], onehot, high, low
        )
        forward_message(fresh, sums, dots, out_ref, 2)
    else:
        lane = iota((NDEV, TILE), 1)
        message = jnp.zeros((NDEV, TILE), F32)
        for at, value in enumerate(dots):
            message = jnp.where(lane == at, value, message)
        out_ref[...] = message


def final_kernel(message_ref, *refs):
    states, moved = refs[:3], refs[3:6]
    forces_ref, motion_ref = refs[6:]
    sums = jnp.sum(message_ref[...], axis=0, keepdims=True)
    beta = states[0][4:5, :]
    a = [states[1][6:7, :], states[1][4:5, :]]
    b = [states[2][6:7, :], states[2][7:8, :], states[2][4:5, :]]
    c = [spread(sums, 1 + i) for i in range(3)]
    square = spread(sums, 0) - c[0] * c[0] - c[1] * c[1] - c[2] * c[2]
    c.append(jnp.sqrt(square))
    inner = lambda p, q: sum([x * y for x, y in zip(p, q)][1:], p[0] * q[0])
    n00, n01, n02 = inner(a, a), inner(a, b), inner(a, c)
    n11, n12, n22 = inner(b, b), inner(b, c), inner(c, c)
    l00 = jnp.sqrt(n00)
    l10, l20 = n01 / l00, n02 / l00
    l11 = jnp.sqrt(n11 - l10 * l10)
    l21 = (n12 - l20 * l10) / l11
    l22 = jnp.sqrt(n22 - l20 * l20 - l21 * l21)
    t0 = beta * a[0] / l00
    t1 = (beta * b[0] - l10 * t0) / l11
    t2 = (beta * c[0] - l20 * t0 - l21 * t1) / l22
    y2 = t2 / l22
    y1 = (t1 - l21 * y2) / l11
    y0 = (t0 - l10 * y1 - l20 * y2) / l00
    forces_ref[...] = y0 * moved[0][...] + y1 * moved[1][...] + y2 * moved[2][...]
    for part in range(6):
        half, at = part // 4, (part % 4) * ROWS
        row = slice(2 + half, 3 + half)
        whole = y0 * states[0][row, :] + y1 * states[1][row, :] + y2 * states[2][row, :]
        motion_ref[part : part + 1, :] = whole[:, at : at + ROWS]


HBM = pl.BlockSpec(memory_space=pltpu.HBM)
VMEM = pl.BlockSpec(memory_space=pltpu.VMEM)


def f32(*shape):
    return jax.ShapeDtypeStruct(shape, F32)


def i32(*shape):
    return jax.ShapeDtypeStruct(shape, jnp.int32)


PAIRS = (TY, TILE // 8, 9, 4, 8, TILE)


def sums_scratch():
    return [
        pltpu.VMEM((NDEV, TY * TILE), BF16),
        pltpu.VMEM((6 * ROWS, TY * TILE), BF16),
        pltpu.VMEM((6 * ROWS, TY * TILE), BF16),
    ]


def call(body, out, scratch=(), mib=16, **options):
    return pl.pallas_call(
        body,
        out_shape=out,
        scratch_shapes=list(scratch),
        compiler_params=pltpu.CompilerParams(vmem_limit_bytes=mib * 1024 * 1024),
        **options,
    )


def exchange(message):
    rows = message.shape[0]
    moved = message.reshape(NDEV, 1, rows * TILE // NDEV)
    moved = lax.all_to_all(moved, CELL_WIDE, split_axis=0, concat_axis=0, tiled=True)
    return moved.reshape(rows, TILE)


def local(positions, rhs, blob_owner, blob_row, blob_arm, body_inverse):
    pos = positions.reshape(24, TILE)
    field = rhs.reshape(24, TILE)
    arm = blob_arm.reshape(24, TILE)
    owner = blob_owner.reshape(TY, TILE)
    row = blob_row.reshape(TY, TILE)
    held = (field, owner, row, arm, pos, body_inverse)
    message, pack, field, inverse = call(
        start_kernel,
        (f32(FIRST * NDEV, TILE), f32(TILE, TILE), f32(24, TILE), f32(6, 6, ROWS)),
        [
            pltpu.VMEM((TY, TILE), jnp.int32),
            pltpu.VMEM((TY, TILE), jnp.int32),
            pltpu.SemaphoreType.DMA((6,)),
        ]
        + sums_scratch(),
        in_specs=[HBM] * 6,
    )(*[pltpu.with_memory_space_constraint(x, pltpu.HBM) for x in held])
    states, bases, moveds = [], [], []
    for step in range(ITERS):
        arrived = exchange(message)
        message, state = call(
            lambda *refs, step=step: owner_kernel(step, *refs),
            (f32(BACK[step] * NDEV, TILE), f32(8, TILE)),
        )(inverse, arrived, *states)
        arrived = exchange(message)
        last = step == ITERS - 1
        outs = [f32(24, TILE), f32(NDEV if last else 2 * NDEV, TILE)]
        if not last:
            outs = [f32(24 * BLOCKS, TILE), f32(24, TILE)] + outs
        scratch = [pltpu.VMEM((96, TILE), F32), pltpu.VMEM((24, TILE), F32)] + sums_scratch()
        if step == 0:
            outs = [
                pltpu.VMEM(PAIRS, F32),
                f32(24 * BLOCKS, TILE),
                i32(8 * BLOCKS, TILE),
                i32(8 * BLOCKS, TILE),
            ] + outs
            scratch.append(pltpu.VMEM((96, TILE), F32))
        results = call(
            lambda *refs, step=step: local_kernel(step, *refs), tuple(outs), scratch
        )(arrived, state, field, *(fixed if step else (pack,)), *bases)
        if step == 0:
            pairs = pltpu.with_memory_space_constraint(results[0], pltpu.VMEM)
            fixed = (pairs, *results[1:4])
        moved, message = results[-2:]
        states.append(state)
        moveds.append(moved)
        if not last:
            bases.append(results[-4])
            field = results[-3]
    arrived = exchange(message)
    forces, motion = call(final_kernel, (f32(24, TILE), f32(6, ROWS)))(arrived, *states, *moveds)
    return (forces.reshape(rhs.shape), motion)


def solution(mesh):
    split = Mesh(
        mesh.devices.reshape(mesh.shape["cell"], 4, 4, 2), ("cell", "wide_0", "wide_1", "wide_2")
    )
    in_specs = (
        P(None, "cell", WIDE, None),
        P(None, "cell", WIDE, None),
        P("cell", WIDE, None, None),
        P("cell", WIDE, None),
        P(None, "cell", WIDE, None),
        P(None, None, CELL_WIDE),
    )
    out_specs = (P(None, "cell", WIDE, None), P(None, CELL_WIDE))
    return jax.shard_map(local, mesh=split, in_specs=in_specs, out_specs=out_specs, check_vma=False)
```

```python
import math

import jax
import jax.numpy as jnp
from jax import lax
from jax.experimental import pallas as pl
from jax.experimental.pallas import tpu as pltpu
from jax.sharding import Mesh
from jax.sharding import PartitionSpec as P

ITERS = 3
WIDE = ("wide_0", "wide_1", "wide_2")
CELL_WIDE = ("cell", "wide_0", "wide_1", "wide_2")
EPS2 = 0.04
KAPPA = 0.3
FACTOR = KAPPA / math.sqrt(9 * 128)
F32 = jnp.float32
BF16 = jnp.bfloat16

TY = 8
TILE = 128
NDEV = 128
NWIDE = 32
ROWS = 32
HALO_AT = 64
DOT_AT = 88
FIRST = 3
BACK = (4, 4, 3)
FIXED = 56
BLOCKS = 6
EDGE_OF = {-1: 3, 0: 4, 1: 5}
ROW_OF = {-1: 1, 0: 0, 1: 2}
EDGES_AT = 64
EDGE_STEP = (1, 0, 2)


def iota(shape, axis):
    return lax.broadcasted_iota(jnp.int32, shape, axis)


def split2(x):
    hi = x.astype(BF16).astype(F32)
    return hi, x - hi


def cross(a, b):
    return (
        a[1] * b[2] - a[2] * b[1],
        a[2] * b[0] - a[0] * b[2],
        a[0] * b[1] - a[1] * b[0],
    )


def rows_of(message_ref, part, parts):
    return message_ref[pl.ds(part, NDEV, stride=parts), :]


def body_sums(field, arms, owner, row, onehot_ref, high_ref, low_ref):
    sent = list(field) + list(cross(arms, field))
    pieces = [split2(x) for x in sent]
    owner_ids = iota((NDEV, TILE), 0)
    row_ids = iota((ROWS, TILE), 0)
    for tile in range(TY):
        lanes = pl.ds(tile * TILE, TILE)
        pick = slice(tile, tile + 1)
        onehot_ref[:, lanes] = jnp.where(owner_ids == owner[pick], 1.0, 0.0).astype(BF16)
        mine = row_ids == row[pick]
        for part in range(6):
            place = slice(part * ROWS, (part + 1) * ROWS)
            high, low = pieces[part]
            high_ref[place, lanes] = jnp.where(mine, high[pick], 0.0).astype(BF16)
            low_ref[place, lanes] = jnp.where(mine, low[pick], 0.0).astype(BF16)
    contract = (((1,), (1,)), ((), ()))
    onehot = onehot_ref[...]
    return lax.dot_general(
        onehot, high_ref[...], contract, preferred_element_type=F32
    ) + lax.dot_general(onehot, low_ref[...], contract, preferred_element_type=F32)


def total(x):
    return jnp.sum(jnp.sum(x, axis=1, keepdims=True), axis=0, keepdims=True)


def forward_message(field, sums, dots, out_ref, parts):
    lane = iota((NDEV, TILE), 1)
    stacked = jnp.concatenate(
        [jnp.zeros((HALO_AT, TILE), F32)]
        + list(field)
        + [jnp.zeros((TILE - DOT_AT, TILE), F32)],
        axis=0,
    )
    second = jnp.concatenate([sums[:, TILE:], jnp.zeros((NDEV, 64), F32)], axis=1)
    second = second + stacked.T
    for at, dot in enumerate(dots):
        second = jnp.where(lane == DOT_AT + at, dot, second)
    out_ref[pl.ds(0, NDEV, stride=parts), :] = sums[:, :TILE]
    out_ref[pl.ds(1, NDEV, stride=parts), :] = second


def start_kernel(
    rhs_hbm, owner_hbm, row_hbm, arm_hbm, pos_hbm, inverse_hbm,
    out_ref, pack_ref, rhs_ref, inverse_ref,
    owner_ref, row_ref, sems, onehot, high, low,
):
    copies = [
        pltpu.make_async_copy(source, target, sems.at[at])
        for at, (source, target) in enumerate(
            (
                (rhs_hbm, rhs_ref),
                (owner_hbm, owner_ref),
                (row_hbm, row_ref),
                (arm_hbm, pack_ref.at[24:48, :]),
                (pos_hbm, pack_ref.at[0:24, :]),
                (inverse_hbm, inverse_ref),
            )
        )
    ]
    for copy in copies:
        copy.start()
    for copy in copies[:4]:
        copy.wait()
    field = [rhs_ref[8 * c : 8 * c + 8, :] for c in range(3)]
    arms = [pack_ref[24 + 8 * c : 32 + 8 * c, :] for c in range(3)]
    owner, row = owner_ref[...], row_ref[...]
    pack_ref[48:56, :] = (owner * ROWS + row).astype(F32)
    pack_ref[56:128, :] = jnp.zeros((72, TILE), F32)
    sums = body_sums(field, arms, owner, row, onehot, high, low)
    square = total(field[0] * field[0] + field[1] * field[1] + field[2] * field[2])
    forward_message(field, sums, [square], out_ref, FIRST)
    for copy in copies[4:]:
        copy.wait()
    out_ref[pl.ds(2, NDEV, stride=FIRST), :] = pack_ref[...].T


def turned(x, by):
    by = (by % 4) * NWIDE
    return x if by == 0 else jnp.concatenate([x[by:], x[:by]], axis=0)


def beside(x, by):
    groups = [x[z * NWIDE : (z + 1) * NWIDE] for z in range(4)]
    return jnp.concatenate([pltpu.roll(g, (-by) % NWIDE, 0) for g in groups], axis=0)


def routed(x, first, width):
    lane = iota((NDEV, TILE), 1)
    x = jnp.where((lane >= first) & (lane < first + width), x, 0.0)
    place = (lane - first) & 7
    edge = jnp.where(place == 7, beside(x, -1), jnp.where(place == 0, beside(x, 1), 0.0))
    return [turned(x, -1), turned(x, 1), turned(edge, -1), edge, turned(edge, 1)]


def shifted(x, by):
    by = by % TILE
    return x if by == 0 else pltpu.roll(x, by, 1)


def spread(row, lane):
    return jnp.broadcast_to(row[:, lane : lane + 1], (1, TILE))


def owner_kernel(step, inverse_ref, message_ref, *refs):
    states = refs[:step]
    out_ref, state_ref = refs[step:]
    parts = FIRST if step == 0 else 2
    first = rows_of(message_ref, 0, parts)
    second = rows_of(message_ref, 1, parts)
    sums = [jnp.sum(first, axis=0, keepdims=True), jnp.sum(second, axis=0, keepdims=True)]
    inners = [spread(sums[1], DOT_AT + 1 + i) for i in range(step)]
    square = spread(sums[1], DOT_AT)
    for inner in inners:
        square = square - inner * inner
    length = jnp.sqrt(square)
    scale = 1.0 / length
    for i in range(step):
        for half in range(2):
            sums[half] = sums[half] - inners[i] * states[i][half : half + 1, :]
    sums = [s * scale for s in sums]
    sub, lane = iota((8, TILE), 0), iota((8, TILE), 1)
    tiled = jnp.where(sub < 4, sums[0], sums[1])
    tiled = jnp.where((lane // ROWS == sub % 4) & (sub < 6), tiled, 0.0)
    tiled = tiled + pltpu.roll(tiled, 32, 1)
    tiled = tiled + pltpu.roll(tiled, 64, 1)
    zero = jnp.zeros((1, TILE), F32)
    by_row = [inverse_ref[a] for a in range(6)]
    by_row += [jnp.zeros((6, ROWS), F32)] * 2
    motion = []
    for half in range(2):
        inverse = jnp.concatenate(by_row[4 * half : 4 * half + 4], axis=1)
        motion.append(jnp.sum(inverse * tiled[0:6], axis=0, keepdims=True))
    state_ref[...] = jnp.concatenate(
        sums + motion + [length, scale] + inners + [zero] * (2 - step), axis=0
    )
    sent = [jnp.broadcast_to(m, (NDEV, TILE)) for m in motion]
    blocks = routed(second, HALO_AT, 24)
    rim = shifted(blocks[0], -HALO_AT)
    for k in range(1, 5):
        rim = rim + shifted(blocks[k], 24 * k - HALO_AT)
    sent.append(rim)
    if step == 0:
        blocks = routed(rows_of(message_ref, 2, parts), 0, FIXED)
        for k in range(3):
            sent[1] = sent[1] + shifted(blocks[2 + k], EDGES_AT + 2 * EDGE_STEP[k])
        sent.append(blocks[0] + shifted(blocks[1], 64))
    sent = sent + [jnp.zeros((NDEV, TILE), F32)] * (BACK[step] - len(sent))
    for part in range(BACK[step]):
        out_ref[pl.ds(part, NDEV, stride=BACK[step]), :] = sent[part]


def picked_motion(first, second, owner_ref, row_ref):
    table = jnp.concatenate([first.T, second.T[:64]], axis=0)
    high, low = split2(table)
    table = jnp.concatenate([high.astype(BF16), low.astype(BF16)], axis=1)
    owner_ids = iota((NDEV, TILE), 0)
    row_ids = iota((ROWS, TILE), 0)
    sub = iota((8, TILE), 0)
    results = []
    for block in range(BLOCKS):
        owner = owner_ref[8 * block : 8 * block + 8, :]
        row = row_ref[8 * block : 8 * block + 8, :]
        values = [jnp.zeros((8, TILE), F32) for _ in range(6)]
        for pair in ((0, 1), (2, 3), (4, 5), (6, 7)) if block < 3 else ((0, 7),):
            onehot = jnp.concatenate(
                [
                    jnp.where(owner_ids == owner[tile : tile + 1], 1.0, 0.0).astype(BF16)
                    for tile in pair
                ],
                axis=1,
            )
            onehot = jnp.concatenate([onehot, onehot], axis=0)
            found = jnp.dot(table, onehot, preferred_element_type=F32)
            for at, tile in enumerate(pair):
                mine = row_ids == row[tile : tile + 1]
                lanes = slice(at * TILE, (at + 1) * TILE)
                for part in range(6):
                    chosen = jnp.where(mine, found[part * ROWS : (part + 1) * ROWS, lanes], 0.0)
                    value = jnp.sum(chosen, axis=0, keepdims=True)
                    values[part] = jnp.where(sub == tile, value, values[part])
        results.append(values)
    return results


def source_rows(get, rows_ref):
    for i, dx in enumerate((-1, 0, 1)):
        for part in range(3):
            at = 30 * part + 10 * i
            edge = get(EDGE_OF[dx], part)
            rows_ref[at : at + 1, :] = edge[7:8]
            rows_ref[at + 1 : at + 9, :] = get(ROW_OF[dx], part)
            rows_ref[at + 9 : at + 10, :] = edge[0:1]


def sources_of(rows_ref, tile):
    return [
        [rows_ref[pl.ds(30 * part + 10 * i + tile + j, 8, stride=0), :] for part in range(3)]
        for i in range(3)
        for j in range(3)
    ]


def mobility(moved, rows_ref, pairs_ref, pair_at, across_ref):
    source_rows(lambda block, part: moved[block][part], rows_ref)

    def of_tile(tile, carry):
        sources = sources_of(rows_ref, tile)
        sums = [[], [], []]
        pair = pair_at(tile)
        for group in range(TILE // 8):
            terms = None
            for k in range(9):
                near, *sep = pair(group, k)
                force = sources[k]
                along = sep[0] * force[0] + sep[1] * force[1] + sep[2] * force[2]
                term = [near * force[a] + along * sep[a] for a in range(3)]
                terms = term if terms is None else [terms[a] + term[a] for a in range(3)]
            for a in range(3):
                sums[a].append(terms[a])
        for a in range(3):
            across = jnp.concatenate(sums[a], axis=0)
            if across_ref is None:
                pairs_ref[pl.ds(8 * a + tile, 1), :] = jnp.sum(across.T, axis=0, keepdims=True)
            else:
                across_ref[a, tile] = across
        return carry

    lax.fori_loop(0, TY, of_tile, 0, unroll=4 if across_ref is None else 4)
    if across_ref is not None:
        for a in range(3):
            for tile in range(TY):
                pairs_ref[8 * a + tile : 8 * a + tile + 1, :] = jnp.sum(
                    across_ref[a, tile].T, axis=0, keepdims=True
                )
    return [pairs_ref[8 * a : 8 * a + 8, :] for a in range(3)]


def stored_pairs(pair_ref):
    def pair_at(tile):
        return lambda group, k: [pair_ref[tile, group, k, part] for part in range(4)]

    return pair_at


def new_pairs(pair_ref, own_position, rows_ref):
    columns = jnp.concatenate([own_position, jnp.zeros((104, TILE), F32)], axis=0).T

    def pair_at(tile):
        turned_columns = pltpu.roll(columns, TILE - tile, 1)
        sources = sources_of(rows_ref, tile)
        targets = {}

        def pair(group, k):
            if group not in targets:
                rows = turned_columns[8 * group : 8 * group + 8]
                targets[group] = [
                    jnp.broadcast_to(rows[:, 8 * a : 8 * a + 1], (8, TILE)) for a in range(3)
                ]
            target = targets[group]
            shift = (float(k // 3 - 1), float(k % 3 - 1), 0.0)
            sep = [target[a] - (sources[k][a] + shift[a]) for a in range(3)]
            soft = sep[0] * sep[0] + sep[1] * sep[1] + (sep[2] * sep[2] + EPS2)
            root = lax.rsqrt(soft)
            square = root * root
            scale = square * lax.rsqrt(root)
            found = [root + EPS2 * (square * root)] + [sep[a] * scale for a in range(3)]
            for part in range(4):
                pair_ref[tile, group, k, part] = found[part]
            return found

        return pair

    return pair_at


def local_kernel(step, *refs):
    refs = list(refs)
    back = BACK[step]
    take = lambda n: [refs.pop(0) for _ in range(n)]
    message_ref, state_ref, field_ref = take(3)
    if step == 0:
        (pack_ref,) = take(1)
    else:
        pair_ref, arm_ref, owner_ref, row_ref = take(4)
    bases = take(step)
    if step == 0:
        pair_ref, arm_ref, owner_ref, row_ref = take(4)
    if step < ITERS - 1:
        basis_ref, fresh_ref = take(2)
    moved_ref, out_ref = take(2)
    rows_ref, pairs_ref, onehot, high, low = take(5)
    across_ref = take(1)[0] if step in DEFERRED else None
    if step == 0:
        (places_ref,) = take(1)
        rows = rows_of(message_ref, 3, back).T
        edges = rows_of(message_ref, 1, back).T
        fixed = [pack_ref[0:FIXED, :], rows[:FIXED], rows[64 : 64 + FIXED]]
        for k in range(3):
            at = EDGES_AT + 2 * EDGE_STEP[k]
            fixed.append(edges[at : at + FIXED])
        for block in range(BLOCKS):
            arm_ref[24 * block : 24 * block + 24, :] = fixed[block][24:48]
            code = fixed[block][48:56].astype(jnp.int32)
            owner_ref[8 * block : 8 * block + 8, :] = lax.shift_right_logical(code, 5)
            row_ref[8 * block : 8 * block + 8, :] = code & (ROWS - 1)
        source_rows(lambda block, part: fixed[block][8 * part : 8 * part + 8], places_ref)
        pair_at = new_pairs(pair_ref, fixed[0][0:24], places_ref)
    else:
        pair_at = stored_pairs(pair_ref)
    rim = rows_of(message_ref, 2, back).T
    basis = jnp.concatenate([field_ref[...], rim[:120]], axis=0)
    for i in range(step):
        basis = basis - state_ref[6 + i : 7 + i, :] * bases[i][...]
    basis = basis * state_ref[5:6, :]
    motions = picked_motion(
        rows_of(message_ref, 0, back), rows_of(message_ref, 1, back), owner_ref, row_ref
    )
    moved = []
    for block in range(BLOCKS):
        arm = [arm_ref[24 * block + 8 * a : 24 * block + 8 * a + 8, :] for a in range(3)]
        turn = cross(motions[block][3:], arm)
        moved.append(
            [
                basis[24 * block + 8 * a : 24 * block + 8 * a + 8]
                + (motions[block][a] + turn[a])
                for a in range(3)
            ]
        )
    pairs = mobility(moved, rows_ref, pairs_ref, pair_at, across_ref)
    fresh = [moved[0][a] + FACTOR * pairs[a] for a in range(3)]
    for a in range(3):
        moved_ref[8 * a : 8 * a + 8, :] = moved[0][a]

    def dot(get):
        return total(fresh[0] * get(0) + fresh[1] * get(1) + fresh[2] * get(2))

    dots = [dot(lambda a: fresh[a])]
    for i in range(step):
        dots.append(dot(lambda a: bases[i][8 * a : 8 * a + 8, :]))
    dots.append(dot(lambda a: basis[8 * a : 8 * a + 8]))
    if step < ITERS - 1:
        basis_ref[...] = basis
        for a in range(3):
            fresh_ref[8 * a : 8 * a + 8, :] = fresh[a]
        arms = [arm_ref[8 * a : 8 * a + 8, :] for a in range(3)]
        sums = body_sums(
            fresh, arms, owner_ref[0:8, :], row_ref[0:8, :], onehot, high, low
        )
        forward_message(fresh, sums, dots, out_ref, 2)
    else:
        lane = iota((NDEV, TILE), 1)
        message = jnp.zeros((NDEV, TILE), F32)
        for at, value in enumerate(dots):
            message = jnp.where(lane == at, value, message)
        out_ref[...] = message


def final_kernel(message_ref, *refs):
    states, moved = refs[:3], refs[3:6]
    forces_ref, motion_ref = refs[6:]
    sums = jnp.sum(message_ref[...], axis=0, keepdims=True)
    beta = states[0][4:5, :]
    a = [states[1][6:7, :], states[1][4:5, :]]
    b = [states[2][6:7, :], states[2][7:8, :], states[2][4:5, :]]
    c = [spread(sums, 1 + i) for i in range(3)]
    inner = lambda p, q: sum([x * y for x, y in zip(p, q)][1:], p[0] * q[0])
    n00, n01, n02 = inner(a, a), inner(a, b), inner(a, c)
    n11, n12 = inner(b, b), inner(b, c)
    n22 = spread(sums, 0)
    i00 = lax.rsqrt(n00)
    l10, l20 = n01 * i00, n02 * i00
    i11 = lax.rsqrt(n11 - l10 * l10)
    l21 = (n12 - l20 * l10) * i11
    i22 = lax.rsqrt(n22 - l20 * l20 - l21 * l21)
    t0 = beta * a[0] * i00
    t1 = (beta * b[0] - l10 * t0) * i11
    t2 = (beta * c[0] - l20 * t0 - l21 * t1) * i22
    y2 = t2 * i22
    y1 = (t1 - l21 * y2) * i11
    y0 = (t0 - l10 * y1 - l20 * y2) * i00
    forces_ref[...] = y0 * moved[0][...] + y1 * moved[1][...] + y2 * moved[2][...]
    for part in range(6):
        half, at = part // 4, (part % 4) * ROWS
        row = slice(2 + half, 3 + half)
        whole = y0 * states[0][row, :] + y1 * states[1][row, :] + y2 * states[2][row, :]
        motion_ref[part : part + 1, :] = whole[:, at : at + ROWS]


HBM = pl.BlockSpec(memory_space=pltpu.HBM)
VMEM = pl.BlockSpec(memory_space=pltpu.VMEM)


def f32(*shape):
    return jax.ShapeDtypeStruct(shape, F32)


def i32(*shape):
    return jax.ShapeDtypeStruct(shape, jnp.int32)


DEFERRED = (0,)
PAIRS = (TY, TILE // 8, 9, 4, 8, TILE)


def sums_scratch():
    return [
        pltpu.VMEM((NDEV, TY * TILE), BF16),
        pltpu.VMEM((6 * ROWS, TY * TILE), BF16),
        pltpu.VMEM((6 * ROWS, TY * TILE), BF16),
    ]


def call(body, out, scratch=(), mib=16, **options):
    return pl.pallas_call(
        body,
        out_shape=out,
        scratch_shapes=list(scratch),
        compiler_params=pltpu.CompilerParams(vmem_limit_bytes=mib * 1024 * 1024),
        **options,
    )


def exchange(message):
    rows = message.shape[0]
    if rows != 3 * NDEV:
        return lax.all_to_all(message, CELL_WIDE, split_axis=0, concat_axis=0, tiled=True)
    moved = message.reshape(NDEV, 1, rows * TILE // NDEV)
    moved = lax.all_to_all(moved, CELL_WIDE, split_axis=0, concat_axis=0, tiled=True)
    return moved.reshape(rows, TILE)


def local(positions, rhs, blob_owner, blob_row, blob_arm, body_inverse):
    pos = positions.reshape(24, TILE)
    field = rhs.reshape(24, TILE)
    arm = blob_arm.reshape(24, TILE)
    owner = blob_owner.reshape(TY, TILE)
    row = blob_row.reshape(TY, TILE)
    held = (field, owner, row, arm, pos, body_inverse)
    message, pack, field, inverse = call(
        start_kernel,
        (f32(FIRST * NDEV, TILE), f32(TILE, TILE), f32(24, TILE), f32(6, 6, ROWS)),
        [
            pltpu.VMEM((TY, TILE), jnp.int32),
            pltpu.VMEM((TY, TILE), jnp.int32),
            pltpu.SemaphoreType.DMA((6,)),
        ]
        + sums_scratch(),
        in_specs=[HBM] * 6,
    )(*[pltpu.with_memory_space_constraint(x, pltpu.HBM) for x in held])
    states, bases, moveds = [], [], []
    for step in range(ITERS):
        arrived = exchange(message)
        message, state = call(
            lambda *refs, step=step: owner_kernel(step, *refs),
            (f32(BACK[step] * NDEV, TILE), f32(8, TILE)),
        )(inverse, arrived, *states)
        arrived = exchange(message)
        last = step == ITERS - 1
        outs = [f32(24, TILE), f32(NDEV if last else 2 * NDEV, TILE)]
        if not last:
            outs = [f32(24 * BLOCKS, TILE), f32(24, TILE)] + outs
        scratch = [pltpu.VMEM((96, TILE), F32), pltpu.VMEM((24, TILE), F32)] + sums_scratch()
        if step in DEFERRED:
            scratch.append(pltpu.VMEM((3, TY, TILE, TILE), F32))
        if step == 0:
            outs = [
                pltpu.VMEM(PAIRS, F32),
                f32(24 * BLOCKS, TILE),
                i32(8 * BLOCKS, TILE),
                i32(8 * BLOCKS, TILE),
            ] + outs
            scratch.append(pltpu.VMEM((96, TILE), F32))
        results = call(
            lambda *refs, step=step: local_kernel(step, *refs), tuple(outs), scratch
        )(arrived, state, field, *(fixed if step else (pack,)), *bases)
        if step == 0:
            pairs = pltpu.with_memory_space_constraint(results[0], pltpu.VMEM)
            fixed = (pairs, *results[1:4])
        moved, message = results[-2:]
        states.append(state)
        moveds.append(moved)
        if not last:
            bases.append(results[-4])
            field = results[-3]
    arrived = exchange(message)
    forces, motion = call(final_kernel, (f32(24, TILE), f32(6, ROWS)))(arrived, *states, *moveds)
    return (forces.reshape(rhs.shape), motion)


def solution(mesh):
    split = Mesh(
        mesh.devices.reshape(mesh.shape["cell"], 4, 4, 2), ("cell", "wide_0", "wide_1", "wide_2")
    )
    in_specs = (
        P(None, "cell", WIDE, None),
        P(None, "cell", WIDE, None),
        P("cell", WIDE, None, None),
        P("cell", WIDE, None),
        P(None, "cell", WIDE, None),
        P(None, None, CELL_WIDE),
    )
    out_specs = (P(None, "cell", WIDE, None), P(None, CELL_WIDE))
    return jax.shard_map(local, mesh=split, in_specs=in_specs, out_specs=out_specs, check_vma=False)
```

```python
import math

import jax
import jax.numpy as jnp
from jax import lax
from jax.experimental import pallas as pl
from jax.experimental.pallas import tpu as pltpu
from jax.sharding import Mesh
from jax.sharding import PartitionSpec as P

ITERS = 3
WIDE = ("wide_0", "wide_1", "wide_2")
CELL_WIDE = ("cell", "wide_0", "wide_1", "wide_2")
EPS2 = 0.04
KAPPA = 0.3
FACTOR = KAPPA / math.sqrt(9 * 128)
F32 = jnp.float32
BF16 = jnp.bfloat16

TY = 8
TILE = 128
NDEV = 128
NWIDE = 32
ROWS = 32
HALO_AT = 64
DOT_AT = 88
FIRST = 3
BACK = (4, 4, 3)
FIXED = 56
BLOCKS = 6
EDGE_OF = {-1: 3, 0: 4, 1: 5}
ROW_OF = {-1: 1, 0: 0, 1: 2}
EDGES_AT = 64
EDGE_STEP = (1, 0, 2)


def iota(shape, axis):
    return lax.broadcasted_iota(jnp.int32, shape, axis)


def split2(x):
    hi = x.astype(BF16).astype(F32)
    return hi, x - hi


def cross(a, b):
    return (
        a[1] * b[2] - a[2] * b[1],
        a[2] * b[0] - a[0] * b[2],
        a[0] * b[1] - a[1] * b[0],
    )


def rows_of(message_ref, part, parts):
    return message_ref[pl.ds(part, NDEV, stride=parts), :]


def body_sums(field, arms, owner, row, onehot_ref, high_ref, low_ref):
    sent = list(field) + list(cross(arms, field))
    pieces = [split2(x) for x in sent]
    owner_ids = iota((NDEV, TILE), 0)
    row_ids = iota((ROWS, TILE), 0)
    for tile in range(TY):
        lanes = pl.ds(tile * TILE, TILE)
        pick = slice(tile, tile + 1)
        onehot_ref[:, lanes] = jnp.where(owner_ids == owner[pick], 1.0, 0.0).astype(BF16)
        mine = row_ids == row[pick]
        for part in range(6):
            place = slice(part * ROWS, (part + 1) * ROWS)
            high, low = pieces[part]
            high_ref[place, lanes] = jnp.where(mine, high[pick], 0.0).astype(BF16)
            low_ref[place, lanes] = jnp.where(mine, low[pick], 0.0).astype(BF16)
    contract = (((1,), (1,)), ((), ()))
    onehot = onehot_ref[...]
    return lax.dot_general(
        onehot, high_ref[...], contract, preferred_element_type=F32
    ) + lax.dot_general(onehot, low_ref[...], contract, preferred_element_type=F32)


def total(x):
    return jnp.sum(jnp.sum(x, axis=1, keepdims=True), axis=0, keepdims=True)


def forward_message(field, sums, dots, out_ref, parts):
    lane = iota((NDEV, TILE), 1)
    stacked = jnp.concatenate(
        [jnp.zeros((HALO_AT, TILE), F32)]
        + list(field)
        + [jnp.zeros((TILE - DOT_AT, TILE), F32)],
        axis=0,
    )
    second = jnp.concatenate([sums[:, TILE:], jnp.zeros((NDEV, 64), F32)], axis=1)
    second = second + stacked.T
    for at, dot in enumerate(dots):
        second = jnp.where(lane == DOT_AT + at, dot, second)
    out_ref[pl.ds(0, NDEV, stride=parts), :] = sums[:, :TILE]
    out_ref[pl.ds(1, NDEV, stride=parts), :] = second


def start_kernel(
    rhs_hbm, owner_hbm, row_hbm, arm_hbm, pos_hbm, inverse_hbm,
    out_ref, pack_ref, rhs_ref, inverse_ref,
    owner_ref, row_ref, sems, onehot, high, low,
):
    copies = [
        pltpu.make_async_copy(source, target, sems.at[at])
        for at, (source, target) in enumerate(
            (
                (rhs_hbm, rhs_ref),
                (owner_hbm, owner_ref),
                (row_hbm, row_ref),
                (arm_hbm, pack_ref.at[24:48, :]),
                (pos_hbm, pack_ref.at[0:24, :]),
                (inverse_hbm, inverse_ref),
            )
        )
    ]
    for copy in copies:
        copy.start()
    for copy in copies[:4]:
        copy.wait()
    field = [rhs_ref[8 * c : 8 * c + 8, :] for c in range(3)]
    arms = [pack_ref[24 + 8 * c : 32 + 8 * c, :] for c in range(3)]
    owner, row = owner_ref[...], row_ref[...]
    pack_ref[48:56, :] = (owner * ROWS + row).astype(F32)
    pack_ref[56:128, :] = jnp.zeros((72, TILE), F32)
    sums = body_sums(field, arms, owner, row, onehot, high, low)
    square = total(field[0] * field[0] + field[1] * field[1] + field[2] * field[2])
    forward_message(field, sums, [square], out_ref, FIRST)
    for copy in copies[4:]:
        copy.wait()
    out_ref[pl.ds(2, NDEV, stride=FIRST), :] = pack_ref[...].T


def turned(x, by):
    by = (by % 4) * NWIDE
    return x if by == 0 else jnp.concatenate([x[by:], x[:by]], axis=0)


def beside(x, by):
    groups = [x[z * NWIDE : (z + 1) * NWIDE] for z in range(4)]
    return jnp.concatenate([pltpu.roll(g, (-by) % NWIDE, 0) for g in groups], axis=0)


def routed(x, first, width):
    lane = iota((NDEV, TILE), 1)
    x = jnp.where((lane >= first) & (lane < first + width), x, 0.0)
    place = (lane - first) & 7
    edge = jnp.where(place == 7, beside(x, -1), jnp.where(place == 0, beside(x, 1), 0.0))
    return [turned(x, -1), turned(x, 1), turned(edge, -1), edge, turned(edge, 1)]


def shifted(x, by):
    by = by % TILE
    return x if by == 0 else pltpu.roll(x, by, 1)


def spread(row, lane):
    return jnp.broadcast_to(row[:, lane : lane + 1], (1, TILE))


def owner_kernel(step, inverse_ref, message_ref, *refs):
    states = refs[:step]
    out_ref, state_ref = refs[step:]
    parts = FIRST if step == 0 else 2
    first = rows_of(message_ref, 0, parts)
    second = rows_of(message_ref, 1, parts)
    sums = [jnp.sum(first, axis=0, keepdims=True), jnp.sum(second, axis=0, keepdims=True)]
    inners = [spread(sums[1], DOT_AT + 1 + i) for i in range(step)]
    square = spread(sums[1], DOT_AT)
    for inner in inners:
        square = square - inner * inner
    length = jnp.sqrt(square)
    scale = 1.0 / length
    for i in range(step):
        for half in range(2):
            sums[half] = sums[half] - inners[i] * states[i][half : half + 1, :]
    sums = [s * scale for s in sums]
    sub, lane = iota((8, TILE), 0), iota((8, TILE), 1)
    tiled = jnp.where(sub < 4, sums[0], sums[1])
    tiled = jnp.where((lane // ROWS == sub % 4) & (sub < 6), tiled, 0.0)
    tiled = tiled + pltpu.roll(tiled, 32, 1)
    tiled = tiled + pltpu.roll(tiled, 64, 1)
    zero = jnp.zeros((1, TILE), F32)
    by_row = [inverse_ref[a] for a in range(6)]
    by_row += [jnp.zeros((6, ROWS), F32)] * 2
    motion = []
    for half in range(2):
        inverse = jnp.concatenate(by_row[4 * half : 4 * half + 4], axis=1)
        motion.append(jnp.sum(inverse * tiled[0:6], axis=0, keepdims=True))
    state_ref[...] = jnp.concatenate(
        sums + motion + [length, scale] + inners + [zero] * (2 - step), axis=0
    )
    sent = [jnp.broadcast_to(m, (NDEV, TILE)) for m in motion]
    blocks = routed(second, HALO_AT, 24)
    rim = shifted(blocks[0], -HALO_AT)
    for k in range(1, 5):
        rim = rim + shifted(blocks[k], 24 * k - HALO_AT)
    sent.append(rim)
    if step == 0:
        blocks = routed(rows_of(message_ref, 2, parts), 0, FIXED)
        for k in range(3):
            sent[1] = sent[1] + shifted(blocks[2 + k], EDGES_AT + 2 * EDGE_STEP[k])
        sent.append(blocks[0] + shifted(blocks[1], 64))
    sent = sent + [jnp.zeros((NDEV, TILE), F32)] * (BACK[step] - len(sent))
    for part in range(BACK[step]):
        out_ref[pl.ds(part, NDEV, stride=BACK[step]), :] = sent[part]


def picked_motion(first, second, owner_ref, row_ref):
    table = jnp.concatenate([first.T, second.T[:64]], axis=0)
    high, low = split2(table)
    table = jnp.concatenate([high.astype(BF16), low.astype(BF16)], axis=1)
    owner_ids = iota((NDEV, TILE), 0)
    row_ids = iota((ROWS, TILE), 0)
    sub = iota((8, TILE), 0)
    results = []
    for block in range(BLOCKS):
        owner = owner_ref[8 * block : 8 * block + 8, :]
        row = row_ref[8 * block : 8 * block + 8, :]
        values = [jnp.zeros((8, TILE), F32) for _ in range(6)]
        for pair in ((0, 1), (2, 3), (4, 5), (6, 7)) if block < 3 else ((0, 7),):
            onehot = jnp.concatenate(
                [
                    jnp.where(owner_ids == owner[tile : tile + 1], 1.0, 0.0).astype(BF16)
                    for tile in pair
                ],
                axis=1,
            )
            onehot = jnp.concatenate([onehot, onehot], axis=0)
            found = jnp.dot(table, onehot, preferred_element_type=F32)
            for at, tile in enumerate(pair):
                mine = row_ids == row[tile : tile + 1]
                lanes = slice(at * TILE, (at + 1) * TILE)
                for part in range(6):
                    chosen = jnp.where(mine, found[part * ROWS : (part + 1) * ROWS, lanes], 0.0)
                    value = jnp.sum(chosen, axis=0, keepdims=True)
                    values[part] = jnp.where(sub == tile, value, values[part])
        results.append(values)
    return results


def source_rows(get, rows_ref):
    for i, dx in enumerate((-1, 0, 1)):
        for part in range(3):
            at = 30 * part + 10 * i
            edge = get(EDGE_OF[dx], part)
            rows_ref[at : at + 1, :] = edge[7:8]
            rows_ref[at + 1 : at + 9, :] = get(ROW_OF[dx], part)
            rows_ref[at + 9 : at + 10, :] = edge[0:1]


def sources_of(rows_ref, tile):
    return [
        [rows_ref[pl.ds(30 * part + 10 * i + tile + j, 8, stride=0), :] for part in range(3)]
        for i in range(3)
        for j in range(3)
    ]


def field_blocks(rows_ref, block_ref):
    block_ref[...] = jnp.zeros_like(block_ref)
    for part in range(3):
        high, low = split2(rows_ref[30 * part : 30 * part + 30, :])
        for tile in range(30):
            block_ref[tile, part : part + 1, :] = high[tile : tile + 1]
            block_ref[tile, 3 + part : 4 + part, :] = low[tile : tile + 1]


def mobility(moved, rows_ref, block_ref, near_ref, pairs_ref, pair_at):
    source_rows(lambda block, part: moved[block][part], rows_ref)
    field_blocks(rows_ref, block_ref)
    contract = (((1,), (1,)), ((), ()))

    def of_tile(tile, carry):
        sources = sources_of(rows_ref, tile)
        sums = [[], [], []]
        pair = pair_at(tile)
        for group in range(TILE // 8):
            terms = None
            for k in range(9):
                sep = pair(group, k)
                force = sources[k]
                along = sep[0] * force[0] + sep[1] * force[1] + sep[2] * force[2]
                term = [along * sep[a] for a in range(3)]
                terms = term if terms is None else [terms[a] + term[a] for a in range(3)]
            for a in range(3):
                sums[a].append(terms[a])
        blocks = [block_ref[10 * (k // 3) + k % 3 + tile].astype(BF16) for k in range(9)]
        blocks = jnp.concatenate(blocks, axis=1)
        near = [
            lax.dot_general(blocks, near_ref[i, tile], contract, preferred_element_type=F32)
            for i in range(2)
        ]
        near = near[0][0:3] + near[0][3:6] + near[1][0:3]
        for a in range(3):
            across = jnp.concatenate(sums[a], axis=0).T
            pairs_ref[pl.ds(8 * a + tile, 1), :] = (
                jnp.sum(across, axis=0, keepdims=True) + near[a : a + 1]
            )
        return carry

    lax.fori_loop(0, TY, of_tile, 0, unroll=4)
    return [pairs_ref[8 * a : 8 * a + 8, :] for a in range(3)]


def stored_pairs(pair_ref):
    def pair_at(tile):
        return lambda group, k: [pair_ref[tile, group, k, part] for part in range(3)]

    return pair_at


def new_pairs(pair_ref, near_ref, own_position, rows_ref):
    columns = jnp.concatenate([own_position, jnp.zeros((104, TILE), F32)], axis=0).T

    def pair_at(tile):
        turned_columns = pltpu.roll(columns, TILE - tile, 1)
        sources = sources_of(rows_ref, tile)
        targets = {}
        nears = {}

        def pair(group, k):
            if group not in targets:
                rows = turned_columns[8 * group : 8 * group + 8]
                targets[group] = [
                    jnp.broadcast_to(rows[:, 8 * a : 8 * a + 1], (8, TILE)) for a in range(3)
                ]
            target = targets[group]
            shift = (float(k // 3 - 1), float(k % 3 - 1), 0.0)
            sep = [target[a] - (sources[k][a] + shift[a]) for a in range(3)]
            soft = sep[0] * sep[0] + sep[1] * sep[1] + (sep[2] * sep[2] + EPS2)
            root = lax.rsqrt(soft)
            square = root * root
            scale = square * lax.rsqrt(root)
            nears[group, k] = root + EPS2 * (square * root)
            if group % 2 == 1:
                both = jnp.concatenate([nears[group - 1, k], nears[group, k]], axis=0)
                high, low = split2(both)
                place = slice(8 * group - 8, 8 * group + 8)
                lanes = slice(k * TILE, (k + 1) * TILE)
                near_ref[0, tile, place, lanes] = high.astype(BF16)
                near_ref[1, tile, place, lanes] = low.astype(BF16)
            found = [sep[a] * scale for a in range(3)]
            for part in range(3):
                pair_ref[tile, group, k, part] = found[part]
            return found

        return pair

    return pair_at


def local_kernel(step, *refs):
    refs = list(refs)
    back = BACK[step]
    take = lambda n: [refs.pop(0) for _ in range(n)]
    message_ref, state_ref, field_ref = take(3)
    if step == 0:
        (pack_ref,) = take(1)
    else:
        pair_ref, near_ref, arm_ref, owner_ref, row_ref = take(5)
    bases = take(step)
    if step == 0:
        pair_ref, near_ref, arm_ref, owner_ref, row_ref = take(5)
    if step < ITERS - 1:
        basis_ref, fresh_ref = take(2)
    moved_ref, out_ref = take(2)
    rows_ref, block_ref, pairs_ref, onehot, high, low = take(6)
    if step == 0:
        (places_ref,) = take(1)
        rows = rows_of(message_ref, 3, back).T
        edges = rows_of(message_ref, 1, back).T
        fixed = [pack_ref[0:FIXED, :], rows[:FIXED], rows[64 : 64 + FIXED]]
        for k in range(3):
            at = EDGES_AT + 2 * EDGE_STEP[k]
            fixed.append(edges[at : at + FIXED])
        for block in range(BLOCKS):
            arm_ref[24 * block : 24 * block + 24, :] = fixed[block][24:48]
            code = fixed[block][48:56].astype(jnp.int32)
            owner_ref[8 * block : 8 * block + 8, :] = lax.shift_right_logical(code, 5)
            row_ref[8 * block : 8 * block + 8, :] = code & (ROWS - 1)
        source_rows(lambda block, part: fixed[block][8 * part : 8 * part + 8], places_ref)
        pair_at = new_pairs(pair_ref, near_ref, fixed[0][0:24], places_ref)
    else:
        pair_at = stored_pairs(pair_ref)
    rim = rows_of(message_ref, 2, back).T
    basis = jnp.concatenate([field_ref[...], rim[:120]], axis=0)
    for i in range(step):
        basis = basis - state_ref[6 + i : 7 + i, :] * bases[i][...]
    basis = basis * state_ref[5:6, :]
    motions = picked_motion(
        rows_of(message_ref, 0, back), rows_of(message_ref, 1, back), owner_ref, row_ref
    )
    moved = []
    for block in range(BLOCKS):
        arm = [arm_ref[24 * block + 8 * a : 24 * block + 8 * a + 8, :] for a in range(3)]
        turn = cross(motions[block][3:], arm)
        moved.append(
            [
                basis[24 * block + 8 * a : 24 * block + 8 * a + 8]
                + (motions[block][a] + turn[a])
                for a in range(3)
            ]
        )
    pairs = mobility(moved, rows_ref, block_ref, near_ref, pairs_ref, pair_at)
    fresh = [moved[0][a] + FACTOR * pairs[a] for a in range(3)]
    for a in range(3):
        moved_ref[8 * a : 8 * a + 8, :] = moved[0][a]

    def dot(get):
        return total(fresh[0] * get(0) + fresh[1] * get(1) + fresh[2] * get(2))

    dots = [dot(lambda a: fresh[a])]
    for i in range(step):
        dots.append(dot(lambda a: bases[i][8 * a : 8 * a + 8, :]))
    dots.append(dot(lambda a: basis[8 * a : 8 * a + 8]))
    if step < ITERS - 1:
        basis_ref[...] = basis
        for a in range(3):
            fresh_ref[8 * a : 8 * a + 8, :] = fresh[a]
        arms = [arm_ref[8 * a : 8 * a + 8, :] for a in range(3)]
        sums = body_sums(
            fresh, arms, owner_ref[0:8, :], row_ref[0:8, :], onehot, high, low
        )
        forward_message(fresh, sums, dots, out_ref, 2)
    else:
        lane = iota((NDEV, TILE), 1)
        message = jnp.zeros((NDEV, TILE), F32)
        for at, value in enumerate(dots):
            message = jnp.where(lane == at, value, message)
        out_ref[...] = message


def final_kernel(message_ref, *refs):
    states, moved = refs[:3], refs[3:6]
    forces_ref, motion_ref = refs[6:]
    sums = jnp.sum(message_ref[...], axis=0, keepdims=True)
    beta = states[0][4:5, :]
    a = [states[1][6:7, :], states[1][4:5, :]]
    b = [states[2][6:7, :], states[2][7:8, :], states[2][4:5, :]]
    c = [spread(sums, 1 + i) for i in range(3)]
    inner = lambda p, q: sum([x * y for x, y in zip(p, q)][1:], p[0] * q[0])
    n00, n01, n02 = inner(a, a), inner(a, b), inner(a, c)
    n11, n12 = inner(b, b), inner(b, c)
    n22 = spread(sums, 0)
    i00 = lax.rsqrt(n00)
    l10, l20 = n01 * i00, n02 * i00
    i11 = lax.rsqrt(n11 - l10 * l10)
    l21 = (n12 - l20 * l10) * i11
    i22 = lax.rsqrt(n22 - l20 * l20 - l21 * l21)
    t0 = beta * a[0] * i00
    t1 = (beta * b[0] - l10 * t0) * i11
    t2 = (beta * c[0] - l20 * t0 - l21 * t1) * i22
    y2 = t2 * i22
    y1 = (t1 - l21 * y2) * i11
    y0 = (t0 - l10 * y1 - l20 * y2) * i00
    forces_ref[...] = y0 * moved[0][...] + y1 * moved[1][...] + y2 * moved[2][...]
    for part in range(6):
        half, at = part // 4, (part % 4) * ROWS
        row = slice(2 + half, 3 + half)
        whole = y0 * states[0][row, :] + y1 * states[1][row, :] + y2 * states[2][row, :]
        motion_ref[part : part + 1, :] = whole[:, at : at + ROWS]


HBM = pl.BlockSpec(memory_space=pltpu.HBM)
VMEM = pl.BlockSpec(memory_space=pltpu.VMEM)


def f32(*shape):
    return jax.ShapeDtypeStruct(shape, F32)


def i32(*shape):
    return jax.ShapeDtypeStruct(shape, jnp.int32)


PAIRS = (TY, TILE // 8, 9, 3, 8, TILE)
NEAR = (2, TY, TILE, 9 * TILE)


def sums_scratch():
    return [
        pltpu.VMEM((NDEV, TY * TILE), BF16),
        pltpu.VMEM((6 * ROWS, TY * TILE), BF16),
        pltpu.VMEM((6 * ROWS, TY * TILE), BF16),
    ]


def call(body, out, scratch=(), mib=16, **options):
    return pl.pallas_call(
        body,
        out_shape=out,
        scratch_shapes=list(scratch),
        compiler_params=pltpu.CompilerParams(vmem_limit_bytes=mib * 1024 * 1024),
        **options,
    )


def exchange(message):
    rows = message.shape[0]
    if rows != 3 * NDEV:
        return lax.all_to_all(message, CELL_WIDE, split_axis=0, concat_axis=0, tiled=True)
    moved = message.reshape(NDEV, 1, rows * TILE // NDEV)
    moved = lax.all_to_all(moved, CELL_WIDE, split_axis=0, concat_axis=0, tiled=True)
    return moved.reshape(rows, TILE)


def local(positions, rhs, blob_owner, blob_row, blob_arm, body_inverse):
    pos = positions.reshape(24, TILE)
    field = rhs.reshape(24, TILE)
    arm = blob_arm.reshape(24, TILE)
    owner = blob_owner.reshape(TY, TILE)
    row = blob_row.reshape(TY, TILE)
    held = (field, owner, row, arm, pos, body_inverse)
    message, pack, field, inverse = call(
        start_kernel,
        (f32(FIRST * NDEV, TILE), f32(TILE, TILE), f32(24, TILE), f32(6, 6, ROWS)),
        [
            pltpu.VMEM((TY, TILE), jnp.int32),
            pltpu.VMEM((TY, TILE), jnp.int32),
            pltpu.SemaphoreType.DMA((6,)),
        ]
        + sums_scratch(),
        in_specs=[HBM] * 6,
    )(*[pltpu.with_memory_space_constraint(x, pltpu.HBM) for x in held])
    states, bases, moveds = [], [], []
    for step in range(ITERS):
        arrived = exchange(message)
        message, state = call(
            lambda *refs, step=step: owner_kernel(step, *refs),
            (f32(BACK[step] * NDEV, TILE), f32(8, TILE)),
        )(inverse, arrived, *states)
        arrived = exchange(message)
        last = step == ITERS - 1
        outs = [f32(24, TILE), f32(NDEV if last else 2 * NDEV, TILE)]
        if not last:
            outs = [f32(24 * BLOCKS, TILE), f32(24, TILE)] + outs
        scratch = [
            pltpu.VMEM((96, TILE), F32),
            pltpu.VMEM((30, 16, TILE), F32),
            pltpu.VMEM((24, TILE), F32),
        ] + sums_scratch()
        if step == 0:
            outs = [
                pltpu.VMEM(PAIRS, F32),
                pltpu.VMEM(NEAR, BF16),
                f32(24 * BLOCKS, TILE),
                i32(8 * BLOCKS, TILE),
                i32(8 * BLOCKS, TILE),
            ] + outs
            scratch.append(pltpu.VMEM((96, TILE), F32))
        results = call(
            lambda *refs, step=step: local_kernel(step, *refs), tuple(outs), scratch
        )(arrived, state, field, *(fixed if step else (pack,)), *bases)
        if step == 0:
            held = [pltpu.with_memory_space_constraint(x, pltpu.VMEM) for x in results[:2]]
            fixed = (*held, *results[2:5])
        moved, message = results[-2:]
        states.append(state)
        moveds.append(moved)
        if not last:
            bases.append(results[-4])
            field = results[-3]
    arrived = exchange(message)
    forces, motion = call(final_kernel, (f32(24, TILE), f32(6, ROWS)))(arrived, *states, *moveds)
    return (forces.reshape(rhs.shape), motion)


def solution(mesh):
    split = Mesh(
        mesh.devices.reshape(mesh.shape["cell"], 4, 4, 2), ("cell", "wide_0", "wide_1", "wide_2")
    )
    in_specs = (
        P(None, "cell", WIDE, None),
        P(None, "cell", WIDE, None),
        P("cell", WIDE, None, None),
        P("cell", WIDE, None),
        P(None, "cell", WIDE, None),
        P(None, None, CELL_WIDE),
    )
    out_specs = (P(None, "cell", WIDE, None), P(None, CELL_WIDE))
    return jax.shard_map(local, mesh=split, in_specs=in_specs, out_specs=out_specs, check_vma=False)
```

```python
import math

import jax
import jax.numpy as jnp
from jax import lax
from jax.experimental import pallas as pl
from jax.experimental.pallas import tpu as pltpu
from jax.sharding import Mesh
from jax.sharding import PartitionSpec as P

ITERS = 3
WIDE = ("wide_0", "wide_1", "wide_2")
CELL_WIDE = ("cell", "wide_0", "wide_1", "wide_2")
EPS2 = 0.04
KAPPA = 0.3
FACTOR = KAPPA / math.sqrt(9 * 128)
F32 = jnp.float32
BF16 = jnp.bfloat16

TY = 8
TILE = 128
NDEV = 128
NWIDE = 32
ROWS = 32
HALO_AT = 64
DOT_AT = 88
FIRST = 3
BACK = (4, 4, 3)
FIXED = 56
BLOCKS = 6
EDGE_OF = {-1: 3, 0: 4, 1: 5}
ROW_OF = {-1: 1, 0: 0, 1: 2}
EDGES_AT = 64
EDGE_STEP = (1, 0, 2)


def iota(shape, axis):
    return lax.broadcasted_iota(jnp.int32, shape, axis)


def split2(x):
    hi = x.astype(BF16).astype(F32)
    return hi, x - hi


def cross(a, b):
    return (
        a[1] * b[2] - a[2] * b[1],
        a[2] * b[0] - a[0] * b[2],
        a[0] * b[1] - a[1] * b[0],
    )


def rows_of(message_ref, part, parts):
    return message_ref[pl.ds(part, NDEV, stride=parts), :]


def body_sums(field, arms, owner, row, onehot_ref, high_ref, low_ref):
    sent = list(field) + list(cross(arms, field))
    pieces = [split2(x) for x in sent]
    owner_ids = iota((NDEV, TILE), 0)
    row_ids = iota((ROWS, TILE), 0)
    for tile in range(TY):
        lanes = pl.ds(tile * TILE, TILE)
        pick = slice(tile, tile + 1)
        onehot_ref[:, lanes] = jnp.where(owner_ids == owner[pick], 1.0, 0.0).astype(BF16)
        mine = row_ids == row[pick]
        for part in range(6):
            place = slice(part * ROWS, (part + 1) * ROWS)
            high, low = pieces[part]
            high_ref[place, lanes] = jnp.where(mine, high[pick], 0.0).astype(BF16)
            low_ref[place, lanes] = jnp.where(mine, low[pick], 0.0).astype(BF16)
    contract = (((1,), (1,)), ((), ()))
    onehot = jnp.concatenate([onehot_ref[...]] * 2, axis=1)
    values = jnp.concatenate([high_ref[...], low_ref[...]], axis=1)
    return lax.dot_general(onehot, values, contract, preferred_element_type=F32)


def total(x):
    return jnp.sum(jnp.sum(x, axis=1, keepdims=True), axis=0, keepdims=True)


def forward_message(field, sums, dots, out_ref, parts):
    lane = iota((NDEV, TILE), 1)
    stacked = jnp.concatenate(
        [jnp.zeros((HALO_AT, TILE), F32)]
        + list(field)
        + [jnp.zeros((TILE - DOT_AT, TILE), F32)],
        axis=0,
    )
    second = jnp.concatenate([sums[:, TILE:], jnp.zeros((NDEV, 64), F32)], axis=1)
    second = second + stacked.T
    for at, dot in enumerate(dots):
        second = jnp.where(lane == DOT_AT + at, dot, second)
    out_ref[pl.ds(0, NDEV, stride=parts), :] = sums[:, :TILE]
    out_ref[pl.ds(1, NDEV, stride=parts), :] = second


def start_kernel(
    rhs_hbm, owner_hbm, row_hbm, arm_hbm, pos_hbm, inverse_hbm,
    out_ref, pack_ref, rhs_ref, inverse_ref,
    owner_ref, row_ref, sems, onehot, high, low,
):
    copies = [
        pltpu.make_async_copy(source, target, sems.at[at])
        for at, (source, target) in enumerate(
            (
                (rhs_hbm, rhs_ref),
                (owner_hbm, owner_ref),
                (row_hbm, row_ref),
                (arm_hbm, pack_ref.at[24:48, :]),
                (pos_hbm, pack_ref.at[0:24, :]),
                (inverse_hbm, inverse_ref),
            )
        )
    ]
    for copy in copies:
        copy.start()
    for copy in copies[:4]:
        copy.wait()
    field = [rhs_ref[8 * c : 8 * c + 8, :] for c in range(3)]
    arms = [pack_ref[24 + 8 * c : 32 + 8 * c, :] for c in range(3)]
    owner, row = owner_ref[...], row_ref[...]
    pack_ref[48:56, :] = (owner * ROWS + row).astype(F32)
    pack_ref[56:128, :] = jnp.zeros((72, TILE), F32)
    sums = body_sums(field, arms, owner, row, onehot, high, low)
    square = total(field[0] * field[0] + field[1] * field[1] + field[2] * field[2])
    forward_message(field, sums, [square], out_ref, FIRST)
    for copy in copies[4:]:
        copy.wait()
    out_ref[pl.ds(2, NDEV, stride=FIRST), :] = pack_ref[...].T


def turned(x, by):
    by = (by % 4) * NWIDE
    return x if by == 0 else jnp.concatenate([x[by:], x[:by]], axis=0)


def beside(x, by):
    groups = [x[z * NWIDE : (z + 1) * NWIDE] for z in range(4)]
    return jnp.concatenate([pltpu.roll(g, (-by) % NWIDE, 0) for g in groups], axis=0)


def routed(x, first, width):
    lane = iota((NDEV, TILE), 1)
    x = jnp.where((lane >= first) & (lane < first + width), x, 0.0)
    place = (lane - first) & 7
    edge = jnp.where(place == 7, beside(x, -1), jnp.where(place == 0, beside(x, 1), 0.0))
    return [turned(x, -1), turned(x, 1), turned(edge, -1), edge, turned(edge, 1)]


def shifted(x, by):
    by = by % TILE
    return x if by == 0 else pltpu.roll(x, by, 1)


def spread(row, lane):
    return jnp.broadcast_to(row[:, lane : lane + 1], (1, TILE))


def owner_kernel(step, inverse_ref, message_ref, *refs):
    states = refs[:step]
    out_ref, state_ref = refs[step:]
    parts = FIRST if step == 0 else 2
    first = rows_of(message_ref, 0, parts)
    second = rows_of(message_ref, 1, parts)
    sums = [jnp.sum(first, axis=0, keepdims=True), jnp.sum(second, axis=0, keepdims=True)]
    inners = [spread(sums[1], DOT_AT + 1 + i) for i in range(step)]
    square = spread(sums[1], DOT_AT)
    for inner in inners:
        square = square - inner * inner
    length = jnp.sqrt(square)
    scale = 1.0 / length
    for i in range(step):
        for half in range(2):
            sums[half] = sums[half] - inners[i] * states[i][half : half + 1, :]
    sums = [s * scale for s in sums]
    sub, lane = iota((8, TILE), 0), iota((8, TILE), 1)
    tiled = jnp.where(sub < 4, sums[0], sums[1])
    tiled = jnp.where((lane // ROWS == sub % 4) & (sub < 6), tiled, 0.0)
    tiled = tiled + pltpu.roll(tiled, 32, 1)
    tiled = tiled + pltpu.roll(tiled, 64, 1)
    zero = jnp.zeros((1, TILE), F32)
    by_row = [inverse_ref[a] for a in range(6)]
    by_row += [jnp.zeros((6, ROWS), F32)] * 2
    motion = []
    for half in range(2):
        inverse = jnp.concatenate(by_row[4 * half : 4 * half + 4], axis=1)
        motion.append(jnp.sum(inverse * tiled[0:6], axis=0, keepdims=True))
    state_ref[...] = jnp.concatenate(
        sums + motion + [length, scale] + inners + [zero] * (2 - step), axis=0
    )
    sent = [jnp.broadcast_to(m, (NDEV, TILE)) for m in motion]
    blocks = routed(second, HALO_AT, 24)
    rim = shifted(blocks[0], -HALO_AT)
    for k in range(1, 5):
        rim = rim + shifted(blocks[k], 24 * k - HALO_AT)
    sent.append(rim)
    if step == 0:
        blocks = routed(rows_of(message_ref, 2, parts), 0, FIXED)
        for k in range(3):
            sent[1] = sent[1] + shifted(blocks[2 + k], EDGES_AT + 2 * EDGE_STEP[k])
        sent.append(blocks[0] + shifted(blocks[1], 64))
    sent = sent + [jnp.zeros((NDEV, TILE), F32)] * (BACK[step] - len(sent))
    for part in range(BACK[step]):
        out_ref[pl.ds(part, NDEV, stride=BACK[step]), :] = sent[part]


def picked_motion(first, second, owner_ref, row_ref):
    table = jnp.concatenate([first.T, second.T[:64]], axis=0)
    high, low = split2(table)
    table = jnp.concatenate([high.astype(BF16), low.astype(BF16)], axis=1)
    owner_ids = iota((NDEV, TILE), 0)
    row_ids = iota((ROWS, TILE), 0)
    sub = iota((8, TILE), 0)
    results = []
    for block in range(BLOCKS):
        owner = owner_ref[8 * block : 8 * block + 8, :]
        row = row_ref[8 * block : 8 * block + 8, :]
        values = [jnp.zeros((8, TILE), F32) for _ in range(6)]
        for pair in ((0, 1), (2, 3), (4, 5), (6, 7)) if block < 3 else ((0, 7),):
            onehot = jnp.concatenate(
                [
                    jnp.where(owner_ids == owner[tile : tile + 1], 1.0, 0.0).astype(BF16)
                    for tile in pair
                ],
                axis=1,
            )
            onehot = jnp.concatenate([onehot, onehot], axis=0)
            found = jnp.dot(table, onehot, preferred_element_type=F32)
            for at, tile in enumerate(pair):
                mine = row_ids == row[tile : tile + 1]
                lanes = slice(at * TILE, (at + 1) * TILE)
                for part in range(6):
                    chosen = jnp.where(mine, found[part * ROWS : (part + 1) * ROWS, lanes], 0.0)
                    value = jnp.sum(chosen, axis=0, keepdims=True)
                    values[part] = jnp.where(sub == tile, value, values[part])
        results.append(values)
    return results


def source_rows(get, rows_ref):
    for i, dx in enumerate((-1, 0, 1)):
        for part in range(3):
            at = 30 * part + 10 * i
            edge = get(EDGE_OF[dx], part)
            rows_ref[at : at + 1, :] = edge[7:8]
            rows_ref[at + 1 : at + 9, :] = get(ROW_OF[dx], part)
            rows_ref[at + 9 : at + 10, :] = edge[0:1]


def sources_of(rows_ref, tile):
    return [
        [rows_ref[pl.ds(30 * part + 10 * i + tile + j, 8, stride=0), :] for part in range(3)]
        for i in range(3)
        for j in range(3)
    ]


def field_blocks(rows_ref, block_ref):
    block_ref[...] = jnp.zeros_like(block_ref)
    for part in range(3):
        high, low = split2(rows_ref[30 * part : 30 * part + 30, :])
        for tile in range(30):
            block_ref[tile, part : part + 1, :] = high[tile : tile + 1]
            block_ref[tile, 3 + part : 4 + part, :] = low[tile : tile + 1]


def mobility(moved, rows_ref, block_ref, near_ref, pairs_ref, pair_at):
    source_rows(lambda block, part: moved[block][part], rows_ref)
    field_blocks(rows_ref, block_ref)
    contract = (((1,), (1,)), ((), ()))

    def of_tile(tile, carry):
        sources = sources_of(rows_ref, tile)
        sums = [[], [], []]
        pair = pair_at(tile)
        for group in range(TILE // 8):
            terms = None
            for k in range(9):
                sep = pair(group, k)
                force = sources[k]
                along = sep[0] * force[0] + sep[1] * force[1] + sep[2] * force[2]
                term = [along * sep[a] for a in range(3)]
                terms = term if terms is None else [terms[a] + term[a] for a in range(3)]
            for a in range(3):
                sums[a].append(terms[a])
        blocks = [block_ref[10 * (k // 3) + k % 3 + tile].astype(BF16) for k in range(9)]
        blocks = jnp.concatenate(blocks, axis=1)
        near = [
            lax.dot_general(blocks, near_ref[i, tile], contract, preferred_element_type=F32)
            for i in range(2)
        ]
        near = near[0][0:3] + near[0][3:6] + near[1][0:3]
        for a in range(3):
            across = jnp.concatenate(sums[a], axis=0).T
            pairs_ref[pl.ds(8 * a + tile, 1), :] = (
                jnp.sum(across, axis=0, keepdims=True) + near[a : a + 1]
            )
        return carry

    lax.fori_loop(0, TY, of_tile, 0, unroll=4)
    return [pairs_ref[8 * a : 8 * a + 8, :] for a in range(3)]


def stored_pairs(pair_ref):
    def pair_at(tile):
        return lambda group, k: [pair_ref[tile, group, k, part] for part in range(3)]

    return pair_at


def new_pairs(pair_ref, near_ref, own_position, rows_ref):
    columns = jnp.concatenate([own_position, jnp.zeros((104, TILE), F32)], axis=0).T

    def pair_at(tile):
        turned_columns = pltpu.roll(columns, TILE - tile, 1)
        sources = sources_of(rows_ref, tile)
        targets = {}
        nears = {}

        def pair(group, k):
            if group not in targets:
                rows = turned_columns[8 * group : 8 * group + 8]
                targets[group] = [
                    jnp.broadcast_to(rows[:, 8 * a : 8 * a + 1], (8, TILE)) for a in range(3)
                ]
            target = targets[group]
            shift = (float(k // 3 - 1), float(k % 3 - 1), 0.0)
            sep = [target[a] - (sources[k][a] + shift[a]) for a in range(3)]
            soft = sep[0] * sep[0] + sep[1] * sep[1] + (sep[2] * sep[2] + EPS2)
            root = lax.rsqrt(soft)
            square = root * root
            scale = square * lax.rsqrt(root)
            nears[group, k] = root + EPS2 * (square * root)
            if group % 2 == 1:
                both = jnp.concatenate([nears[group - 1, k], nears[group, k]], axis=0)
                high, low = split2(both)
                place = slice(8 * group - 8, 8 * group + 8)
                lanes = slice(k * TILE, (k + 1) * TILE)
                near_ref[0, tile, place, lanes] = high.astype(BF16)
                near_ref[1, tile, place, lanes] = low.astype(BF16)
            found = [sep[a] * scale for a in range(3)]
            for part in range(3):
                pair_ref[tile, group, k, part] = found[part]
            return found

        return pair

    return pair_at


def local_kernel(step, *refs):
    refs = list(refs)
    back = BACK[step]
    take = lambda n: [refs.pop(0) for _ in range(n)]
    message_ref, state_ref, field_ref = take(3)
    if step == 0:
        (pack_ref,) = take(1)
    else:
        pair_ref, near_ref, arm_ref, owner_ref, row_ref = take(5)
    bases = take(step)
    if step == 0:
        pair_ref, near_ref, arm_ref, owner_ref, row_ref = take(5)
    if step < ITERS - 1:
        basis_ref, fresh_ref = take(2)
    moved_ref, out_ref = take(2)
    rows_ref, block_ref, pairs_ref, onehot, high, low = take(6)
    if step == 0:
        (places_ref,) = take(1)
        rows = rows_of(message_ref, 3, back).T
        edges = rows_of(message_ref, 1, back).T
        fixed = [pack_ref[0:FIXED, :], rows[:FIXED], rows[64 : 64 + FIXED]]
        for k in range(3):
            at = EDGES_AT + 2 * EDGE_STEP[k]
            fixed.append(edges[at : at + FIXED])
        for block in range(BLOCKS):
            arm_ref[24 * block : 24 * block + 24, :] = fixed[block][24:48]
            code = fixed[block][48:56].astype(jnp.int32)
            owner_ref[8 * block : 8 * block + 8, :] = lax.shift_right_logical(code, 5)
            row_ref[8 * block : 8 * block + 8, :] = code & (ROWS - 1)
        source_rows(lambda block, part: fixed[block][8 * part : 8 * part + 8], places_ref)
        pair_at = new_pairs(pair_ref, near_ref, fixed[0][0:24], places_ref)
    else:
        pair_at = stored_pairs(pair_ref)
    rim = rows_of(message_ref, 2, back).T
    basis = jnp.concatenate([field_ref[...], rim[:120]], axis=0)
    for i in range(step):
        basis = basis - state_ref[6 + i : 7 + i, :] * bases[i][...]
    basis = basis * state_ref[5:6, :]
    motions = picked_motion(
        rows_of(message_ref, 0, back), rows_of(message_ref, 1, back), owner_ref, row_ref
    )
    moved = []
    for block in range(BLOCKS):
        arm = [arm_ref[24 * block + 8 * a : 24 * block + 8 * a + 8, :] for a in range(3)]
        turn = cross(motions[block][3:], arm)
        moved.append(
            [
                basis[24 * block + 8 * a : 24 * block + 8 * a + 8]
                + (motions[block][a] + turn[a])
                for a in range(3)
            ]
        )
    pairs = mobility(moved, rows_ref, block_ref, near_ref, pairs_ref, pair_at)
    fresh = [moved[0][a] + FACTOR * pairs[a] for a in range(3)]
    for a in range(3):
        moved_ref[8 * a : 8 * a + 8, :] = moved[0][a]

    def dot(get):
        return total(fresh[0] * get(0) + fresh[1] * get(1) + fresh[2] * get(2))

    dots = [dot(lambda a: fresh[a])]
    for i in range(step):
        dots.append(dot(lambda a: bases[i][8 * a : 8 * a + 8, :]))
    dots.append(dot(lambda a: basis[8 * a : 8 * a + 8]))
    if step < ITERS - 1:
        basis_ref[...] = basis
        for a in range(3):
            fresh_ref[8 * a : 8 * a + 8, :] = fresh[a]
        arms = [arm_ref[8 * a : 8 * a + 8, :] for a in range(3)]
        sums = body_sums(
            fresh, arms, owner_ref[0:8, :], row_ref[0:8, :], onehot, high, low
        )
        forward_message(fresh, sums, dots, out_ref, 2)
    else:
        lane = iota((NDEV, TILE), 1)
        message = jnp.zeros((NDEV, TILE), F32)
        for at, value in enumerate(dots):
            message = jnp.where(lane == at, value, message)
        out_ref[...] = message


def final_kernel(message_ref, *refs):
    states, moved = refs[:3], refs[3:6]
    forces_ref, motion_ref = refs[6:]
    sums = jnp.sum(message_ref[...], axis=0, keepdims=True)
    beta = states[0][4:5, :]
    a = [states[1][6:7, :], states[1][4:5, :]]
    b = [states[2][6:7, :], states[2][7:8, :], states[2][4:5, :]]
    c = [spread(sums, 1 + i) for i in range(3)]
    inner = lambda p, q: sum([x * y for x, y in zip(p, q)][1:], p[0] * q[0])
    n00, n01, n02 = inner(a, a), inner(a, b), inner(a, c)
    n11, n12 = inner(b, b), inner(b, c)
    n22 = spread(sums, 0)
    i00 = lax.rsqrt(n00)
    l10, l20 = n01 * i00, n02 * i00
    i11 = lax.rsqrt(n11 - l10 * l10)
    l21 = (n12 - l20 * l10) * i11
    i22 = lax.rsqrt(n22 - l20 * l20 - l21 * l21)
    t0 = beta * a[0] * i00
    t1 = (beta * b[0] - l10 * t0) * i11
    t2 = (beta * c[0] - l20 * t0 - l21 * t1) * i22
    y2 = t2 * i22
    y1 = (t1 - l21 * y2) * i11
    y0 = (t0 - l10 * y1 - l20 * y2) * i00
    forces_ref[...] = y0 * moved[0][...] + y1 * moved[1][...] + y2 * moved[2][...]
    for part in range(6):
        half, at = part // 4, (part % 4) * ROWS
        row = slice(2 + half, 3 + half)
        whole = y0 * states[0][row, :] + y1 * states[1][row, :] + y2 * states[2][row, :]
        motion_ref[part : part + 1, :] = whole[:, at : at + ROWS]


HBM = pl.BlockSpec(memory_space=pltpu.HBM)
VMEM = pl.BlockSpec(memory_space=pltpu.VMEM)


def f32(*shape):
    return jax.ShapeDtypeStruct(shape, F32)


def i32(*shape):
    return jax.ShapeDtypeStruct(shape, jnp.int32)


PAIRS = (TY, TILE // 8, 9, 3, 8, TILE)
NEAR = (2, TY, TILE, 9 * TILE)


def sums_scratch():
    return [
        pltpu.VMEM((NDEV, TY * TILE), BF16),
        pltpu.VMEM((6 * ROWS, TY * TILE), BF16),
        pltpu.VMEM((6 * ROWS, TY * TILE), BF16),
    ]


def call(body, out, scratch=(), mib=16, **options):
    return pl.pallas_call(
        body,
        out_shape=out,
        scratch_shapes=list(scratch),
        compiler_params=pltpu.CompilerParams(vmem_limit_bytes=mib * 1024 * 1024),
        **options,
    )


def exchange(message):
    rows = message.shape[0]
    if rows != 3 * NDEV:
        return lax.all_to_all(message, CELL_WIDE, split_axis=0, concat_axis=0, tiled=True)
    moved = message.reshape(NDEV, 1, rows * TILE // NDEV)
    moved = lax.all_to_all(moved, CELL_WIDE, split_axis=0, concat_axis=0, tiled=True)
    return moved.reshape(rows, TILE)


def local(positions, rhs, blob_owner, blob_row, blob_arm, body_inverse):
    pos = positions.reshape(24, TILE)
    field = rhs.reshape(24, TILE)
    arm = blob_arm.reshape(24, TILE)
    owner = blob_owner.reshape(TY, TILE)
    row = blob_row.reshape(TY, TILE)
    held = (field, owner, row, arm, pos, body_inverse)
    message, pack, field, inverse = call(
        start_kernel,
        (f32(FIRST * NDEV, TILE), f32(TILE, TILE), f32(24, TILE), f32(6, 6, ROWS)),
        [
            pltpu.VMEM((TY, TILE), jnp.int32),
            pltpu.VMEM((TY, TILE), jnp.int32),
            pltpu.SemaphoreType.DMA((6,)),
        ]
        + sums_scratch(),
        in_specs=[HBM] * 6,
    )(*[pltpu.with_memory_space_constraint(x, pltpu.HBM) for x in held])
    states, bases, moveds = [], [], []
    for step in range(ITERS):
        arrived = exchange(message)
        message, state = call(
            lambda *refs, step=step: owner_kernel(step, *refs),
            (f32(BACK[step] * NDEV, TILE), f32(8, TILE)),
        )(inverse, arrived, *states)
        arrived = exchange(message)
        last = step == ITERS - 1
        outs = [f32(24, TILE), f32(NDEV if last else 2 * NDEV, TILE)]
        if not last:
            outs = [f32(24 * BLOCKS, TILE), f32(24, TILE)] + outs
        scratch = [
            pltpu.VMEM((96, TILE), F32),
            pltpu.VMEM((30, 16, TILE), F32),
            pltpu.VMEM((24, TILE), F32),
        ] + sums_scratch()
        if step == 0:
            outs = [
                pltpu.VMEM(PAIRS, F32),
                pltpu.VMEM(NEAR, BF16),
                f32(24 * BLOCKS, TILE),
                i32(8 * BLOCKS, TILE),
                i32(8 * BLOCKS, TILE),
            ] + outs
            scratch.append(pltpu.VMEM((96, TILE), F32))
        results = call(
            lambda *refs, step=step: local_kernel(step, *refs), tuple(outs), scratch
        )(arrived, state, field, *(fixed if step else (pack,)), *bases)
        if step == 0:
            held = [pltpu.with_memory_space_constraint(x, pltpu.VMEM) for x in results[:2]]
            fixed = (*held, *results[2:5])
        moved, message = results[-2:]
        states.append(state)
        moveds.append(moved)
        if not last:
            bases.append(results[-4])
            field = results[-3]
    arrived = exchange(message)
    forces, motion = call(final_kernel, (f32(24, TILE), f32(6, ROWS)))(arrived, *states, *moveds)
    return (forces.reshape(rhs.shape), motion)


def solution(mesh):
    split = Mesh(
        mesh.devices.reshape(mesh.shape["cell"], 4, 4, 2), ("cell", "wide_0", "wide_1", "wide_2")
    )
    in_specs = (
        P(None, "cell", WIDE, None),
        P(None, "cell", WIDE, None),
        P("cell", WIDE, None, None),
        P("cell", WIDE, None),
        P(None, "cell", WIDE, None),
        P(None, None, CELL_WIDE),
    )
    out_specs = (P(None, "cell", WIDE, None), P(None, CELL_WIDE))
    return jax.shard_map(local, mesh=split, in_specs=in_specs, out_specs=out_specs, check_vma=False)
```

```python
import math

import jax
import jax.numpy as jnp
from jax import lax
from jax.experimental import pallas as pl
from jax.experimental.pallas import tpu as pltpu
from jax.sharding import Mesh
from jax.sharding import PartitionSpec as P

ITERS = 3
WIDE = ("wide_0", "wide_1", "wide_2")
CELL_WIDE = ("cell", "wide_0", "wide_1", "wide_2")
EPS2 = 0.04
KAPPA = 0.3
FACTOR = KAPPA / math.sqrt(9 * 128)
F32 = jnp.float32
BF16 = jnp.bfloat16

TY = 8
TILE = 128
NDEV = 128
NWIDE = 32
ROWS = 32
HALO_AT = 64
DOT_AT = 88
FIRST = 3
BACK = (4, 4, 3)
FIXED = 56
BLOCKS = 6
EDGE_OF = {-1: 3, 0: 4, 1: 5}
ROW_OF = {-1: 1, 0: 0, 1: 2}
EDGES_AT = 64
EDGE_STEP = (1, 0, 2)


def iota(shape, axis):
    return lax.broadcasted_iota(jnp.int32, shape, axis)


def split2(x):
    hi = x.astype(BF16).astype(F32)
    return hi, x - hi


def cross(a, b):
    return (
        a[1] * b[2] - a[2] * b[1],
        a[2] * b[0] - a[0] * b[2],
        a[0] * b[1] - a[1] * b[0],
    )


def rows_of(message_ref, part, parts):
    return message_ref[pl.ds(part, NDEV, stride=parts), :]


def body_sums(field, arms, owner, row, onehot_ref, high_ref, low_ref):
    sent = list(field) + list(cross(arms, field))
    pieces = [split2(x) for x in sent]
    owner_ids = iota((NDEV, TILE), 0)
    row_ids = iota((ROWS, TILE), 0)
    for tile in range(TY):
        lanes = pl.ds(tile * TILE, TILE)
        pick = slice(tile, tile + 1)
        onehot_ref[:, lanes] = jnp.where(owner_ids == owner[pick], 1.0, 0.0).astype(BF16)
        mine = row_ids == row[pick]
        for part in range(6):
            place = slice(part * ROWS, (part + 1) * ROWS)
            high, low = pieces[part]
            high_ref[place, lanes] = jnp.where(mine, high[pick], 0.0).astype(BF16)
            low_ref[place, lanes] = jnp.where(mine, low[pick], 0.0).astype(BF16)
    contract = (((1,), (1,)), ((), ()))
    onehot = onehot_ref[...]
    return lax.dot_general(
        onehot, high_ref[...], contract, preferred_element_type=F32
    ) + lax.dot_general(onehot, low_ref[...], contract, preferred_element_type=F32)


def total(x):
    return jnp.sum(jnp.sum(x, axis=1, keepdims=True), axis=0, keepdims=True)


def forward_message(field, sums, dots, out_ref, parts):
    lane = iota((NDEV, TILE), 1)
    stacked = jnp.concatenate(
        [jnp.zeros((HALO_AT, TILE), F32)]
        + list(field)
        + [jnp.zeros((TILE - DOT_AT, TILE), F32)],
        axis=0,
    )
    second = jnp.concatenate([sums[:, TILE:], jnp.zeros((NDEV, 64), F32)], axis=1)
    second = second + stacked.T
    for at, dot in enumerate(dots):
        second = jnp.where(lane == DOT_AT + at, dot, second)
    out_ref[pl.ds(0, NDEV, stride=parts), :] = sums[:, :TILE]
    out_ref[pl.ds(1, NDEV, stride=parts), :] = second


def start_kernel(
    rhs_hbm, owner_hbm, row_hbm, arm_hbm, pos_hbm, inverse_hbm,
    out_ref, pack_ref, rhs_ref, inverse_ref,
    owner_ref, row_ref, sems, onehot, high, low,
):
    copies = [
        pltpu.make_async_copy(source, target, sems.at[at])
        for at, (source, target) in enumerate(
            (
                (rhs_hbm, rhs_ref),
                (owner_hbm, owner_ref),
                (row_hbm, row_ref),
                (arm_hbm, pack_ref.at[24:48, :]),
                (pos_hbm, pack_ref.at[0:24, :]),
                (inverse_hbm, inverse_ref),
            )
        )
    ]
    for copy in copies:
        copy.start()
    for copy in copies[:4]:
        copy.wait()
    field = [rhs_ref[8 * c : 8 * c + 8, :] for c in range(3)]
    arms = [pack_ref[24 + 8 * c : 32 + 8 * c, :] for c in range(3)]
    owner, row = owner_ref[...], row_ref[...]
    pack_ref[48:56, :] = (owner * ROWS + row).astype(F32)
    pack_ref[56:128, :] = jnp.zeros((72, TILE), F32)
    sums = body_sums(field, arms, owner, row, onehot, high, low)
    square = total(field[0] * field[0] + field[1] * field[1] + field[2] * field[2])
    forward_message(field, sums, [square], out_ref, FIRST)
    for copy in copies[4:]:
        copy.wait()
    out_ref[pl.ds(2, NDEV, stride=FIRST), :] = pack_ref[...].T


def turned(x, by):
    by = (by % 4) * NWIDE
    return x if by == 0 else jnp.concatenate([x[by:], x[:by]], axis=0)


def beside(x, by):
    groups = [x[z * NWIDE : (z + 1) * NWIDE] for z in range(4)]
    return jnp.concatenate([pltpu.roll(g, (-by) % NWIDE, 0) for g in groups], axis=0)


def routed(x, first, width):
    lane = iota((NDEV, TILE), 1)
    x = jnp.where((lane >= first) & (lane < first + width), x, 0.0)
    place = (lane - first) & 7
    edge = jnp.where(place == 7, beside(x, -1), jnp.where(place == 0, beside(x, 1), 0.0))
    return [turned(x, -1), turned(x, 1), turned(edge, -1), edge, turned(edge, 1)]


def shifted(x, by):
    by = by % TILE
    return x if by == 0 else pltpu.roll(x, by, 1)


def spread(row, lane):
    return jnp.broadcast_to(row[:, lane : lane + 1], (1, TILE))


def owner_kernel(step, inverse_ref, message_ref, *refs):
    states = refs[:step]
    out_ref, state_ref = refs[step:]
    parts = FIRST if step == 0 else 2
    first = rows_of(message_ref, 0, parts)
    second = rows_of(message_ref, 1, parts)
    sums = [jnp.sum(first, axis=0, keepdims=True), jnp.sum(second, axis=0, keepdims=True)]
    inners = [spread(sums[1], DOT_AT + 1 + i) for i in range(step)]
    square = spread(sums[1], DOT_AT)
    for inner in inners:
        square = square - inner * inner
    length = jnp.sqrt(square)
    scale = 1.0 / length
    for i in range(step):
        for half in range(2):
            sums[half] = sums[half] - inners[i] * states[i][half : half + 1, :]
    sums = [s * scale for s in sums]
    sub, lane = iota((8, TILE), 0), iota((8, TILE), 1)
    tiled = jnp.where(sub < 4, sums[0], sums[1])
    tiled = jnp.where((lane // ROWS == sub % 4) & (sub < 6), tiled, 0.0)
    tiled = tiled + pltpu.roll(tiled, 32, 1)
    tiled = tiled + pltpu.roll(tiled, 64, 1)
    zero = jnp.zeros((1, TILE), F32)
    by_row = [inverse_ref[a] for a in range(6)]
    by_row += [jnp.zeros((6, ROWS), F32)] * 2
    motion = []
    for half in range(2):
        inverse = jnp.concatenate(by_row[4 * half : 4 * half + 4], axis=1)
        motion.append(jnp.sum(inverse * tiled[0:6], axis=0, keepdims=True))
    state_ref[...] = jnp.concatenate(
        sums + motion + [length, scale] + inners + [zero] * (2 - step), axis=0
    )
    sent = [jnp.broadcast_to(m, (NDEV, TILE)) for m in motion]
    blocks = routed(second, HALO_AT, 24)
    rim = shifted(blocks[0], -HALO_AT)
    for k in range(1, 5):
        rim = rim + shifted(blocks[k], 24 * k - HALO_AT)
    sent.append(rim)
    if step == 0:
        blocks = routed(rows_of(message_ref, 2, parts), 0, FIXED)
        for k in range(3):
            sent[1] = sent[1] + shifted(blocks[2 + k], EDGES_AT + 2 * EDGE_STEP[k])
        sent.append(blocks[0] + shifted(blocks[1], 64))
    sent = sent + [jnp.zeros((NDEV, TILE), F32)] * (BACK[step] - len(sent))
    for part in range(BACK[step]):
        out_ref[pl.ds(part, NDEV, stride=BACK[step]), :] = sent[part]


def picked_motion(first, second, owner_ref, row_ref):
    table = jnp.concatenate([first.T, second.T[:64]], axis=0)
    high, low = split2(table)
    table = jnp.concatenate([high.astype(BF16), low.astype(BF16)], axis=1)
    owner_ids = iota((NDEV, TILE), 0)
    row_ids = iota((ROWS, TILE), 0)
    sub = iota((8, TILE), 0)
    results = []
    for block in range(BLOCKS):
        owner = owner_ref[8 * block : 8 * block + 8, :]
        row = row_ref[8 * block : 8 * block + 8, :]
        values = [jnp.zeros((8, TILE), F32) for _ in range(6)]
        for pair in ((0, 1), (2, 3), (4, 5), (6, 7)) if block < 3 else ((0, 7),):
            onehot = jnp.concatenate(
                [
                    jnp.where(owner_ids == owner[tile : tile + 1], 1.0, 0.0).astype(BF16)
                    for tile in pair
                ],
                axis=1,
            )
            onehot = jnp.concatenate([onehot, onehot], axis=0)
            found = jnp.dot(table, onehot, preferred_element_type=F32)
            for at, tile in enumerate(pair):
                mine = row_ids == row[tile : tile + 1]
                lanes = slice(at * TILE, (at + 1) * TILE)
                for part in range(6):
                    chosen = jnp.where(mine, found[part * ROWS : (part + 1) * ROWS, lanes], 0.0)
                    value = jnp.sum(chosen, axis=0, keepdims=True)
                    values[part] = jnp.where(sub == tile, value, values[part])
        results.append(values)
    return results


def source_rows(get, rows_ref):
    for i, dx in enumerate((-1, 0, 1)):
        for part in range(3):
            at = 30 * part + 10 * i
            edge = get(EDGE_OF[dx], part)
            rows_ref[at : at + 1, :] = edge[7:8]
            rows_ref[at + 1 : at + 9, :] = get(ROW_OF[dx], part)
            rows_ref[at + 9 : at + 10, :] = edge[0:1]


def sources_of(rows_ref, tile):
    return [
        [rows_ref[pl.ds(30 * part + 10 * i + tile + j, 8, stride=0), :] for part in range(3)]
        for i in range(3)
        for j in range(3)
    ]


def field_blocks(rows_ref, block_ref):
    block_ref[...] = jnp.zeros_like(block_ref)
    for part in range(3):
        high, low = split2(rows_ref[30 * part : 30 * part + 30, :])
        for tile in range(30):
            block_ref[tile, part : part + 1, :] = high[tile : tile + 1]
            block_ref[tile, 3 + part : 4 + part, :] = low[tile : tile + 1]


def mobility(moved, rows_ref, block_ref, near_ref, pairs_ref, pair_at, across_ref):
    source_rows(lambda block, part: moved[block][part], rows_ref)
    field_blocks(rows_ref, block_ref)
    contract = (((1,), (1,)), ((), ()))

    def of_tile(tile, carry):
        sources = sources_of(rows_ref, tile)
        sums = [[], [], []]
        pair = pair_at(tile)
        for group in range(TILE // 8):
            terms = None
            for k in range(9):
                sep = pair(group, k)
                force = sources[k]
                along = sep[0] * force[0] + sep[1] * force[1] + sep[2] * force[2]
                term = [along * sep[a] for a in range(3)]
                terms = term if terms is None else [terms[a] + term[a] for a in range(3)]
            for a in range(3):
                sums[a].append(terms[a])
        blocks = [block_ref[10 * (k // 3) + k % 3 + tile].astype(BF16) for k in range(9)]
        blocks = jnp.concatenate(blocks, axis=1)
        near = [
            lax.dot_general(blocks, near_ref[i, tile], contract, preferred_element_type=F32)
            for i in range(2)
        ]
        near = near[0][0:3] + near[0][3:6] + near[1][0:3]
        for a in range(3):
            across = jnp.concatenate(sums[a], axis=0)
            found = near[a : a + 1]
            if across_ref is None:
                found = found + jnp.sum(across.T, axis=0, keepdims=True)
            else:
                across_ref[a, tile] = across
            pairs_ref[pl.ds(8 * a + tile, 1), :] = found
        return carry

    lax.fori_loop(0, TY, of_tile, 0, unroll=4)
    if across_ref is not None:
        for a in range(3):
            for tile in range(TY):
                place = slice(8 * a + tile, 8 * a + tile + 1)
                across = jnp.sum(across_ref[a, tile].T, axis=0, keepdims=True)
                pairs_ref[place, :] = pairs_ref[place, :] + across
    return [pairs_ref[8 * a : 8 * a + 8, :] for a in range(3)]


def stored_pairs(pair_ref):
    def pair_at(tile):
        return lambda group, k: [pair_ref[tile, group, k, part] for part in range(3)]

    return pair_at


def new_pairs(pair_ref, near_ref, own_position, rows_ref):
    columns = jnp.concatenate([own_position, jnp.zeros((104, TILE), F32)], axis=0).T

    def pair_at(tile):
        turned_columns = pltpu.roll(columns, TILE - tile, 1)
        sources = sources_of(rows_ref, tile)
        targets = {}
        nears = {}

        def pair(group, k):
            if group not in targets:
                rows = turned_columns[8 * group : 8 * group + 8]
                targets[group] = [
                    jnp.broadcast_to(rows[:, 8 * a : 8 * a + 1], (8, TILE)) for a in range(3)
                ]
            target = targets[group]
            shift = (float(k // 3 - 1), float(k % 3 - 1), 0.0)
            sep = [target[a] - (sources[k][a] + shift[a]) for a in range(3)]
            soft = sep[0] * sep[0] + sep[1] * sep[1] + (sep[2] * sep[2] + EPS2)
            root = lax.rsqrt(soft)
            square = root * root
            scale = square * lax.rsqrt(root)
            nears[group, k] = root + EPS2 * (square * root)
            if group % 2 == 1:
                both = jnp.concatenate([nears[group - 1, k], nears[group, k]], axis=0)
                high, low = split2(both)
                place = slice(8 * group - 8, 8 * group + 8)
                lanes = slice(k * TILE, (k + 1) * TILE)
                near_ref[0, tile, place, lanes] = high.astype(BF16)
                near_ref[1, tile, place, lanes] = low.astype(BF16)
            found = [sep[a] * scale for a in range(3)]
            for part in range(3):
                pair_ref[tile, group, k, part] = found[part]
            return found

        return pair

    return pair_at


def local_kernel(step, *refs):
    refs = list(refs)
    back = BACK[step]
    take = lambda n: [refs.pop(0) for _ in range(n)]
    message_ref, state_ref, field_ref = take(3)
    if step == 0:
        (pack_ref,) = take(1)
    else:
        pair_ref, near_ref, arm_ref, owner_ref, row_ref = take(5)
    bases = take(step)
    if step == 0:
        pair_ref, near_ref, arm_ref, owner_ref, row_ref = take(5)
    if step < ITERS - 1:
        basis_ref, fresh_ref = take(2)
    moved_ref, out_ref = take(2)
    rows_ref, block_ref, pairs_ref, onehot, high, low = take(6)
    across_ref = take(1)[0] if step in DEFERRED else None
    if step == 0:
        (places_ref,) = take(1)
        rows = rows_of(message_ref, 3, back).T
        edges = rows_of(message_ref, 1, back).T
        fixed = [pack_ref[0:FIXED, :], rows[:FIXED], rows[64 : 64 + FIXED]]
        for k in range(3):
            at = EDGES_AT + 2 * EDGE_STEP[k]
            fixed.append(edges[at : at + FIXED])
        for block in range(BLOCKS):
            arm_ref[24 * block : 24 * block + 24, :] = fixed[block][24:48]
            code = fixed[block][48:56].astype(jnp.int32)
            owner_ref[8 * block : 8 * block + 8, :] = lax.shift_right_logical(code, 5)
            row_ref[8 * block : 8 * block + 8, :] = code & (ROWS - 1)
        source_rows(lambda block, part: fixed[block][8 * part : 8 * part + 8], places_ref)
        pair_at = new_pairs(pair_ref, near_ref, fixed[0][0:24], places_ref)
    else:
        pair_at = stored_pairs(pair_ref)
    rim = rows_of(message_ref, 2, back).T
    basis = jnp.concatenate([field_ref[...], rim[:120]], axis=0)
    for i in range(step):
        basis = basis - state_ref[6 + i : 7 + i, :] * bases[i][...]
    basis = basis * state_ref[5:6, :]
    motions = picked_motion(
        rows_of(message_ref, 0, back), rows_of(message_ref, 1, back), owner_ref, row_ref
    )
    moved = []
    for block in range(BLOCKS):
        arm = [arm_ref[24 * block + 8 * a : 24 * block + 8 * a + 8, :] for a in range(3)]
        turn = cross(motions[block][3:], arm)
        moved.append(
            [
                basis[24 * block + 8 * a : 24 * block + 8 * a + 8]
                + (motions[block][a] + turn[a])
                for a in range(3)
            ]
        )
    pairs = mobility(moved, rows_ref, block_ref, near_ref, pairs_ref, pair_at, across_ref)
    fresh = [moved[0][a] + FACTOR * pairs[a] for a in range(3)]
    for a in range(3):
        moved_ref[8 * a : 8 * a + 8, :] = moved[0][a]

    def dot(get):
        return total(fresh[0] * get(0) + fresh[1] * get(1) + fresh[2] * get(2))

    dots = [dot(lambda a: fresh[a])]
    for i in range(step):
        dots.append(dot(lambda a: bases[i][8 * a : 8 * a + 8, :]))
    dots.append(dot(lambda a: basis[8 * a : 8 * a + 8]))
    if step < ITERS - 1:
        basis_ref[...] = basis
        for a in range(3):
            fresh_ref[8 * a : 8 * a + 8, :] = fresh[a]
        arms = [arm_ref[8 * a : 8 * a + 8, :] for a in range(3)]
        sums = body_sums(
            fresh, arms, owner_ref[0:8, :], row_ref[0:8, :], onehot, high, low
        )
        forward_message(fresh, sums, dots, out_ref, 2)
    else:
        lane = iota((NDEV, TILE), 1)
        message = jnp.zeros((NDEV, TILE), F32)
        for at, value in enumerate(dots):
            message = jnp.where(lane == at, value, message)
        out_ref[...] = message


def final_kernel(message_ref, *refs):
    states, moved = refs[:3], refs[3:6]
    forces_ref, motion_ref = refs[6:]
    sums = jnp.sum(message_ref[...], axis=0, keepdims=True)
    beta = states[0][4:5, :]
    a = [states[1][6:7, :], states[1][4:5, :]]
    b = [states[2][6:7, :], states[2][7:8, :], states[2][4:5, :]]
    c = [spread(sums, 1 + i) for i in range(3)]
    inner = lambda p, q: sum([x * y for x, y in zip(p, q)][1:], p[0] * q[0])
    n00, n01, n02 = inner(a, a), inner(a, b), inner(a, c)
    n11, n12 = inner(b, b), inner(b, c)
    n22 = spread(sums, 0)
    i00 = lax.rsqrt(n00)
    l10, l20 = n01 * i00, n02 * i00
    i11 = lax.rsqrt(n11 - l10 * l10)
    l21 = (n12 - l20 * l10) * i11
    i22 = lax.rsqrt(n22 - l20 * l20 - l21 * l21)
    t0 = beta * a[0] * i00
    t1 = (beta * b[0] - l10 * t0) * i11
    t2 = (beta * c[0] - l20 * t0 - l21 * t1) * i22
    y2 = t2 * i22
    y1 = (t1 - l21 * y2) * i11
    y0 = (t0 - l10 * y1 - l20 * y2) * i00
    forces_ref[...] = y0 * moved[0][...] + y1 * moved[1][...] + y2 * moved[2][...]
    for part in range(6):
        half, at = part // 4, (part % 4) * ROWS
        row = slice(2 + half, 3 + half)
        whole = y0 * states[0][row, :] + y1 * states[1][row, :] + y2 * states[2][row, :]
        motion_ref[part : part + 1, :] = whole[:, at : at + ROWS]


HBM = pl.BlockSpec(memory_space=pltpu.HBM)
VMEM = pl.BlockSpec(memory_space=pltpu.VMEM)


def f32(*shape):
    return jax.ShapeDtypeStruct(shape, F32)


def i32(*shape):
    return jax.ShapeDtypeStruct(shape, jnp.int32)


DEFERRED = (0,)
PAIRS = (TY, TILE // 8, 9, 3, 8, TILE)
NEAR = (2, TY, TILE, 9 * TILE)


def sums_scratch():
    return [
        pltpu.VMEM((NDEV, TY * TILE), BF16),
        pltpu.VMEM((6 * ROWS, TY * TILE), BF16),
        pltpu.VMEM((6 * ROWS, TY * TILE), BF16),
    ]


def call(body, out, scratch=(), mib=16, **options):
    return pl.pallas_call(
        body,
        out_shape=out,
        scratch_shapes=list(scratch),
        compiler_params=pltpu.CompilerParams(vmem_limit_bytes=mib * 1024 * 1024),
        **options,
    )


def exchange(message):
    rows = message.shape[0]
    if rows != 3 * NDEV:
        return lax.all_to_all(message, CELL_WIDE, split_axis=0, concat_axis=0, tiled=True)
    moved = message.reshape(NDEV, 1, rows * TILE // NDEV)
    moved = lax.all_to_all(moved, CELL_WIDE, split_axis=0, concat_axis=0, tiled=True)
    return moved.reshape(rows, TILE)


def local(positions, rhs, blob_owner, blob_row, blob_arm, body_inverse):
    pos = positions.reshape(24, TILE)
    field = rhs.reshape(24, TILE)
    arm = blob_arm.reshape(24, TILE)
    owner = blob_owner.reshape(TY, TILE)
    row = blob_row.reshape(TY, TILE)
    held = (field, owner, row, arm, pos, body_inverse)
    message, pack, field, inverse = call(
        start_kernel,
        (f32(FIRST * NDEV, TILE), f32(TILE, TILE), f32(24, TILE), f32(6, 6, ROWS)),
        [
            pltpu.VMEM((TY, TILE), jnp.int32),
            pltpu.VMEM((TY, TILE), jnp.int32),
            pltpu.SemaphoreType.DMA((6,)),
        ]
        + sums_scratch(),
        in_specs=[HBM] * 6,
    )(*[pltpu.with_memory_space_constraint(x, pltpu.HBM) for x in held])
    states, bases, moveds = [], [], []
    for step in range(ITERS):
        arrived = exchange(message)
        message, state = call(
            lambda *refs, step=step: owner_kernel(step, *refs),
            (f32(BACK[step] * NDEV, TILE), f32(8, TILE)),
        )(inverse, arrived, *states)
        arrived = exchange(message)
        last = step == ITERS - 1
        outs = [f32(24, TILE), f32(NDEV if last else 2 * NDEV, TILE)]
        if not last:
            outs = [f32(24 * BLOCKS, TILE), f32(24, TILE)] + outs
        scratch = [
            pltpu.VMEM((96, TILE), F32),
            pltpu.VMEM((30, 16, TILE), F32),
            pltpu.VMEM((24, TILE), F32),
        ] + sums_scratch()
        if step in DEFERRED:
            scratch.append(pltpu.VMEM((3, TY, TILE, TILE), F32))
        if step == 0:
            outs = [
                pltpu.VMEM(PAIRS, F32),
                pltpu.VMEM(NEAR, BF16),
                f32(24 * BLOCKS, TILE),
                i32(8 * BLOCKS, TILE),
                i32(8 * BLOCKS, TILE),
            ] + outs
            scratch.append(pltpu.VMEM((96, TILE), F32))
        results = call(
            lambda *refs, step=step: local_kernel(step, *refs), tuple(outs), scratch
        )(arrived, state, field, *(fixed if step else (pack,)), *bases)
        if step == 0:
            held = [pltpu.with_memory_space_constraint(x, pltpu.VMEM) for x in results[:2]]
            fixed = (*held, *results[2:5])
        moved, message = results[-2:]
        states.append(state)
        moveds.append(moved)
        if not last:
            bases.append(results[-4])
            field = results[-3]
    arrived = exchange(message)
    forces, motion = call(final_kernel, (f32(24, TILE), f32(6, ROWS)))(arrived, *states, *moveds)
    return (forces.reshape(rhs.shape), motion)


def solution(mesh):
    split = Mesh(
        mesh.devices.reshape(mesh.shape["cell"], 4, 4, 2), ("cell", "wide_0", "wide_1", "wide_2")
    )
    in_specs = (
        P(None, "cell", WIDE, None),
        P(None, "cell", WIDE, None),
        P("cell", WIDE, None, None),
        P("cell", WIDE, None),
        P(None, "cell", WIDE, None),
        P(None, None, CELL_WIDE),
    )
    out_specs = (P(None, "cell", WIDE, None), P(None, CELL_WIDE))
    return jax.shard_map(local, mesh=split, in_specs=in_specs, out_specs=out_specs, check_vma=False)
```
